32 devices in a mesh: dom: 16 (over z, x, core), head: 2 (over y).
Axes of the slice: x: 2, y: 2, z: 4, core: 2. Of those that a mesh axis runs over, the one named last changes fastest.
Arguments:
- node_features: float32 [16384, 256], P('dom'), may hold values from -16 to 16, as said below
- w_query: float32 [256, 256], P(None, 'head'), may hold values from -0.375 to 0.375
- w_key: float32 [256, 256], P(None, 'head'), may hold values from -0.375 to 0.375
- w_value: float32 [256, 256], P(None, 'head'), may hold values from -0.375 to 0.375
- w_out: float32 [256, 256], P('head'), may hold values from -0.375 to 0.375
- nbr_part: int32 [128, 7], P('dom'), may hold values from 0 to 15, all different within a row; in each aligned block of 8 rows (0 to 7, 8 to 15, ...) at most 4 rows name the same one
- nbr_slot: int32 [128, 7], P('dom'), may hold values from 0 to 7
- key_mask: int32 [128, 7, 128], P('dom'), may hold values 0 or 1
- out_cotangent: float32 [16384, 256], P('dom'), may hold values from -6 to 6
Outputs:
- layer_out: float32 [16384, 256], P('dom', 'head')
- grad_features: float32 [16384, 256], P('dom', 'head')
- grad_query: float32 [256, 256], P(None, 'head')
- grad_key: float32 [256, 256], P(None, 'head')
- grad_value: float32 [256, 256], P(None, 'head')
- grad_out: float32 [256, 256], P('head')
The draws below stay inside these ranges and needn't reach their ends.
Inputs may be any that keep to these rules, and one draw needn't show every extreme that they name: `nbr_part`: each block's 7 entries name different partitions; among the blocks of one partition, no partition is named by more than 4 entries, and 4 is reached. `node_features`: real node features.
All inputs are finite; a program needn't handle non-finite values. No bound on the sum of `key_mask` on one device may be relied on, other than what follows from the above.
Results may differ from the reference program's by a relative error of at most 0.0003.
Values sent between devices are 32-bit elements; how exact they have to be, the bound alone decides.
No kernel may reach another device: no remote copies, remote signals or barrier semaphores. Data moves between devices by JAX's collectives and lax.ppermute only.
A program may use at most 192 MiB of HBM per device.

```python
import math
import jax
import jax.numpy as jnp
import numpy as np
from jax import lax

D = 256
H = 8
BLK = 128
L = 7
NB = 8
NBLOCKS = 128
NODES = 16384
C = 4
N_DOM = 16


def draw_node_features(key, part):
    key_base = jax.random.fold_in(jax.random.fold_in(key, 11), 0)
    return jnp.clip(jax.random.normal(key_base, (NODES, D), jnp.float32), -6.0, 6.0)


def place_ends(result, rng, low, largest):
    spot = [jax.random.randint(jax.random.fold_in(rng, axis), (), 0, length) for axis, length in enumerate(result.shape)]
    longest = result.shape.index(max(result.shape))
    beside = spot[:longest] + [(spot[longest] + 1) % result.shape[longest]] + spot[longest + 1:]
    return result.at[tuple(spot)].set(low).at[tuple(beside)].set(largest)


def shard_levels(own_key, shape, cuts, low, high):
    level = 1.0
    for axis_at, shards_of in cuts:
        draws = jax.random.uniform(jax.random.fold_in(jax.random.fold_in(own_key, 6), axis_at), (shards_of,), jnp.float32, low / len(cuts), high / len(cuts))
        level = level * jnp.repeat(jnp.exp(draws), shape[axis_at] // shards_of).reshape((-1,) + (1,) * (len(shape) - 1 - axis_at))
    return level


def routed_block(rng, own, number, rows, count, top, most, skew):
    sequence = jax.random.permutation(rng, count)
    packed, usual = shares(count, rows * top, most, skew, True), shares(count, rows * top, most, skew, False)
    places = jnp.arange(count)

    def named(tallies, offset_by):
        used = int((tallies > 0).sum())
        fixed = max(1, used // 4)
        shifted = fixed + (places - fixed + offset_by * (used - fixed)) % max(1, count - fixed)
        return jnp.zeros((count,), jnp.int32).at[sequence[jnp.where(places < fixed, places, shifted)]].set(jnp.asarray(tallies, jnp.int32))

    tallies = jnp.where(number % 4 == 0, named(packed, number // 4), named(usual, number - number // 4 - 1))
    mixed = jax.random.permutation(jax.random.fold_in(own, 3), count)
    source_of, receiver = mixed[0:count // 2 * 2:2], mixed[1:count // 2 * 2:2]
    slack = jnp.minimum(tallies[source_of] - 1, most - tallies[receiver]) // 2
    slack = jnp.where((source_of == sequence[0]) | (receiver == sequence[0]) | (tallies[receiver] == 0), 0, jnp.maximum(slack, 0))
    shifted = jax.random.randint(jax.random.fold_in(own, 4), (count // 2,), 0, 1 << 20) % (slack + 1)
    tallies = tallies.at[source_of].add(-shifted).at[receiver].add(shifted)
    labels = jnp.searchsorted(jnp.cumsum(tallies), jnp.arange(rows * top), side="right").astype(jnp.int32)
    table = labels.reshape(top, rows).T
    table = table[jax.random.permutation(jax.random.fold_in(own, 1), rows)]
    offset_by = jax.random.randint(jax.random.fold_in(own, 2), (rows, 1), 0, top)
    return jnp.take_along_axis(table, (jnp.arange(top)[None, :] + offset_by) % top, axis=1)


def shares(amount, total, most, slope, full):
    weights = [(1 << 20) // math.isqrt(rank ** slope) + 1 for rank in range(1, amount + 1)]
    largest = most if full else min(most, max(-(-total // amount), total * weights[0] // sum(weights)))
    least = 1 if total - largest >= amount - 1 else 0
    holding, surplus = [largest] + [least] * (amount - 1), total - largest - least * (amount - 1)
    while surplus > 0:
        movable = [i for i in range(1, amount) if holding[i] < largest] or [i for i in range(1, amount) if holding[i] < most]
        pool, remaining = sum([weights[i] for i in movable]), surplus
        for i in movable:
            extra = min(most - holding[i], max(1, remaining * weights[i] // pool), surplus)
            holding[i] = holding[i] + extra
            surplus = surplus - extra
    return np.array(holding)


def normal_values(rng, dims, width, most, cuts=(), kind=jnp.bfloat16):
    entries = width * jax.random.normal(rng, dims, jnp.float32)
    if cuts:
        entries = entries * shard_levels(rng, dims, cuts, -0.22, 0.18)
    return jnp.clip(entries, -most, most).astype(kind)


def setup_inputs(seed: int = 0) -> dict:
    streams_of = jax.random.split(jax.random.key(seed), 10)
    node_features = draw_node_features(jax.random.fold_in(streams_of[9], 71), 0)
    w_query = normal_values(streams_of[1], (D, D), D ** -0.5, 0.375, ((1, 2),), jnp.float32)
    w_key = normal_values(streams_of[2], (D, D), D ** -0.5, 0.375, ((1, 2),), jnp.float32)
    w_value = normal_values(streams_of[3], (D, D), D ** -0.5, 0.375, ((1, 2),), jnp.float32)
    w_out = normal_values(streams_of[4], (D, D), D ** -0.5, 0.375, ((0, 2),), jnp.float32)
    nbr_part_keys = jax.random.split(jax.random.fold_in(streams_of[5], 1), NBLOCKS // NB)
    nbr_part_turns = jax.random.permutation(jax.random.fold_in(streams_of[5], 3), NBLOCKS // NB)
    nbr_part = jax.vmap(lambda own, number: routed_block(jax.random.fold_in(streams_of[5], 2), own, number, NB, N_DOM, L, C, 2))(nbr_part_keys, nbr_part_turns).reshape((NBLOCKS, L))
    nbr_slot = place_ends(jax.random.randint(streams_of[6], (NBLOCKS, L), 0, NB), jax.random.fold_in(streams_of[6], 1), 0, NB - 1).astype(jnp.int32)
    key_mask = place_ends((jax.random.randint(streams_of[7], (NBLOCKS, L, BLK), 0, 4) < 3).astype(jnp.int32), jax.random.fold_in(streams_of[7], 1), 0, 1)
    out_cotangent = normal_values(streams_of[8], (NODES, D), 1.0, 6.0, ((0, 16),), jnp.float32)
    return dict(node_features=node_features, w_query=w_query, w_key=w_key, w_value=w_value, w_out=w_out, nbr_part=nbr_part, nbr_slot=nbr_slot, key_mask=key_mask, out_cotangent=out_cotangent)


def reference(node_features, w_query, w_key, w_value, w_out, nbr_part, nbr_slot, key_mask, out_cotangent):
    highest = lax.Precision.HIGHEST
    num_blocks = NB * N_DOM
    head_size = D // H
    scale = head_size ** (-0.5)
    self_ids = jnp.arange(num_blocks, dtype=jnp.int32)[:, None]
    block_ids = jnp.concatenate([self_ids, (nbr_part * NB + nbr_slot).astype(jnp.int32)], axis=1)
    full_mask = jnp.concatenate([jnp.ones((num_blocks, 1, BLK), jnp.int32), key_mask], axis=1)
    full_mask = full_mask.reshape(num_blocks, (L + 1) * BLK) > 0

    def forward(inputs, w_query, w_key, w_value, w_out):
        queries = jnp.dot(inputs, w_query, precision=highest).reshape(num_blocks, BLK, H, head_size)
        keys_all = jnp.dot(inputs, w_key, precision=highest).reshape(num_blocks, BLK, H, head_size)
        values_all = jnp.dot(inputs, w_value, precision=highest).reshape(num_blocks, BLK, H, head_size)

        @jax.checkpoint
        def per_block(items):
            query_block, id_list, mask_row = items
            key_rows = keys_all[id_list].reshape((L + 1) * BLK, H, head_size)
            value_rows = values_all[id_list].reshape((L + 1) * BLK, H, head_size)
            scores = jnp.einsum('qhd,khd->hqk', query_block, key_rows, precision=highest) * scale
            scores = jnp.where(mask_row[None, None, :], scores, -1e+30)
            scores = scores - lax.optimization_barrier(jnp.max(scores, axis=-1, keepdims=True))
            probs = jnp.exp(scores)
            probs = probs / lax.optimization_barrier(jnp.sum(probs, axis=-1, keepdims=True))
            return jnp.einsum('hqk,khd->qhd', probs, value_rows, precision=highest)
        attended = lax.map(per_block, (queries, block_ids, full_mask)).reshape(num_blocks * BLK, D)
        return jnp.dot(attended, w_out, precision=highest)
    layer_out, pullback = jax.vjp(forward, node_features, w_query, w_key, w_value, w_out)
    grad_features, grad_query, grad_key, grad_value, grad_out = pullback(out_cotangent)
    return (layer_out, grad_features, grad_query, grad_key, grad_value, grad_out)
```

```python
import functools

import jax
import jax.numpy as jnp
from jax import lax
from jax.experimental import pallas as pl
from jax.experimental.pallas import tpu as pltpu
from jax.sharding import PartitionSpec as P

HEAD_SIZE = 32
GROUP = 4
SCALE = HEAD_SIZE ** (-0.5)
MASKED = -1e30
F32 = jnp.float32
BF16 = jnp.bfloat16


def split(value):
    high = value.astype(BF16)
    return high, (value - high.astype(F32)).astype(BF16)


def mul(left, right, left_dim=1, right_dim=0):
    return lax.dot_general(
        left, right, (((left_dim,), (right_dim,)), ((), ())), preferred_element_type=F32
    )


def mul3(left, right, left_dim=1, right_dim=0):
    left_high, left_low = left
    right_high, right_low = right
    return (
        mul(left_high, right_high, left_dim, right_dim)
        + mul(left_high, right_low, left_dim, right_dim)
        + mul(left_low, right_high, left_dim, right_dim)
    )


def wide(first, second):
    return jnp.concatenate([first, second], axis=1)


def fold(value):
    half = value.shape[1] // 2
    return value[:, :half] + value[:, half:]


def forward_kernel(entries, ids, *refs):
    feats = refs[:entries]
    (cot_ref, bias_ref, wq_ref, wk_ref, wv_ref, wo_ref,
     out_ref, feat_ref, stat_ref, gq_ref, go_ref) = refs[entries:]
    rows = cot_ref.shape[0]
    cols = wq_ref.shape[1]
    heads = cols // HEAD_SIZE
    inputs = split(jnp.concatenate([ref[...] for ref in feats], axis=0))
    w_query = split(wq_ref[...])
    w_out = split(wo_ref[...])
    pairs = mul3(inputs, split(wide(wk_ref[...], wv_ref[...])))
    key_high, key_low = split(pairs[:, :cols])
    value_high, value_low = split(pairs[:, cols:])
    key_twice, key_both = wide(key_high, key_high), wide(key_high, key_low)
    value_twice, value_both = wide(value_high, value_high), wide(value_high, value_low)
    own = (inputs[0][:rows], inputs[1][:rows])
    query = mul3(own, w_query) * SCALE
    cot = split(cot_ref[...])
    grad_mixed = mul3(cot, w_out, 1, 1)
    bias = bias_ref[0]
    lane = lax.broadcasted_iota(jnp.int32, (rows, cols), 1) // HEAD_SIZE
    stat_lane = lax.broadcasted_iota(jnp.int32, (rows, rows), 1)
    mixed = jnp.zeros((rows, cols), F32)
    grad_query = jnp.zeros((rows, cols), F32)
    stats = jnp.zeros((rows, rows), F32)
    for head in range(heads):
        here = lane == head
        q_high, q_low = split(jnp.where(here, query, 0.0))
        scores = mul(wide(q_high, q_low), key_twice, 1, 1) + mul(q_high, key_low, 1, 1) + bias
        top = jnp.max(scores, axis=1, keepdims=True)
        probs = jnp.exp(scores - top)
        total = jnp.sum(probs, axis=1, keepdims=True)
        p_high, p_low = split(probs)
        weighted = fold(mul(p_high, value_both)) + mul(p_low, value_high)
        inverse = 1.0 / total
        part = jnp.where(here, weighted * inverse, 0.0)
        mixed = mixed + part
        grad_part = jnp.where(here, grad_mixed, 0.0)
        delta = jnp.sum(grad_part * part, axis=1, keepdims=True)
        g_high, g_low = split(grad_part)
        grad_probs = mul(wide(g_high, g_low), value_twice, 1, 1) + mul(g_high, value_low, 1, 1)
        s_high, s_low = split(probs * (grad_probs - delta))
        back = fold(mul(s_high, key_both)) + mul(s_low, key_high)
        grad_query = grad_query + jnp.where(here, back * (inverse * SCALE), 0.0)
        stats = jnp.where(stat_lane == head, top + jnp.log(total), stats)
        stats = jnp.where(stat_lane == heads + head, delta, stats)
    mixed = split(mixed)
    grad_query = split(grad_query)
    out_ref[...] = mul3(mixed, w_out)
    feat_ref[...] = mul3(grad_query, w_query, 1, 1)
    stat_ref[0] = jnp.transpose(stats)[: 2 * heads]

    @pl.when(pl.program_id(0) == 0)
    def _():
        gq_ref[...] = jnp.zeros_like(gq_ref)
        go_ref[...] = jnp.zeros_like(go_ref)

    gq_ref[...] += mul3(own, grad_query, 0, 0)
    go_ref[...] += mul3(mixed, cot, 0, 0)


def attend_forward(ids, all_feats, out_cotangent, bias, w_query, w_key, w_value, w_out):
    block_count, entries = ids.shape
    node_rows, width = out_cotangent.shape
    rows = node_rows // block_count
    cols = w_query.shape[1]
    heads = cols // HEAD_SIZE

    def picked(entry):
        return pl.BlockSpec((rows, width), lambda b, ids: (ids[b, entry], 0))

    def whole(array):
        return pl.BlockSpec(array.shape, lambda b, ids: (0,) * array.ndim)

    own = pl.BlockSpec((rows, width), lambda b, ids: (b, 0))
    grad_shape = jax.ShapeDtypeStruct((width, cols), F32)
    out_shape = jax.ShapeDtypeStruct((cols, width), F32)
    node_shape = jax.ShapeDtypeStruct((node_rows, width), F32)
    return pl.pallas_call(
        functools.partial(forward_kernel, entries),
        out_shape=(
            node_shape,
            node_shape,
            jax.ShapeDtypeStruct((block_count, 2 * heads, rows), F32),
            grad_shape,
            out_shape,
        ),
        grid_spec=pltpu.PrefetchScalarGridSpec(
            num_scalar_prefetch=1,
            grid=(block_count,),
            in_specs=[picked(entry) for entry in range(entries)]
            + [own, pl.BlockSpec((1, 1, entries * rows), lambda b, ids: (b, 0, 0))]
            + [whole(w) for w in (w_query, w_key, w_value, w_out)],
            out_specs=(
                own,
                own,
                pl.BlockSpec((1, 2 * heads, rows), lambda b, ids: (b, 0, 0)),
                whole(grad_shape),
                whole(out_shape),
            ),
        ),
        compiler_params=pltpu.CompilerParams(
            dimension_semantics=("arbitrary",), vmem_limit_bytes=50 * 1024 * 1024
        ),
        name="attend_forward",
    )(ids, *([all_feats] * entries), out_cotangent, bias, w_query, w_key, w_value, w_out)


def backward_kernel(steps_ref, readers_ref, *refs):
    feats, cots, stats = refs[:GROUP], refs[GROUP:2 * GROUP], refs[2 * GROUP:3 * GROUP]
    (own_ref, bias_ref, part_ref, wq_ref, wk_ref, wv_ref, wo_ref,
     feat_ref, gk_ref, gv_ref, key_mem, value_mem, dk_mem, dv_mem) = refs[3 * GROUP:]
    step = pl.program_id(0)
    rows = own_ref.shape[0]
    cols = wq_ref.shape[1]
    heads = cols // HEAD_SIZE
    lane = lax.broadcasted_iota(jnp.int32, (rows, cols), 1) // HEAD_SIZE
    kind = steps_ref[1, step]

    @pl.when(step == 0)
    def _():
        gk_ref[...] = jnp.zeros_like(gk_ref)
        gv_ref[...] = jnp.zeros_like(gv_ref)

    @pl.when(kind % 2 == 1)
    def _():
        pairs = mul3(split(own_ref[...]), split(wide(wk_ref[...], wv_ref[...])))
        for head in range(heads):
            here = lane == head
            at = pl.ds(head * rows, rows)
            key_mem[at, :] = wide(*split(jnp.where(here, pairs[:, :cols], 0.0)))
            value_mem[at, :] = wide(*split(jnp.where(here, pairs[:, cols:], 0.0)))
        dk_mem[...] = jnp.zeros_like(dk_mem)
        dv_mem[...] = jnp.zeros_like(dv_mem)

    @pl.when(kind >= 4)
    def _():
        inputs = split(jnp.concatenate([ref[...] for ref in feats], axis=0))
        q_high, q_low = split(mul3(inputs, split(wq_ref[...])) * SCALE)
        cot = split(jnp.concatenate([ref[...] for ref in cots], axis=0))
        g_high, g_low = split(mul3(cot, split(wo_ref[...]), 1, 1))
        q_twice, q_both = wide(q_high, q_high), wide(q_high, q_low)
        g_twice, g_both = wide(g_high, g_high), wide(g_high, g_low)
        mark_row = lax.broadcasted_iota(jnp.int32, (8, GROUP * rows), 0)
        mark_col = lax.broadcasted_iota(jnp.int32, (8, GROUP * rows), 1)
        marks = (mark_row == mark_col // rows).astype(BF16)
        bias = mul(bias_ref[0].astype(BF16), marks, 0, 0)
        stat = jnp.concatenate([ref[0] for ref in stats], axis=1)
        grad_key = dk_mem[...]
        grad_value = dv_mem[...]
        for head in range(heads):
            here = lane == head
            keys = key_mem[pl.ds(head * rows, rows), :]
            values = value_mem[pl.ds(head * rows, rows), :]
            scores = mul(keys, q_twice, 1, 1) + mul(keys[:, :cols], q_low, 1, 1)
            probs = jnp.exp(scores + (bias - stat[head:head + 1]))
            grad_probs = mul(values, g_twice, 1, 1) + mul(values[:, :cols], g_low, 1, 1)
            grad_scores = probs * (grad_probs - stat[heads + head:heads + head + 1])
            p_high, p_low = split(probs)
            term = fold(mul(p_high, g_both)) + mul(p_low, g_high)
            grad_value = grad_value + jnp.where(here, term, 0.0)
            s_high, s_low = split(grad_scores)
            term = fold(mul(s_high, q_both)) + mul(s_low, q_high)
            grad_key = grad_key + jnp.where(here, term, 0.0)
        dk_mem[...] = grad_key
        dv_mem[...] = grad_value

    @pl.when((kind // 2) % 2 == 1)
    def _():
        grad_key, grad_value = split(dk_mem[...]), split(dv_mem[...])
        own = split(own_ref[...])
        feat_ref[...] = (
            part_ref[...]
            + mul3(grad_key, split(wk_ref[...]), 1, 1)
            + mul3(grad_value, split(wv_ref[...]), 1, 1)
        )
        gk_ref[...] += mul3(own, grad_key, 0, 0)
        gv_ref[...] += mul3(own, grad_value, 0, 0)


def attend_backward(
    steps, readers, all_feats, all_cots, all_stats, own_feats, bias, part,
    w_query, w_key, w_value, w_out, rows,
):
    count = steps.shape[1]
    node_rows, width = own_feats.shape
    cols = w_query.shape[1]
    heads = cols // HEAD_SIZE

    def picked(at):
        return pl.BlockSpec((rows, width), lambda s, steps, readers: (readers[s * GROUP + at], 0))

    def picked_stat(at):
        return pl.BlockSpec(
            (1, 2 * heads, rows), lambda s, steps, readers: (readers[s * GROUP + at], 0, 0)
        )

    def whole(array):
        return pl.BlockSpec(array.shape, lambda s, steps, readers: (0,) * array.ndim)

    own = pl.BlockSpec((rows, width), lambda s, steps, readers: (steps[0, s], 0))
    grad_shape = jax.ShapeDtypeStruct((width, cols), F32)
    return pl.pallas_call(
        backward_kernel,
        out_shape=(jax.ShapeDtypeStruct((node_rows, width), F32), grad_shape, grad_shape),
        grid_spec=pltpu.PrefetchScalarGridSpec(
            num_scalar_prefetch=2,
            grid=(count,),
            in_specs=[picked(at) for at in range(GROUP)]
            + [picked(at) for at in range(GROUP)]
            + [picked_stat(at) for at in range(GROUP)]
            + [own, pl.BlockSpec((1, 8, rows), lambda s, steps, readers: (s, 0, 0)), own]
            + [whole(w) for w in (w_query, w_key, w_value, w_out)],
            out_specs=(own, whole(grad_shape), whole(grad_shape)),
            scratch_shapes=[
                pltpu.VMEM((heads * rows, 2 * cols), BF16),
                pltpu.VMEM((heads * rows, 2 * cols), BF16),
                pltpu.VMEM((rows, cols), F32),
                pltpu.VMEM((rows, cols), F32),
            ],
        ),
        compiler_params=pltpu.CompilerParams(
            dimension_semantics=("arbitrary",), vmem_limit_bytes=50 * 1024 * 1024
        ),
        name="attend_backward",
    )(
        steps, readers, *([all_feats] * GROUP), *([all_cots] * GROUP), *([all_stats] * GROUP),
        own_feats, bias, part, w_query, w_key, w_value, w_out,
    )


def plan_backward(all_ids, all_mask, me, block_count, pair_limit):
    blocks, entries = all_ids.shape
    candidates = blocks * entries
    flat = all_ids.reshape(-1)
    slot = jnp.where(flat // block_count == me, flat % block_count, block_count)
    order = jnp.arange(candidates, dtype=jnp.int32)
    same = (slot[:, None] == slot[None, :]) & (order[None, :] < order[:, None])
    rank = jnp.sum(same.astype(jnp.int32), axis=1)
    block_range = jnp.arange(block_count, dtype=jnp.int32)
    tally = jnp.sum((slot[None, :] == block_range[:, None]).astype(jnp.int32), axis=1)
    chunks = (tally + GROUP - 1) // GROUP
    ends = jnp.sum(
        jnp.where(block_range[None, :] <= block_range[:, None], chunks[None, :], 0), axis=1
    )
    starts = ends - chunks
    count = (pair_limit + block_count * GROUP) // GROUP
    places = count * GROUP
    start_of = jnp.sum(
        jnp.where(slot[:, None] == block_range[None, :], starts[None, :], 0), axis=1
    )
    place = jnp.where(slot < block_count, start_of * GROUP + rank, places)
    spot = jnp.arange(places, dtype=jnp.int32)
    hit = place[None, :] == spot[:, None]
    source = jnp.sum(jnp.where(hit, order[None, :], 0), axis=1)
    filled = jnp.sum(hit.astype(jnp.int32), axis=1) > 0
    readers = source // entries
    mask = all_mask.reshape(candidates, -1)[source]
    bias = jnp.where((mask > 0) & filled[:, None], 0.0, MASKED)
    bias = bias.reshape(count, GROUP, -1)
    bias = jnp.concatenate([bias, jnp.zeros((count, 8 - GROUP, bias.shape[2]), F32)], axis=1)
    step = jnp.arange(count, dtype=jnp.int32)
    block = jnp.sum((step[:, None] >= ends[None, :]).astype(jnp.int32), axis=1)
    live = block < block_count
    block = jnp.minimum(block, block_count - 1)
    first = jnp.sum((step[:, None] == starts[None, :]).astype(jnp.int32), axis=1) > 0
    last = jnp.sum((step[:, None] == ends[None, :] - 1).astype(jnp.int32), axis=1) > 0
    kind = jnp.where(
        live, first.astype(jnp.int32) + 2 * last.astype(jnp.int32) + 4, 0
    )
    return jnp.stack([block, kind]), readers, bias


def head_scatter(part):
    size = lax.axis_size("head")
    if size != 2:
        return lax.psum_scatter(part, "head", scatter_dimension=1, tiled=True)
    me = lax.axis_index("head")
    half = part.shape[1] // 2
    sent = lax.dynamic_slice_in_dim(part, (1 - me) * half, half, axis=1)
    kept = lax.dynamic_slice_in_dim(part, me * half, half, axis=1)
    return kept + lax.ppermute(sent, "head", [(0, 1), (1, 0)])


def per_device(
    node_features, w_query, w_key, w_value, w_out, nbr_part, nbr_slot, key_mask, out_cotangent
):
    dom_count = lax.axis_size("dom")
    block_count, list_len = nbr_part.shape
    node_rows, width = node_features.shape
    rows = node_rows // block_count
    me = lax.axis_index("dom")
    slot_cap = min(block_count, max(2, (block_count * list_len + dom_count - 1) // dom_count))
    self_ids = me * block_count + jnp.arange(block_count, dtype=jnp.int32)[:, None]
    ids = jnp.concatenate([self_ids, nbr_part * block_count + nbr_slot], axis=1)
    mask = jnp.concatenate([jnp.ones((block_count, 1, rows), jnp.int32), key_mask], axis=1)
    bias = jnp.where(mask > 0, 0.0, MASKED).reshape(block_count, 1, (list_len + 1) * rows)
    all_feats = lax.all_gather(node_features, "dom", axis=0, tiled=True)
    all_cots = lax.all_gather(out_cotangent, "dom", axis=0, tiled=True)
    all_ids = lax.all_gather(ids, "dom", axis=0, tiled=True)
    all_mask = lax.all_gather(mask, "dom", axis=0, tiled=True)
    steps, readers, back_bias = plan_backward(
        all_ids, all_mask, me, block_count, dom_count * slot_cap
    )
    out_part, feat_part, stats, grad_query, grad_out = attend_forward(
        ids, all_feats, out_cotangent, bias, w_query, w_key, w_value, w_out
    )
    layer_out = head_scatter(out_part)
    all_stats = lax.all_gather(stats, "dom", axis=0, tiled=True)
    feats_part, grad_key, grad_value = attend_backward(
        steps, readers, all_feats, all_cots, all_stats, node_features, back_bias, feat_part,
        w_query, w_key, w_value, w_out, rows,
    )
    grad_features = head_scatter(feats_part)
    grad_query, grad_key, grad_value, grad_out = lax.psum(
        (grad_query, grad_key, grad_value, grad_out), "dom"
    )
    return (layer_out, grad_features, grad_query, grad_key, grad_value, grad_out)


def solution(mesh):
    placed = (
        P("dom", None),
        P(None, "head"),
        P(None, "head"),
        P(None, "head"),
        P("head", None),
        P("dom", None),
        P("dom", None),
        P("dom", None, None),
        P("dom", None),
    )
    return jax.shard_map(
        per_device,
        mesh=mesh,
        in_specs=placed,
        out_specs=(
            P("dom", "head"),
            P("dom", "head"),
            P(None, "head"),
            P(None, "head"),
            P(None, "head"),
            P("head", None),
        ),
        check_vma=False,
    )
```

```python
import functools

import jax
import jax.numpy as jnp
from jax import lax
from jax.experimental import pallas as pl
from jax.experimental.pallas import tpu as pltpu
from jax.sharding import PartitionSpec as P

HEAD_SIZE = 32
GROUP = 4
SCALE = HEAD_SIZE ** (-0.5)
MASKED = -1e30
F32 = jnp.float32
BF16 = jnp.bfloat16


def split(value):
    high = value.astype(BF16)
    return high, (value - high.astype(F32)).astype(BF16)


def mul(left, right, left_dim=1, right_dim=0):
    return lax.dot_general(
        left, right, (((left_dim,), (right_dim,)), ((), ())), preferred_element_type=F32
    )


def mul3(left, right, left_dim=1, right_dim=0):
    left_high, left_low = left
    right_high, right_low = right
    return (
        mul(left_high, right_high, left_dim, right_dim)
        + mul(left_high, right_low, left_dim, right_dim)
        + mul(left_low, right_high, left_dim, right_dim)
    )


def wide(first, second):
    return jnp.concatenate([first, second], axis=1)


def fold(value):
    half = value.shape[1] // 2
    return value[:, :half] + value[:, half:]


def forward_kernel(entries, ids, *refs):
    feats = refs[:entries]
    (cot_ref, grad_ref, bias_ref, wq_ref, wk_ref, wv_ref, wo_ref,
     out_ref, feat_ref, stat_ref, gq_ref, go_ref) = refs[entries:]
    rows = cot_ref.shape[0]
    cols = wq_ref.shape[1]
    heads = cols // HEAD_SIZE
    inputs = split(jnp.concatenate([ref[...] for ref in feats], axis=0))
    w_query = split(wq_ref[...])
    w_out = split(wo_ref[...])
    pairs = mul3(inputs, split(wide(wk_ref[...], wv_ref[...])))
    key_high, key_low = split(pairs[:, :cols])
    value_high, value_low = split(pairs[:, cols:])
    key_twice, key_both = wide(key_high, key_high), wide(key_high, key_low)
    value_twice, value_both = wide(value_high, value_high), wide(value_high, value_low)
    own = (inputs[0][:rows], inputs[1][:rows])
    query = mul3(own, w_query) * SCALE
    cot = split(cot_ref[...])
    grad_mixed = grad_ref[...]
    bias = bias_ref[0]
    lane = lax.broadcasted_iota(jnp.int32, (rows, cols), 1) // HEAD_SIZE
    stat_lane = lax.broadcasted_iota(jnp.int32, (rows, rows), 1)
    mixed = jnp.zeros((rows, cols), F32)
    grad_query = jnp.zeros((rows, cols), F32)
    stats = jnp.zeros((rows, rows), F32)
    for head in range(heads):
        here = lane == head
        q_high, q_low = split(jnp.where(here, query, 0.0))
        scores = mul(wide(q_high, q_low), key_twice, 1, 1) + mul(q_high, key_low, 1, 1) + bias
        top = jnp.max(scores, axis=1, keepdims=True)
        probs = jnp.exp(scores - top)
        total = jnp.sum(probs, axis=1, keepdims=True)
        p_high, p_low = split(probs)
        weighted = fold(mul(p_high, value_both)) + mul(p_low, value_high)
        inverse = 1.0 / total
        part = jnp.where(here, weighted * inverse, 0.0)
        mixed = mixed + part
        grad_part = jnp.where(here, grad_mixed, 0.0)
        delta = jnp.sum(grad_part * part, axis=1, keepdims=True)
        g_high, g_low = split(grad_part)
        grad_probs = mul(wide(g_high, g_low), value_twice, 1, 1) + mul(g_high, value_low, 1, 1)
        s_high, s_low = split(probs * (grad_probs - delta))
        back = fold(mul(s_high, key_both)) + mul(s_low, key_high)
        grad_query = grad_query + jnp.where(here, back * (inverse * SCALE), 0.0)
        stats = jnp.where(stat_lane == head, top + jnp.log(total), stats)
        stats = jnp.where(stat_lane == heads + head, delta, stats)
    mixed = split(mixed)
    grad_query = split(grad_query)
    out_ref[...] = mul3(mixed, w_out)
    feat_ref[...] = mul3(grad_query, w_query, 1, 1)
    stat_ref[0] = jnp.transpose(stats)[: 2 * heads]

    @pl.when(pl.program_id(0) == 0)
    def _():
        gq_ref[...] = jnp.zeros_like(gq_ref)
        go_ref[...] = jnp.zeros_like(go_ref)

    gq_ref[...] += mul3(own, grad_query, 0, 0)
    go_ref[...] += mul3(mixed, cot, 0, 0)


def attend_forward(ids, all_feats, out_cotangent, grad_mixed, bias, w_query, w_key, w_value, w_out):
    block_count, entries = ids.shape
    node_rows, width = out_cotangent.shape
    rows = node_rows // block_count
    cols = w_query.shape[1]
    heads = cols // HEAD_SIZE

    def picked(entry):
        return pl.BlockSpec((rows, width), lambda b, ids: (ids[b, entry], 0))

    def whole(array):
        return pl.BlockSpec(array.shape, lambda b, ids: (0,) * array.ndim)

    own = pl.BlockSpec((rows, width), lambda b, ids: (b, 0))
    grad_shape = jax.ShapeDtypeStruct((width, cols), F32)
    out_shape = jax.ShapeDtypeStruct((cols, width), F32)
    node_shape = jax.ShapeDtypeStruct((node_rows, width), F32)
    return pl.pallas_call(
        functools.partial(forward_kernel, entries),
        out_shape=(
            node_shape,
            node_shape,
            jax.ShapeDtypeStruct((block_count, 2 * heads, rows), F32),
            grad_shape,
            out_shape,
        ),
        grid_spec=pltpu.PrefetchScalarGridSpec(
            num_scalar_prefetch=1,
            grid=(block_count,),
            in_specs=[picked(entry) for entry in range(entries)]
            + [own, pl.BlockSpec((rows, cols), lambda b, ids: (b, 0))]
            + [pl.BlockSpec((1, 1, entries * rows), lambda b, ids: (b, 0, 0))]
            + [whole(w) for w in (w_query, w_key, w_value, w_out)],
            out_specs=(
                own,
                own,
                pl.BlockSpec((1, 2 * heads, rows), lambda b, ids: (b, 0, 0)),
                whole(grad_shape),
                whole(out_shape),
            ),
        ),
        compiler_params=pltpu.CompilerParams(
            dimension_semantics=("arbitrary",), vmem_limit_bytes=50 * 1024 * 1024
        ),
        name="attend_forward",
    )(ids, *([all_feats] * entries), out_cotangent, grad_mixed, bias, w_query, w_key, w_value, w_out)


def backward_kernel(steps_ref, readers_ref, *refs):
    feats, cots, stats = refs[:GROUP], refs[GROUP:2 * GROUP], refs[2 * GROUP:3 * GROUP]
    (own_ref, bias_ref, part_ref, wq_ref, wk_ref, wv_ref,
     feat_ref, gk_ref, gv_ref, key_mem, value_mem, dk_mem, dv_mem) = refs[3 * GROUP:]
    step = pl.program_id(0)
    rows = own_ref.shape[0]
    cols = wq_ref.shape[1]
    heads = cols // HEAD_SIZE
    lane = lax.broadcasted_iota(jnp.int32, (rows, cols), 1) // HEAD_SIZE
    kind = steps_ref[1, step]

    @pl.when(step == 0)
    def _():
        gk_ref[...] = jnp.zeros_like(gk_ref)
        gv_ref[...] = jnp.zeros_like(gv_ref)

    @pl.when(kind % 2 == 1)
    def _():
        pairs = mul3(split(own_ref[...]), split(wide(wk_ref[...], wv_ref[...])))
        for head in range(heads):
            here = lane == head
            at = pl.ds(head * rows, rows)
            key_mem[at, :] = wide(*split(jnp.where(here, pairs[:, :cols], 0.0)))
            value_mem[at, :] = wide(*split(jnp.where(here, pairs[:, cols:], 0.0)))
        dk_mem[...] = jnp.zeros_like(dk_mem)
        dv_mem[...] = jnp.zeros_like(dv_mem)

    @pl.when(kind >= 4)
    def _():
        inputs = split(jnp.concatenate([ref[...] for ref in feats], axis=0))
        q_high, q_low = split(mul3(inputs, split(wq_ref[...])) * SCALE)
        g_high, g_low = split(jnp.concatenate([ref[...] for ref in cots], axis=0))
        q_twice, q_both = wide(q_high, q_high), wide(q_high, q_low)
        g_twice, g_both = wide(g_high, g_high), wide(g_high, g_low)
        mark_row = lax.broadcasted_iota(jnp.int32, (8, GROUP * rows), 0)
        mark_col = lax.broadcasted_iota(jnp.int32, (8, GROUP * rows), 1)
        marks = (mark_row == mark_col // rows).astype(BF16)
        bias = mul(bias_ref[0].astype(BF16), marks, 0, 0)
        stat = jnp.concatenate([ref[0] for ref in stats], axis=1)
        grad_key = dk_mem[...]
        grad_value = dv_mem[...]
        for head in range(heads):
            here = lane == head
            keys = key_mem[pl.ds(head * rows, rows), :]
            values = value_mem[pl.ds(head * rows, rows), :]
            scores = mul(keys, q_twice, 1, 1) + mul(keys[:, :cols], q_low, 1, 1)
            probs = jnp.exp(scores + (bias - stat[head:head + 1]))
            grad_probs = mul(values, g_twice, 1, 1) + mul(values[:, :cols], g_low, 1, 1)
            grad_scores = probs * (grad_probs - stat[heads + head:heads + head + 1])
            p_high, p_low = split(probs)
            term = fold(mul(p_high, g_both)) + mul(p_low, g_high)
            grad_value = grad_value + jnp.where(here, term, 0.0)
            s_high, s_low = split(grad_scores)
            term = fold(mul(s_high, q_both)) + mul(s_low, q_high)
            grad_key = grad_key + jnp.where(here, term, 0.0)
        dk_mem[...] = grad_key
        dv_mem[...] = grad_value

    @pl.when((kind // 2) % 2 == 1)
    def _():
        grad_key, grad_value = split(dk_mem[...]), split(dv_mem[...])
        own = split(own_ref[...])
        feat_ref[...] = (
            part_ref[...]
            + mul3(grad_key, split(wk_ref[...]), 1, 1)
            + mul3(grad_value, split(wv_ref[...]), 1, 1)
        )
        gk_ref[...] += mul3(own, grad_key, 0, 0)
        gv_ref[...] += mul3(own, grad_value, 0, 0)


def attend_backward(
    steps, readers, all_feats, all_cots, all_stats, own_feats, bias, part,
    w_query, w_key, w_value, rows,
):
    count = steps.shape[1]
    node_rows, width = own_feats.shape
    cols = w_query.shape[1]
    heads = cols // HEAD_SIZE

    def picked(at, lanes):
        return pl.BlockSpec((rows, lanes), lambda s, steps, readers: (readers[s * GROUP + at], 0))

    def picked_stat(at):
        return pl.BlockSpec(
            (1, 2 * heads, rows), lambda s, steps, readers: (readers[s * GROUP + at], 0, 0)
        )

    def whole(array):
        return pl.BlockSpec(array.shape, lambda s, steps, readers: (0,) * array.ndim)

    own = pl.BlockSpec((rows, width), lambda s, steps, readers: (steps[0, s], 0))
    grad_shape = jax.ShapeDtypeStruct((width, cols), F32)
    return pl.pallas_call(
        backward_kernel,
        out_shape=(jax.ShapeDtypeStruct((node_rows, width), F32), grad_shape, grad_shape),
        grid_spec=pltpu.PrefetchScalarGridSpec(
            num_scalar_prefetch=2,
            grid=(count,),
            in_specs=[picked(at, width) for at in range(GROUP)]
            + [picked(at, cols) for at in range(GROUP)]
            + [picked_stat(at) for at in range(GROUP)]
            + [own, pl.BlockSpec((1, 8, rows), lambda s, steps, readers: (s, 0, 0)), own]
            + [whole(w) for w in (w_query, w_key, w_value)],
            out_specs=(own, whole(grad_shape), whole(grad_shape)),
            scratch_shapes=[
                pltpu.VMEM((heads * rows, 2 * cols), BF16),
                pltpu.VMEM((heads * rows, 2 * cols), BF16),
                pltpu.VMEM((rows, cols), F32),
                pltpu.VMEM((rows, cols), F32),
            ],
        ),
        compiler_params=pltpu.CompilerParams(
            dimension_semantics=("arbitrary",), vmem_limit_bytes=50 * 1024 * 1024
        ),
        name="attend_backward",
    )(
        steps, readers, *([all_feats] * GROUP), *([all_cots] * GROUP), *([all_stats] * GROUP),
        own_feats, bias, part, w_query, w_key, w_value,
    )


def plan_backward(all_ids, all_mask, me, block_count, pair_limit):
    blocks, entries = all_ids.shape
    candidates = blocks * entries
    flat = all_ids.reshape(-1)
    slot = jnp.where(flat // block_count == me, flat % block_count, block_count)
    order = jnp.arange(candidates, dtype=jnp.int32)
    same = (slot[:, None] == slot[None, :]) & (order[None, :] < order[:, None])
    rank = jnp.sum(same.astype(jnp.int32), axis=1)
    block_range = jnp.arange(block_count, dtype=jnp.int32)
    tally = jnp.sum((slot[None, :] == block_range[:, None]).astype(jnp.int32), axis=1)
    chunks = (tally + GROUP - 1) // GROUP
    ends = jnp.sum(
        jnp.where(block_range[None, :] <= block_range[:, None], chunks[None, :], 0), axis=1
    )
    starts = ends - chunks
    count = (pair_limit + block_count * GROUP) // GROUP
    places = count * GROUP
    start_of = jnp.sum(
        jnp.where(slot[:, None] == block_range[None, :], starts[None, :], 0), axis=1
    )
    place = jnp.where(slot < block_count, start_of * GROUP + rank, places)
    spot = jnp.arange(places, dtype=jnp.int32)
    hit = place[None, :] == spot[:, None]
    source = jnp.sum(jnp.where(hit, order[None, :], 0), axis=1)
    filled = jnp.sum(hit.astype(jnp.int32), axis=1) > 0
    readers = source // entries
    mask = all_mask.reshape(candidates, -1)[source]
    bias = jnp.where((mask > 0) & filled[:, None], 0.0, MASKED)
    bias = bias.reshape(count, GROUP, -1)
    bias = jnp.concatenate([bias, jnp.zeros((count, 8 - GROUP, bias.shape[2]), F32)], axis=1)
    step = jnp.arange(count, dtype=jnp.int32)
    block = jnp.sum((step[:, None] >= ends[None, :]).astype(jnp.int32), axis=1)
    live = block < block_count
    block = jnp.minimum(block, block_count - 1)
    first = jnp.sum((step[:, None] == starts[None, :]).astype(jnp.int32), axis=1) > 0
    last = jnp.sum((step[:, None] == ends[None, :] - 1).astype(jnp.int32), axis=1) > 0
    kind = jnp.where(
        live, first.astype(jnp.int32) + 2 * last.astype(jnp.int32) + 4, 0
    )
    return jnp.stack([block, kind]), readers, bias


def head_scatter(part):
    size = lax.axis_size("head")
    if size != 2:
        return lax.psum_scatter(part, "head", scatter_dimension=1, tiled=True)
    me = lax.axis_index("head")
    half = part.shape[1] // 2
    sent = lax.dynamic_slice_in_dim(part, (1 - me) * half, half, axis=1)
    kept = lax.dynamic_slice_in_dim(part, me * half, half, axis=1)
    return kept + lax.ppermute(sent, "head", [(0, 1), (1, 0)])


def dom_sum(first, second):
    size = lax.axis_size("dom")
    odd = lax.axis_index("dom") % 2 == 1

    def from_across(value, bit):
        return lax.ppermute(value, "dom", [(at, at ^ bit) for at in range(size)])

    mine = jnp.where(odd, second, first) + from_across(jnp.where(odd, first, second), 1)
    bit = 2
    while bit < size:
        mine = mine + from_across(mine, bit)
        bit *= 2
    other = from_across(mine, 1)
    return jnp.where(odd, other, mine), jnp.where(odd, mine, other)


def per_device(
    node_features, w_query, w_key, w_value, w_out, nbr_part, nbr_slot, key_mask, out_cotangent
):
    dom_count = lax.axis_size("dom")
    block_count, list_len = nbr_part.shape
    node_rows, width = node_features.shape
    rows = node_rows // block_count
    me = lax.axis_index("dom")
    slot_cap = min(block_count, max(2, (block_count * list_len + dom_count - 1) // dom_count))
    self_ids = me * block_count + jnp.arange(block_count, dtype=jnp.int32)[:, None]
    ids = jnp.concatenate([self_ids, nbr_part * block_count + nbr_slot], axis=1)
    mask = jnp.concatenate([jnp.ones((block_count, 1, rows), jnp.int32), key_mask], axis=1)
    bias = jnp.where(mask > 0, 0.0, MASKED).reshape(block_count, 1, (list_len + 1) * rows)
    all_feats = lax.all_gather(node_features, "dom", axis=0, tiled=True)
    grad_mixed = lax.dot_general(
        out_cotangent, w_out, (((1,), (1,)), ((), ())), precision=lax.Precision.HIGHEST
    )
    all_grads = lax.all_gather(grad_mixed, "dom", axis=0, tiled=True)
    all_ids = lax.all_gather(ids, "dom", axis=0, tiled=True)
    all_mask = lax.all_gather(mask, "dom", axis=0, tiled=True)
    steps, readers, back_bias = plan_backward(
        all_ids, all_mask, me, block_count, dom_count * slot_cap
    )
    out_part, feat_part, stats, grad_query, grad_out = attend_forward(
        ids, all_feats, out_cotangent, grad_mixed, bias, w_query, w_key, w_value, w_out
    )
    layer_out = head_scatter(out_part)
    cols = w_query.shape[1]
    pieces = [grad_out[:, at:at + cols] for at in range(0, width, cols)]
    grad_query, grad_out = dom_sum(grad_query, jnp.concatenate(pieces, axis=0))
    pieces = [grad_out[at:at + cols] for at in range(0, width, cols)]
    grad_out = jnp.concatenate(pieces, axis=1)
    all_stats = lax.all_gather(stats, "dom", axis=0, tiled=True)
    feats_part, grad_key, grad_value = attend_backward(
        steps, readers, all_feats, all_grads, all_stats, node_features, back_bias, feat_part,
        w_query, w_key, w_value, rows,
    )
    grad_features = head_scatter(feats_part)
    grad_key, grad_value = dom_sum(grad_key, grad_value)
    return (layer_out, grad_features, grad_query, grad_key, grad_value, grad_out)


def solution(mesh):
    placed = (
        P("dom", None),
        P(None, "head"),
        P(None, "head"),
        P(None, "head"),
        P("head", None),
        P("dom", None),
        P("dom", None),
        P("dom", None, None),
        P("dom", None),
    )
    return jax.shard_map(
        per_device,
        mesh=mesh,
        in_specs=placed,
        out_specs=(
            P("dom", "head"),
            P("dom", "head"),
            P(None, "head"),
            P(None, "head"),
            P(None, "head"),
            P("head", None),
        ),
        check_vma=False,
    )
```

```python
import functools

import jax
import jax.numpy as jnp
from jax import lax
from jax.experimental import pallas as pl
from jax.experimental.pallas import tpu as pltpu
from jax.sharding import PartitionSpec as P

HEAD_SIZE = 32
GROUP = 4
SCALE = HEAD_SIZE ** (-0.5)
MASKED = -1e30
F32 = jnp.float32
BF16 = jnp.bfloat16


def split(value):
    high = value.astype(BF16)
    return high, (value - high.astype(F32)).astype(BF16)


def mul(left, right, left_dim=1, right_dim=0):
    return lax.dot_general(
        left, right, (((left_dim,), (right_dim,)), ((), ())), preferred_element_type=F32
    )


def mul3(left, right, left_dim=1, right_dim=0):
    left_high, left_low = left
    right_high, right_low = right
    return (
        mul(left_high, right_high, left_dim, right_dim)
        + mul(left_high, right_low, left_dim, right_dim)
        + mul(left_low, right_high, left_dim, right_dim)
    )


def wide(first, second):
    return jnp.concatenate([first, second], axis=1)


def fold(value):
    half = value.shape[1] // 2
    return value[:, :half] + value[:, half:]


def forward_kernel(entries, ids, *refs):
    feats = refs[:entries]
    (cot_ref, grad_ref, bias_ref, wq_ref, wk_ref, wv_ref, wo_ref,
     out_ref, feat_ref, stat_ref, gq_ref, go_ref) = refs[entries:]
    rows = cot_ref.shape[0]
    cols = wq_ref.shape[1]
    heads = cols // HEAD_SIZE
    inputs = split(jnp.concatenate([ref[...] for ref in feats], axis=0))
    w_query = split(wq_ref[...])
    w_out = split(wo_ref[...])
    pairs = mul3(inputs, split(wide(wk_ref[...], wv_ref[...])))
    key_high, key_low = split(pairs[:, :cols])
    value_high, value_low = split(pairs[:, cols:])
    key_twice, key_both = wide(key_high, key_high), wide(key_high, key_low)
    value_twice, value_both = wide(value_high, value_high), wide(value_high, value_low)
    own = (inputs[0][:rows], inputs[1][:rows])
    query = mul3(own, w_query) * SCALE
    cot = split(cot_ref[...])
    grad_mixed = grad_ref[...]
    bias = bias_ref[0]
    lane = lax.broadcasted_iota(jnp.int32, (rows, cols), 1) // HEAD_SIZE
    stat_lane = lax.broadcasted_iota(jnp.int32, (rows, rows), 1)
    mixed = jnp.zeros((rows, cols), F32)
    grad_query = jnp.zeros((rows, cols), F32)
    stats = jnp.zeros((rows, rows), F32)
    for head in range(heads):
        here = lane == head
        q_high, q_low = split(jnp.where(here, query, 0.0))
        scores = mul(wide(q_high, q_low), key_twice, 1, 1) + mul(q_high, key_low, 1, 1) + bias
        top = jnp.max(scores, axis=1, keepdims=True)
        probs = jnp.exp(scores - top)
        total = jnp.sum(probs, axis=1, keepdims=True)
        p_high, p_low = split(probs)
        weighted = fold(mul(p_high, value_both)) + mul(p_low, value_high)
        inverse = 1.0 / total
        part = jnp.where(here, weighted * inverse, 0.0)
        mixed = mixed + part
        grad_part = jnp.where(here, grad_mixed, 0.0)
        delta = jnp.sum(grad_part * part, axis=1, keepdims=True)
        g_high, g_low = split(grad_part)
        grad_probs = mul(wide(g_high, g_low), value_twice, 1, 1) + mul(g_high, value_low, 1, 1)
        s_high, s_low = split(probs * (grad_probs - delta))
        back = fold(mul(s_high, key_both)) + mul(s_low, key_high)
        grad_query = grad_query + jnp.where(here, back * (inverse * SCALE), 0.0)
        stats = jnp.where(stat_lane == head, top + jnp.log(total), stats)
        stats = jnp.where(stat_lane == heads + head, delta, stats)
    mixed = split(mixed)
    grad_query = split(grad_query)
    out_ref[...] = mul3(mixed, w_out)
    feat_ref[...] = mul3(grad_query, w_query, 1, 1)
    stat_ref[0] = jnp.transpose(stats)[: 2 * heads]

    @pl.when(pl.program_id(0) == 0)
    def _():
        gq_ref[...] = jnp.zeros_like(gq_ref)
        go_ref[...] = jnp.zeros_like(go_ref)

    gq_ref[...] += mul3(own, grad_query, 0, 0)
    go_ref[...] += mul3(mixed, cot, 0, 0)


def attend_forward(ids, all_feats, out_cotangent, grad_mixed, bias, w_query, w_key, w_value, w_out):
    block_count, entries = ids.shape
    node_rows, width = out_cotangent.shape
    rows = node_rows // block_count
    cols = w_query.shape[1]
    heads = cols // HEAD_SIZE

    def picked(entry):
        return pl.BlockSpec((rows, width), lambda b, ids: (ids[b, entry], 0))

    def whole(array):
        return pl.BlockSpec(array.shape, lambda b, ids: (0,) * array.ndim)

    own = pl.BlockSpec((rows, width), lambda b, ids: (b, 0))
    grad_shape = jax.ShapeDtypeStruct((width, cols), F32)
    out_shape = jax.ShapeDtypeStruct((cols, width), F32)
    node_shape = jax.ShapeDtypeStruct((node_rows, width), F32)
    return pl.pallas_call(
        functools.partial(forward_kernel, entries),
        out_shape=(
            node_shape,
            node_shape,
            jax.ShapeDtypeStruct((block_count, 2 * heads, rows), F32),
            grad_shape,
            out_shape,
        ),
        grid_spec=pltpu.PrefetchScalarGridSpec(
            num_scalar_prefetch=1,
            grid=(block_count,),
            in_specs=[picked(entry) for entry in range(entries)]
            + [own, pl.BlockSpec((rows, cols), lambda b, ids: (b, 0))]
            + [pl.BlockSpec((1, 1, entries * rows), lambda b, ids: (b, 0, 0))]
            + [whole(w) for w in (w_query, w_key, w_value, w_out)],
            out_specs=(
                own,
                own,
                pl.BlockSpec((1, 2 * heads, rows), lambda b, ids: (b, 0, 0)),
                whole(grad_shape),
                whole(out_shape),
            ),
        ),
        compiler_params=pltpu.CompilerParams(
            dimension_semantics=("arbitrary",), vmem_limit_bytes=50 * 1024 * 1024
        ),
        name="attend_forward",
    )(ids, *([all_feats] * entries), out_cotangent, grad_mixed, bias, w_query, w_key, w_value, w_out)


def backward_kernel(steps_ref, readers_ref, *refs):
    feats, cots, stats = refs[:GROUP], refs[GROUP:2 * GROUP], refs[2 * GROUP:3 * GROUP]
    (own_ref, bias_ref, part_ref, wq_ref, wk_ref, wv_ref,
     feat_ref, gk_ref, gv_ref, key_mem, value_mem, dk_mem, dv_mem) = refs[3 * GROUP:]
    step = pl.program_id(0)
    rows = own_ref.shape[0]
    cols = wq_ref.shape[1]
    heads = cols // HEAD_SIZE
    lane = lax.broadcasted_iota(jnp.int32, (rows, cols), 1) // HEAD_SIZE
    kind = steps_ref[1, step]

    @pl.when(step == 0)
    def _():
        gk_ref[...] = jnp.zeros_like(gk_ref)
        gv_ref[...] = jnp.zeros_like(gv_ref)

    @pl.when(kind % 2 == 1)
    def _():
        pairs = mul3(split(own_ref[...]), split(wide(wk_ref[...], wv_ref[...])))
        for head in range(heads):
            here = lane == head
            at = pl.ds(head * rows, rows)
            key_mem[at, :] = wide(*split(jnp.where(here, pairs[:, :cols], 0.0)))
            value_mem[at, :] = wide(*split(jnp.where(here, pairs[:, cols:], 0.0)))
        dk_mem[...] = jnp.zeros_like(dk_mem)
        dv_mem[...] = jnp.zeros_like(dv_mem)

    @pl.when(kind >= 4)
    def _():
        inputs = split(jnp.concatenate([ref[...] for ref in feats], axis=0))
        q_high, q_low = split(mul3(inputs, split(wq_ref[...])) * SCALE)
        g_high, g_low = split(jnp.concatenate([ref[...] for ref in cots], axis=0))
        q_twice, q_both = wide(q_high, q_high), wide(q_high, q_low)
        g_twice, g_both = wide(g_high, g_high), wide(g_high, g_low)
        mark_row = lax.broadcasted_iota(jnp.int32, (8, GROUP * rows), 0)
        mark_col = lax.broadcasted_iota(jnp.int32, (8, GROUP * rows), 1)
        marks = (mark_row == mark_col // rows).astype(BF16)
        bias = mul(bias_ref[0].astype(BF16), marks, 0, 0)
        stat = jnp.concatenate([ref[0] for ref in stats], axis=1)
        grad_key = dk_mem[...]
        grad_value = dv_mem[...]
        for head in range(heads):
            here = lane == head
            keys = key_mem[pl.ds(head * rows, rows), :]
            values = value_mem[pl.ds(head * rows, rows), :]
            scores = mul(keys, q_twice, 1, 1) + mul(keys[:, :cols], q_low, 1, 1)
            probs = jnp.exp(scores + (bias - stat[head:head + 1]))
            grad_probs = mul(values, g_twice, 1, 1) + mul(values[:, :cols], g_low, 1, 1)
            grad_scores = probs * (grad_probs - stat[heads + head:heads + head + 1])
            p_high, p_low = split(probs)
            term = fold(mul(p_high, g_both)) + mul(p_low, g_high)
            grad_value = grad_value + jnp.where(here, term, 0.0)
            s_high, s_low = split(grad_scores)
            term = fold(mul(s_high, q_both)) + mul(s_low, q_high)
            grad_key = grad_key + jnp.where(here, term, 0.0)
        dk_mem[...] = grad_key
        dv_mem[...] = grad_value

    @pl.when((kind // 2) % 2 == 1)
    def _():
        grad_key, grad_value = split(dk_mem[...]), split(dv_mem[...])
        own = split(own_ref[...])
        feat_ref[...] = (
            part_ref[...]
            + mul3(grad_key, split(wk_ref[...]), 1, 1)
            + mul3(grad_value, split(wv_ref[...]), 1, 1)
        )
        gk_ref[...] += mul3(own, grad_key, 0, 0)
        gv_ref[...] += mul3(own, grad_value, 0, 0)


def attend_backward(
    steps, readers, all_feats, all_cots, all_stats, own_feats, bias, part,
    w_query, w_key, w_value, rows,
):
    count = steps.shape[1]
    node_rows, width = own_feats.shape
    cols = w_query.shape[1]
    heads = cols // HEAD_SIZE

    def picked(at, lanes, kind):
        return pl.BlockSpec(
            (rows, lanes), lambda s, steps, readers: (readers[kind, s * GROUP + at], 0)
        )

    def picked_stat(at):
        return pl.BlockSpec(
            (1, 2 * heads, rows), lambda s, steps, readers: (readers[0, s * GROUP + at], 0, 0)
        )

    def whole(array):
        return pl.BlockSpec(array.shape, lambda s, steps, readers: (0,) * array.ndim)

    own = pl.BlockSpec((rows, width), lambda s, steps, readers: (steps[0, s], 0))
    grad_shape = jax.ShapeDtypeStruct((width, cols), F32)
    return pl.pallas_call(
        backward_kernel,
        out_shape=(jax.ShapeDtypeStruct((node_rows, width), F32), grad_shape, grad_shape),
        grid_spec=pltpu.PrefetchScalarGridSpec(
            num_scalar_prefetch=2,
            grid=(count,),
            in_specs=[picked(at, width, 1) for at in range(GROUP)]
            + [picked(at, cols, 2) for at in range(GROUP)]
            + [picked_stat(at) for at in range(GROUP)]
            + [own, pl.BlockSpec((1, 8, rows), lambda s, steps, readers: (s, 0, 0)), own]
            + [whole(w) for w in (w_query, w_key, w_value)],
            out_specs=(own, whole(grad_shape), whole(grad_shape)),
            scratch_shapes=[
                pltpu.VMEM((heads * rows, 2 * cols), BF16),
                pltpu.VMEM((heads * rows, 2 * cols), BF16),
                pltpu.VMEM((rows, cols), F32),
                pltpu.VMEM((rows, cols), F32),
            ],
        ),
        compiler_params=pltpu.CompilerParams(
            dimension_semantics=("arbitrary",), vmem_limit_bytes=50 * 1024 * 1024
        ),
        name="attend_backward",
    )(
        steps, readers, *([all_feats] * GROUP), *([all_cots] * GROUP), *([all_stats] * GROUP),
        own_feats, bias, part, w_query, w_key, w_value,
    )


def plan_backward(all_ids, all_mask, me, block_count, pair_limit):
    blocks, entries = all_ids.shape
    candidates = blocks * entries
    flat = all_ids.reshape(-1)
    slot = jnp.where(flat // block_count == me, flat % block_count, block_count)
    order = jnp.arange(candidates, dtype=jnp.int32)
    same = (slot[:, None] == slot[None, :]) & (order[None, :] < order[:, None])
    rank = jnp.sum(same.astype(jnp.int32), axis=1)
    block_range = jnp.arange(block_count, dtype=jnp.int32)
    tally = jnp.sum((slot[None, :] == block_range[:, None]).astype(jnp.int32), axis=1)
    chunks = (tally + GROUP - 1) // GROUP
    ends = jnp.sum(
        jnp.where(block_range[None, :] <= block_range[:, None], chunks[None, :], 0), axis=1
    )
    starts = ends - chunks
    count = (pair_limit + block_count * GROUP) // GROUP
    places = count * GROUP
    start_of = jnp.sum(
        jnp.where(slot[:, None] == block_range[None, :], starts[None, :], 0), axis=1
    )
    place = jnp.where(slot < block_count, start_of * GROUP + rank, places)
    spot = jnp.arange(places, dtype=jnp.int32)
    hit = place[None, :] == spot[:, None]
    source = jnp.sum(jnp.where(hit, order[None, :], 0), axis=1)
    filled = jnp.sum(hit.astype(jnp.int32), axis=1) > 0
    readers = source // entries
    mask = all_mask.reshape(candidates, -1)[source]
    bias = jnp.where((mask > 0) & filled[:, None], 0.0, MASKED)
    bias = bias.reshape(count, GROUP, -1)
    bias = jnp.concatenate([bias, jnp.zeros((count, 8 - GROUP, bias.shape[2]), F32)], axis=1)
    step = jnp.arange(count, dtype=jnp.int32)
    block = jnp.sum((step[:, None] >= ends[None, :]).astype(jnp.int32), axis=1)
    live = block < block_count
    block = jnp.minimum(block, block_count - 1)
    first = jnp.sum((step[:, None] == starts[None, :]).astype(jnp.int32), axis=1) > 0
    last = jnp.sum((step[:, None] == ends[None, :] - 1).astype(jnp.int32), axis=1) > 0
    kind = jnp.where(
        live, first.astype(jnp.int32) + 2 * last.astype(jnp.int32) + 4, 0
    )
    return jnp.stack([block, kind]), readers, bias


def head_scatter(part):
    size = lax.axis_size("head")
    if size != 2:
        return lax.psum_scatter(part, "head", scatter_dimension=1, tiled=True)
    me = lax.axis_index("head")
    half = part.shape[1] // 2
    sent = lax.dynamic_slice_in_dim(part, (1 - me) * half, half, axis=1)
    kept = lax.dynamic_slice_in_dim(part, me * half, half, axis=1)
    return kept + lax.ppermute(sent, "head", [(0, 1), (1, 0)])


def dom_sum(first, second):
    size = lax.axis_size("dom")
    odd = lax.axis_index("dom") % 2 == 1

    def from_across(value, bit):
        return lax.ppermute(value, "dom", [(at, at ^ bit) for at in range(size)])

    mine = jnp.where(odd, second, first) + from_across(jnp.where(odd, first, second), 1)
    bit = 2
    while bit < size:
        mine = mine + from_across(mine, bit)
        bit *= 2
    other = from_across(mine, 1)
    return jnp.where(odd, other, mine), jnp.where(odd, mine, other)


def gather_feats(part, block_count):
    size, me = lax.axis_size("dom"), lax.axis_index("dom")
    if size != 16 or lax.axis_size("head") != 2 or block_count != 8:
        return lax.all_gather(part, "dom", axis=0, tiled=True), lambda ids: ids, part
    side = lax.axis_index("head")
    rows = part.shape[0] // block_count
    total = size * block_count

    ring = [0, 2, 4, 6, 7, 5, 3, 1]
    onward, back = [], []
    for at in range(8):
        for core in range(2):
            here, there = 2 * ring[at] + core, 2 * ring[(at + 1) % 8] + core
            onward.append((here, there))
            back.append((there, here))
    across = [(at, at ^ 1) for at in range(size)]
    other_head = [(0, 1), (1, 0)]

    def blocks(value, start, count):
        return lax.slice_in_dim(value, start * rows, (start + count) * rows, axis=0)

    def lacking(value):
        return lax.dynamic_slice_in_dim(value, 2 * side * rows, 3 * rows, axis=0)

    result = jnp.zeros((total * rows, part.shape[1]), F32)

    def put(value, start):
        nonlocal result
        result = lax.dynamic_update_slice_in_dim(result, value, start * rows, axis=0)

    half = total // 2
    put(part, 0)

    def swap(value):
        return lax.ppermute(value, "dom", across)

    start = lax.dynamic_slice_in_dim(part, 3 * side * rows, 5 * rows, axis=0)
    held = (lax.ppermute(start, "dom", onward), lax.ppermute(start, "dom", back))
    twin = swap(part)
    held, twin = lax.optimization_barrier((held, twin))
    put(twin, half)
    slots, lack, lack_slots = (1, 2), (), ()
    for step in range(1, 5):
        if step < 3:
            coming = (
                lax.ppermute(held[0], "dom", onward), lax.ppermute(held[1], "dom", back)
            )
        elif step == 3:
            coming = (
                lax.ppermute(blocks(held[0], 0, 3), "dom", onward),
                lax.ppermute(blocks(held[1], 3, 2), "dom", back),
            )
        else:
            coming = ()
        more = tuple(lax.ppermute(lacking(value), "head", other_head) for value in held)
        swapped = tuple(swap(value) for value in held)
        swapped_lack = tuple(swap(value) for value in lack)
        coming, held, more, swapped, lack, swapped_lack = lax.optimization_barrier(
            (coming, held, more, swapped, lack, swapped_lack)
        )
        for at, slot in enumerate(slots):
            put(held[at], slot * block_count)
            put(swapped[at], half + slot * block_count)
        for at, slot in enumerate(lack_slots):
            put(lack[at], slot * block_count + 5)
            put(swapped_lack[at], half + slot * block_count + 5)
        lack, lack_slots = more, slots
        if step == 3:
            held, slots = (jnp.concatenate(coming, axis=0),), (7,)
            late = held[0]
        else:
            held, slots = coming, (2 * step + 1, 2 * step + 2)
    put(lack[0], 7 * block_count + 5)
    put(swap(lack[0]), half + 7 * block_count + 5)

    def chip_place(chip):
        level, column = chip // 2, chip % 2
        return jnp.where(column == 0, level, 7 - level)

    def place(ids):
        owner, block = ids // block_count, ids % block_count
        gap = (chip_place(owner // 2) - chip_place(me // 2)) % 8
        slot = jnp.where(gap < 4, 2 * gap, 2 * (8 - gap) - 1)
        moved = jnp.where(gap == 0, block, (block + 5 * side) % block_count)
        spot = slot * block_count + moved
        return spot + jnp.where(owner % 2 == me % 2, 0, half)

    return result, place, late


def per_device(
    node_features, w_query, w_key, w_value, w_out, nbr_part, nbr_slot, key_mask, out_cotangent
):
    dom_count = lax.axis_size("dom")
    block_count, list_len = nbr_part.shape
    node_rows, width = node_features.shape
    rows = node_rows // block_count
    me = lax.axis_index("dom")
    slot_cap = min(block_count, max(2, (block_count * list_len + dom_count - 1) // dom_count))
    self_ids = me * block_count + jnp.arange(block_count, dtype=jnp.int32)[:, None]
    ids = jnp.concatenate([self_ids, nbr_part * block_count + nbr_slot], axis=1)
    mask = jnp.concatenate([jnp.ones((block_count, 1, rows), jnp.int32), key_mask], axis=1)
    bias = jnp.where(mask > 0, 0.0, MASKED).reshape(block_count, 1, (list_len + 1) * rows)
    all_feats, place, late = gather_feats(node_features, block_count)
    grad_mixed = lax.dot_general(
        out_cotangent, w_out, (((1,), (1,)), ((), ())), precision=lax.Precision.HIGHEST
    )
    cols = w_query.shape[1]
    names = jnp.pad(ids, ((0, 0), (0, rows - list_len - 1))).astype(F32)
    extra = jnp.concatenate([names, key_mask.reshape(-1, rows).astype(F32)], axis=0)
    extra = extra.reshape(-1, cols)
    extra_blocks = -(-extra.shape[0] // rows)
    extra = jnp.pad(extra, ((0, extra_blocks * rows - extra.shape[0]), (0, 0)))
    sent = jnp.concatenate([grad_mixed, extra], axis=0)
    sent, late = lax.optimization_barrier((sent, late))
    all_grads = lax.all_gather(sent, "dom", axis=0, tiled=True)
    extra = all_grads.reshape(dom_count, -1, cols)[:, node_rows:].reshape(dom_count, -1, rows)
    all_ids = extra[:, :block_count, : list_len + 1].astype(jnp.int32)
    all_ids = all_ids.reshape(-1, list_len + 1)
    all_mask = extra[:, block_count:(list_len + 1) * block_count].reshape(-1, list_len, rows)
    all_mask = jnp.concatenate([jnp.ones_like(all_mask[:, :1]), all_mask], axis=1)
    steps, readers, back_bias = plan_backward(
        all_ids, all_mask, me, block_count, dom_count * slot_cap
    )
    grad_spots = readers + readers // block_count * extra_blocks
    out_part, feat_part, stats, grad_query, grad_out = attend_forward(
        place(ids), all_feats, out_cotangent, grad_mixed, bias, w_query, w_key, w_value, w_out
    )
    layer_out = head_scatter(out_part)
    pieces = [grad_out[:, at:at + cols] for at in range(0, width, cols)]
    grad_query, grad_out = dom_sum(grad_query, jnp.concatenate(pieces, axis=0))
    pieces = [grad_out[at:at + cols] for at in range(0, width, cols)]
    grad_out = jnp.concatenate(pieces, axis=1)
    all_stats = lax.all_gather(stats, "dom", axis=0, tiled=True)
    feats_part, grad_key, grad_value = attend_backward(
        steps, jnp.stack([readers, place(readers), grad_spots]), all_feats, all_grads, all_stats, node_features, back_bias, feat_part,
        w_query, w_key, w_value, rows,
    )
    grad_features = head_scatter(feats_part)
    grad_key, grad_value = dom_sum(grad_key, grad_value)
    return (layer_out, grad_features, grad_query, grad_key, grad_value, grad_out)


def solution(mesh):
    placed = (
        P("dom", None),
        P(None, "head"),
        P(None, "head"),
        P(None, "head"),
        P("head", None),
        P("dom", None),
        P("dom", None),
        P("dom", None, None),
        P("dom", None),
    )
    return jax.shard_map(
        per_device,
        mesh=mesh,
        in_specs=placed,
        out_specs=(
            P("dom", "head"),
            P("dom", "head"),
            P(None, "head"),
            P(None, "head"),
            P(None, "head"),
            P("head", None),
        ),
        check_vma=False,
    )
```

```python
import functools

import jax
import jax.numpy as jnp
from jax import lax
from jax.experimental import pallas as pl
from jax.experimental.pallas import tpu as pltpu
from jax.sharding import PartitionSpec as P

HEAD_SIZE = 32
GROUP = 4
SCALE = HEAD_SIZE ** (-0.5)
MASKED = -1e30
F32 = jnp.float32
BF16 = jnp.bfloat16


def split(value):
    high = value.astype(BF16)
    return high, (value - high.astype(F32)).astype(BF16)


def mul(left, right, left_dim=1, right_dim=0):
    return lax.dot_general(
        left, right, (((left_dim,), (right_dim,)), ((), ())), preferred_element_type=F32
    )


def mul3(left, right, left_dim=1, right_dim=0):
    left_high, left_low = left
    right_high, right_low = right
    return (
        mul(left_high, right_high, left_dim, right_dim)
        + mul(left_high, right_low, left_dim, right_dim)
        + mul(left_low, right_high, left_dim, right_dim)
    )


def wide(first, second):
    return jnp.concatenate([first, second], axis=1)


def fold(value):
    half = value.shape[1] // 2
    return value[:, :half] + value[:, half:]


def choose(index, sources, use, base=0):
    if len(sources) == 1:
        use(sources[0])
        return
    half = len(sources) // 2

    @pl.when(index < base + half)
    def _():
        choose(index, sources[:half], use, base)

    @pl.when(index >= base + half)
    def _():
        choose(index, sources[half:], use, base + half)


def fetch(code_of, count, total, sources, target, sem):
    rows = target.shape[0] // count

    def one(at, carry):
        code = code_of(at)
        place = pl.ds(pl.multiple_of(code % total * rows, rows), rows)
        to = target.at[pl.ds(pl.multiple_of(at * rows, rows), rows), :]

        def use(source):
            pltpu.make_async_copy(source.at[place, :], to, sem).start()

        choose(code // total, sources, use)
        return carry

    lax.fori_loop(0, count, one, 0)


def forward_kernel(entries, total, source_count, ids, *refs):
    sources = refs[:source_count]
    (cot_ref, grad_ref, bias_ref, wq_ref, wk_ref, wv_ref, wo_ref,
     out_ref, feat_ref, stat_ref, gq_ref, go_ref, buffer, sems) = refs[source_count:]
    rows = cot_ref.shape[0]
    step = pl.program_id(0)
    turn = step % 2

    def load(at, into):
        fetch(
            lambda entry: ids[at, entry], entries, total, sources, buffer.at[into], sems.at[into]
        )

    @pl.when(step == 0)
    def _():
        load(0, 0)

    @pl.when(step + 1 < pl.num_programs(0))
    def _():
        load(step + 1, 1 - turn)

    pltpu.make_async_copy(buffer.at[turn], buffer.at[turn], sems.at[turn]).wait()
    cols = wq_ref.shape[1]
    heads = cols // HEAD_SIZE
    inputs = split(buffer[turn])
    w_query = split(wq_ref[...])
    w_out = split(wo_ref[...])
    pairs = mul3(inputs, split(wide(wk_ref[...], wv_ref[...])))
    key_high, key_low = split(pairs[:, :cols])
    value_high, value_low = split(pairs[:, cols:])
    key_twice, key_both = wide(key_high, key_high), wide(key_high, key_low)
    value_twice, value_both = wide(value_high, value_high), wide(value_high, value_low)
    own = (inputs[0][:rows], inputs[1][:rows])
    query = mul3(own, w_query) * SCALE
    cot = split(cot_ref[...])
    grad_mixed = grad_ref[...]
    bias = bias_ref[0]
    lane = lax.broadcasted_iota(jnp.int32, (rows, cols), 1) // HEAD_SIZE
    stat_lane = lax.broadcasted_iota(jnp.int32, (rows, rows), 1)
    mixed = jnp.zeros((rows, cols), F32)
    grad_query = jnp.zeros((rows, cols), F32)
    stats = jnp.zeros((rows, rows), F32)
    for head in range(heads):
        here = lane == head
        q_high, q_low = split(jnp.where(here, query, 0.0))
        scores = mul(wide(q_high, q_low), key_twice, 1, 1) + mul(q_high, key_low, 1, 1) + bias
        top = jnp.max(scores, axis=1, keepdims=True)
        probs = jnp.exp(scores - top)
        total = jnp.sum(probs, axis=1, keepdims=True)
        p_high, p_low = split(probs)
        weighted = fold(mul(p_high, value_both)) + mul(p_low, value_high)
        inverse = 1.0 / total
        part = jnp.where(here, weighted * inverse, 0.0)
        mixed = mixed + part
        grad_part = jnp.where(here, grad_mixed, 0.0)
        delta = jnp.sum(grad_part * part, axis=1, keepdims=True)
        g_high, g_low = split(grad_part)
        grad_probs = mul(wide(g_high, g_low), value_twice, 1, 1) + mul(g_high, value_low, 1, 1)
        s_high, s_low = split(probs * (grad_probs - delta))
        back = fold(mul(s_high, key_both)) + mul(s_low, key_high)
        grad_query = grad_query + jnp.where(here, back * (inverse * SCALE), 0.0)
        stats = jnp.where(stat_lane == head, top + jnp.log(total), stats)
        stats = jnp.where(stat_lane == heads + head, delta, stats)
    mixed = split(mixed)
    grad_query = split(grad_query)
    out_ref[...] = mul3(mixed, w_out)
    feat_ref[...] = mul3(grad_query, w_query, 1, 1)
    stat_ref[0] = jnp.transpose(stats)[: 2 * heads]

    @pl.when(pl.program_id(0) == 0)
    def _():
        gq_ref[...] = jnp.zeros_like(gq_ref)
        go_ref[...] = jnp.zeros_like(go_ref)

    gq_ref[...] += mul3(own, grad_query, 0, 0)
    go_ref[...] += mul3(mixed, cot, 0, 0)


def attend_forward(ids, sources, total, out_cotangent, grad_mixed, bias, w_query, w_key, w_value, w_out):
    block_count, entries = ids.shape
    node_rows, width = out_cotangent.shape
    rows = node_rows // block_count
    cols = w_query.shape[1]
    heads = cols // HEAD_SIZE

    def whole(array):
        return pl.BlockSpec(array.shape, lambda b, ids: (0,) * array.ndim)

    own = pl.BlockSpec((rows, width), lambda b, ids: (b, 0))
    grad_shape = jax.ShapeDtypeStruct((width, cols), F32)
    out_shape = jax.ShapeDtypeStruct((cols, width), F32)
    node_shape = jax.ShapeDtypeStruct((node_rows, width), F32)
    return pl.pallas_call(
        functools.partial(forward_kernel, entries, total, len(sources)),
        out_shape=(
            node_shape,
            node_shape,
            jax.ShapeDtypeStruct((block_count, 2 * heads, rows), F32),
            grad_shape,
            out_shape,
        ),
        grid_spec=pltpu.PrefetchScalarGridSpec(
            num_scalar_prefetch=1,
            grid=(block_count,),
            in_specs=[pl.BlockSpec(memory_space=pl.ANY) for _ in sources]
            + [own, pl.BlockSpec((rows, cols), lambda b, ids: (b, 0))]
            + [pl.BlockSpec((1, 1, entries * rows), lambda b, ids: (b, 0, 0))]
            + [whole(w) for w in (w_query, w_key, w_value, w_out)],
            out_specs=(
                own,
                own,
                pl.BlockSpec((1, 2 * heads, rows), lambda b, ids: (b, 0, 0)),
                whole(grad_shape),
                whole(out_shape),
            ),
            scratch_shapes=[
                pltpu.VMEM((2, entries * rows, width), F32),
                pltpu.SemaphoreType.DMA((2,)),
            ],
        ),
        compiler_params=pltpu.CompilerParams(
            dimension_semantics=("arbitrary",), vmem_limit_bytes=50 * 1024 * 1024
        ),
        name="attend_forward",
    )(ids, *sources, out_cotangent, grad_mixed, bias, w_query, w_key, w_value, w_out)


def backward_kernel(total, source_count, steps_ref, readers_ref, *refs):
    cots, stats, refs = refs[:GROUP], refs[GROUP:2 * GROUP], refs[2 * GROUP:]
    sources = refs[:source_count]
    (own_ref, bias_ref, part_ref, wq_ref, wk_ref, wv_ref, feat_ref, gk_ref, gv_ref,
     key_mem, value_mem, dk_mem, dv_mem, buffer, sems) = refs[source_count:]
    step = pl.program_id(0)
    rows = own_ref.shape[0]
    cols = wq_ref.shape[1]
    heads = cols // HEAD_SIZE
    lane = lax.broadcasted_iota(jnp.int32, (rows, cols), 1) // HEAD_SIZE
    kind = steps_ref[1, step]
    turn = step % 2

    def load(at, into):
        fetch(
            lambda reader: readers_ref[1, at * GROUP + reader],
            GROUP, total, sources, buffer.at[into], sems.at[into],
        )

    @pl.when(step == 0)
    def _():
        load(0, 0)

    following = jnp.minimum(step + 1, pl.num_programs(0) - 1)

    @pl.when((following > step) & (steps_ref[1, following] >= 4))
    def _():
        load(step + 1, 1 - turn)

    @pl.when(step == 0)
    def _():
        gk_ref[...] = jnp.zeros_like(gk_ref)
        gv_ref[...] = jnp.zeros_like(gv_ref)

    @pl.when(kind % 2 == 1)
    def _():
        pairs = mul3(split(own_ref[...]), split(wide(wk_ref[...], wv_ref[...])))
        for head in range(heads):
            here = lane == head
            at = pl.ds(head * rows, rows)
            key_mem[at, :] = wide(*split(jnp.where(here, pairs[:, :cols], 0.0)))
            value_mem[at, :] = wide(*split(jnp.where(here, pairs[:, cols:], 0.0)))
        dk_mem[...] = jnp.zeros_like(dk_mem)
        dv_mem[...] = jnp.zeros_like(dv_mem)

    @pl.when(kind >= 4)
    def _():
        pltpu.make_async_copy(buffer.at[turn], buffer.at[turn], sems.at[turn]).wait()
        inputs = split(buffer[turn])
        q_high, q_low = split(mul3(inputs, split(wq_ref[...])) * SCALE)
        g_high, g_low = split(jnp.concatenate([ref[...] for ref in cots], axis=0))
        q_twice, q_both = wide(q_high, q_high), wide(q_high, q_low)
        g_twice, g_both = wide(g_high, g_high), wide(g_high, g_low)
        mark_row = lax.broadcasted_iota(jnp.int32, (8, GROUP * rows), 0)
        mark_col = lax.broadcasted_iota(jnp.int32, (8, GROUP * rows), 1)
        marks = (mark_row == mark_col // rows).astype(BF16)
        bias = mul(bias_ref[0].astype(BF16), marks, 0, 0)
        stat = jnp.concatenate([ref[0] for ref in stats], axis=1)
        grad_key = dk_mem[...]
        grad_value = dv_mem[...]
        for head in range(heads):
            here = lane == head
            keys = key_mem[pl.ds(head * rows, rows), :]
            values = value_mem[pl.ds(head * rows, rows), :]
            scores = mul(keys, q_twice, 1, 1) + mul(keys[:, :cols], q_low, 1, 1)
            probs = jnp.exp(scores + (bias - stat[head:head + 1]))
            grad_probs = mul(values, g_twice, 1, 1) + mul(values[:, :cols], g_low, 1, 1)
            grad_scores = probs * (grad_probs - stat[heads + head:heads + head + 1])
            p_high, p_low = split(probs)
            term = fold(mul(p_high, g_both)) + mul(p_low, g_high)
            grad_value = grad_value + jnp.where(here, term, 0.0)
            s_high, s_low = split(grad_scores)
            term = fold(mul(s_high, q_both)) + mul(s_low, q_high)
            grad_key = grad_key + jnp.where(here, term, 0.0)
        dk_mem[...] = grad_key
        dv_mem[...] = grad_value

    @pl.when((kind // 2) % 2 == 1)
    def _():
        grad_key, grad_value = split(dk_mem[...]), split(dv_mem[...])
        own = split(own_ref[...])
        feat_ref[...] = (
            part_ref[...]
            + mul3(grad_key, split(wk_ref[...]), 1, 1)
            + mul3(grad_value, split(wv_ref[...]), 1, 1)
        )
        gk_ref[...] += mul3(own, grad_key, 0, 0)
        gv_ref[...] += mul3(own, grad_value, 0, 0)


def attend_backward(
    steps, readers, sources, total, all_cots, all_stats, own_feats, bias, part,
    w_query, w_key, w_value, rows,
):
    count = steps.shape[1]
    node_rows, width = own_feats.shape
    cols = w_query.shape[1]
    heads = cols // HEAD_SIZE

    def picked(at, lanes, kind):
        return pl.BlockSpec(
            (rows, lanes), lambda s, steps, readers: (readers[kind, s * GROUP + at], 0)
        )

    def picked_stat(at):
        return pl.BlockSpec(
            (1, 2 * heads, rows), lambda s, steps, readers: (readers[0, s * GROUP + at], 0, 0)
        )

    def whole(array):
        return pl.BlockSpec(array.shape, lambda s, steps, readers: (0,) * array.ndim)

    own = pl.BlockSpec((rows, width), lambda s, steps, readers: (steps[0, s], 0))
    grad_shape = jax.ShapeDtypeStruct((width, cols), F32)
    return pl.pallas_call(
        functools.partial(backward_kernel, total, len(sources)),
        out_shape=(jax.ShapeDtypeStruct((node_rows, width), F32), grad_shape, grad_shape),
        grid_spec=pltpu.PrefetchScalarGridSpec(
            num_scalar_prefetch=2,
            grid=(count,),
            in_specs=[picked(at, cols, 0) for at in range(GROUP)]
            + [picked_stat(at) for at in range(GROUP)]
            + [pl.BlockSpec(memory_space=pl.ANY) for _ in sources]
            + [own, pl.BlockSpec((1, 8, rows), lambda s, steps, readers: (s, 0, 0)), own]
            + [whole(w) for w in (w_query, w_key, w_value)],
            out_specs=(own, whole(grad_shape), whole(grad_shape)),
            scratch_shapes=[
                pltpu.VMEM((heads * rows, 2 * cols), BF16),
                pltpu.VMEM((heads * rows, 2 * cols), BF16),
                pltpu.VMEM((rows, cols), F32),
                pltpu.VMEM((rows, cols), F32),
                pltpu.VMEM((2, GROUP * rows, width), F32),
                pltpu.SemaphoreType.DMA((2,)),
            ],
        ),
        compiler_params=pltpu.CompilerParams(
            dimension_semantics=("arbitrary",), vmem_limit_bytes=50 * 1024 * 1024
        ),
        name="attend_backward",
    )(
        steps, readers, *([all_cots] * GROUP), *([all_stats] * GROUP), *sources,
        own_feats, bias, part, w_query, w_key, w_value,
    )


def plan_backward(all_ids, all_mask, me, block_count, pair_limit):
    blocks, entries = all_ids.shape
    candidates = blocks * entries
    flat = all_ids.reshape(-1)
    slot = jnp.where(flat // block_count == me, flat % block_count, block_count)
    order = jnp.arange(candidates, dtype=jnp.int32)
    same = (slot[:, None] == slot[None, :]) & (order[None, :] < order[:, None])
    rank = jnp.sum(same.astype(jnp.int32), axis=1)
    block_range = jnp.arange(block_count, dtype=jnp.int32)
    tally = jnp.sum((slot[None, :] == block_range[:, None]).astype(jnp.int32), axis=1)
    chunks = (tally + GROUP - 1) // GROUP
    ends = jnp.sum(
        jnp.where(block_range[None, :] <= block_range[:, None], chunks[None, :], 0), axis=1
    )
    starts = ends - chunks
    count = (pair_limit + block_count * GROUP) // GROUP
    places = count * GROUP
    start_of = jnp.sum(
        jnp.where(slot[:, None] == block_range[None, :], starts[None, :], 0), axis=1
    )
    place = jnp.where(slot < block_count, start_of * GROUP + rank, places)
    spot = jnp.arange(places, dtype=jnp.int32)
    hit = place[None, :] == spot[:, None]
    source = jnp.sum(jnp.where(hit, order[None, :], 0), axis=1)
    filled = jnp.sum(hit.astype(jnp.int32), axis=1) > 0
    readers = source // entries
    mask = all_mask.reshape(candidates, -1)[source]
    bias = jnp.where((mask > 0) & filled[:, None], 0.0, MASKED)
    bias = bias.reshape(count, GROUP, -1)
    bias = jnp.concatenate([bias, jnp.zeros((count, 8 - GROUP, bias.shape[2]), F32)], axis=1)
    step = jnp.arange(count, dtype=jnp.int32)
    block = jnp.sum((step[:, None] >= ends[None, :]).astype(jnp.int32), axis=1)
    live = block < block_count
    block = jnp.minimum(block, block_count - 1)
    first = jnp.sum((step[:, None] == starts[None, :]).astype(jnp.int32), axis=1) > 0
    last = jnp.sum((step[:, None] == ends[None, :] - 1).astype(jnp.int32), axis=1) > 0
    kind = jnp.where(
        live, first.astype(jnp.int32) + 2 * last.astype(jnp.int32) + 4, 0
    )
    return jnp.stack([block, kind]), readers, bias


def head_scatter(part):
    size = lax.axis_size("head")
    if size != 2:
        return lax.psum_scatter(part, "head", scatter_dimension=1, tiled=True)
    me = lax.axis_index("head")
    half = part.shape[1] // 2
    sent = lax.dynamic_slice_in_dim(part, (1 - me) * half, half, axis=1)
    kept = lax.dynamic_slice_in_dim(part, me * half, half, axis=1)
    return kept + lax.ppermute(sent, "head", [(0, 1), (1, 0)])


def dom_sum(first, second):
    size = lax.axis_size("dom")
    odd = lax.axis_index("dom") % 2 == 1

    def from_across(value, bit):
        return lax.ppermute(value, "dom", [(at, at ^ bit) for at in range(size)])

    mine = jnp.where(odd, second, first) + from_across(jnp.where(odd, first, second), 1)
    bit = 2
    while bit < size:
        mine = mine + from_across(mine, bit)
        bit *= 2
    other = from_across(mine, 1)
    return jnp.where(odd, other, mine), jnp.where(odd, mine, other)


def double(value, bit):
    size, me = lax.axis_size("dom"), lax.axis_index("dom")
    other = lax.ppermute(value, "dom", [(at, at ^ bit) for at in range(size)])
    upper = me & bit != 0
    low, high = jnp.where(upper, other, value), jnp.where(upper, value, other)
    return jnp.concatenate([low, high], axis=0)


def gather_feats(part, lists, block_count):
    size, me = lax.axis_size("dom"), lax.axis_index("dom")
    if size != 16 or lax.axis_size("head") != 2 or block_count != 8:
        bit = 1
        while bit < size:
            lists, bit = double(lists, bit), bit * 2
        return (lax.all_gather(part, "dom", axis=0, tiled=True),), lambda ids: ids, part, lists
    side = lax.axis_index("head")
    rows = part.shape[0] // block_count
    total = size * block_count

    ring = [0, 2, 4, 6, 7, 5, 3, 1]
    onward, back = [], []
    for at in range(8):
        for core in range(2):
            here, there = 2 * ring[at] + core, 2 * ring[(at + 1) % 8] + core
            onward.append((here, there))
            back.append((there, here))
    across = [(at, at ^ 1) for at in range(size)]
    other_head = [(0, 1), (1, 0)]

    def blocks(value, start, count):
        return lax.slice_in_dim(value, start * rows, (start + count) * rows, axis=0)

    def lacking(value):
        return lax.dynamic_slice_in_dim(value, 2 * side * rows, 3 * rows, axis=0)

    def swap(value):
        return lax.ppermute(value, "dom", across)

    start = lax.dynamic_slice_in_dim(part, 3 * side * rows, 5 * rows, axis=0)
    held = (lax.ppermute(start, "dom", onward), lax.ppermute(start, "dom", back))
    twin = swap(part)
    lists = double(lists, 1)
    held, twin, lists = lax.optimization_barrier((held, twin, lists))
    sources = [None] * 30
    sources[0], sources[1] = part, twin
    slots, lack, lack_slots = (1, 2), (), ()

    def keep(slot, value, swapped, offset):
        sources[4 * slot - 2 + offset] = value
        sources[4 * slot + offset] = swapped

    for step in range(1, 5):
        if step < 3:
            coming = (
                lax.ppermute(held[0], "dom", onward), lax.ppermute(held[1], "dom", back)
            )
        elif step == 3:
            coming = (
                lax.ppermute(blocks(held[0], 0, 3), "dom", onward),
                lax.ppermute(blocks(held[1], 3, 2), "dom", back),
            )
        else:
            coming = ()
        more = tuple(lax.ppermute(lacking(value), "head", other_head) for value in held)
        swapped = tuple(swap(value) for value in held)
        swapped_lack = tuple(swap(value) for value in lack)
        if step < 4:
            lists = double(lists, 1 << step)
        coming, held, more, swapped, lack, swapped_lack, lists = lax.optimization_barrier(
            (coming, held, more, swapped, lack, swapped_lack, lists)
        )
        for at, slot in enumerate(slots):
            keep(slot, held[at], swapped[at], 0)
        for at, slot in enumerate(lack_slots):
            keep(slot, lack[at], swapped_lack[at], 1)
        lack, lack_slots = more, slots
        if step == 3:
            held, slots = (jnp.concatenate(coming, axis=0),), (7,)
            late = held[0]
        else:
            held, slots = coming, (2 * step + 1, 2 * step + 2)
    keep(7, lack[0], swap(lack[0]), 1)

    def chip_place(chip):
        level, column = chip // 2, chip % 2
        return jnp.where(column == 0, level, 7 - level)

    def place(ids):
        owner, block = ids // block_count, ids % block_count
        gap = (chip_place(owner // 2) - chip_place(me // 2)) % 8
        slot = jnp.where(gap < 4, 2 * gap, 2 * (8 - gap) - 1)
        moved = (block + 5 * side) % block_count
        far = owner % 2 != me % 2
        source = 4 * slot - 2 + 2 * far + (moved >= 5)
        inside = jnp.where(moved < 5, moved, moved - 5)
        source = jnp.where(gap == 0, far, source)
        return source * total + jnp.where(gap == 0, block, inside)

    return tuple(sources), place, late, lists


def per_device(
    node_features, w_query, w_key, w_value, w_out, nbr_part, nbr_slot, key_mask, out_cotangent
):
    dom_count = lax.axis_size("dom")
    block_count, list_len = nbr_part.shape
    node_rows, width = node_features.shape
    rows = node_rows // block_count
    me = lax.axis_index("dom")
    slot_cap = min(block_count, max(2, (block_count * list_len + dom_count - 1) // dom_count))
    self_ids = me * block_count + jnp.arange(block_count, dtype=jnp.int32)[:, None]
    ids = jnp.concatenate([self_ids, nbr_part * block_count + nbr_slot], axis=1)
    mask = jnp.concatenate([jnp.ones((block_count, 1, rows), jnp.int32), key_mask], axis=1)
    bias = jnp.where(mask > 0, 0.0, MASKED).reshape(block_count, 1, (list_len + 1) * rows)
    names = jnp.pad(ids, ((0, 0), (0, rows - list_len - 1))).astype(F32)[:, None]
    lists = jnp.concatenate([names, key_mask.astype(F32)], axis=1)
    sources, place, late, lists = gather_feats(node_features, lists, block_count)
    all_ids = lists[:, 0, : list_len + 1].astype(jnp.int32)
    all_mask = jnp.concatenate([jnp.ones_like(lists[:, :1]), lists[:, 1:]], axis=1)
    steps, readers, back_bias = plan_backward(
        all_ids, all_mask, me, block_count, dom_count * slot_cap
    )
    spots = jnp.stack([readers, place(readers)])
    grad_mixed = lax.dot_general(
        out_cotangent, w_out, (((1,), (1,)), ((), ())), precision=lax.Precision.HIGHEST
    )
    sent, late = lax.optimization_barrier((grad_mixed, late))
    all_grads = lax.all_gather(sent, "dom", axis=0, tiled=True)
    sources, steps, spots, back_bias = lax.optimization_barrier(
        (sources, steps, spots, back_bias)
    )
    total = dom_count * block_count
    cols = w_query.shape[1]
    out_part, feat_part, stats, grad_query, grad_out = attend_forward(
        place(ids), sources, total, out_cotangent, grad_mixed, bias, w_query, w_key, w_value, w_out
    )
    layer_out = head_scatter(out_part)
    pieces = [grad_out[:, at:at + cols] for at in range(0, width, cols)]
    grad_query, grad_out = dom_sum(grad_query, jnp.concatenate(pieces, axis=0))
    pieces = [grad_out[at:at + cols] for at in range(0, width, cols)]
    grad_out = jnp.concatenate(pieces, axis=1)
    all_stats = lax.all_gather(stats, "dom", axis=0, tiled=True)
    feats_part, grad_key, grad_value = attend_backward(
        steps, spots, sources, total, all_grads, all_stats, node_features, back_bias, feat_part,
        w_query, w_key, w_value, rows,
    )
    grad_features = head_scatter(feats_part)
    grad_key, grad_value = dom_sum(grad_key, grad_value)
    return (layer_out, grad_features, grad_query, grad_key, grad_value, grad_out)


def solution(mesh):
    placed = (
        P("dom", None),
        P(None, "head"),
        P(None, "head"),
        P(None, "head"),
        P("head", None),
        P("dom", None),
        P("dom", None),
        P("dom", None, None),
        P("dom", None),
    )
    return jax.shard_map(
        per_device,
        mesh=mesh,
        in_specs=placed,
        out_specs=(
            P("dom", "head"),
            P("dom", "head"),
            P(None, "head"),
            P(None, "head"),
            P(None, "head"),
            P("head", None),
        ),
        check_vma=False,
    )
```

```python
import functools

import jax
import jax.numpy as jnp
from jax import lax
from jax.experimental import pallas as pl
from jax.experimental.pallas import tpu as pltpu
from jax.sharding import PartitionSpec as P

HEAD_SIZE = 32
GROUP = 4
SCALE = HEAD_SIZE ** (-0.5)
MASKED = -1e30
F32 = jnp.float32
BF16 = jnp.bfloat16


def split(value):
    high = value.astype(BF16)
    return high, (value - high.astype(F32)).astype(BF16)


def mul(left, right, left_dim=1, right_dim=0):
    return lax.dot_general(
        left, right, (((left_dim,), (right_dim,)), ((), ())), preferred_element_type=F32
    )


def mul3(left, right, left_dim=1, right_dim=0):
    left_high, left_low = left
    right_high, right_low = right
    return (
        mul(left_high, right_high, left_dim, right_dim)
        + mul(left_high, right_low, left_dim, right_dim)
        + mul(left_low, right_high, left_dim, right_dim)
    )


def wide(first, second):
    return jnp.concatenate([first, second], axis=1)


def fold(value):
    half = value.shape[1] // 2
    return value[:, :half] + value[:, half:]


def forward_kernel(entries, layout, ids, *refs):
    sources = refs[:len(layout)]
    (cot_ref, grad_ref, bias_ref, wq_ref, wk_ref, wv_ref, wo_ref,
     all_ref, out_ref, feat_ref, stat_ref, gq_ref, go_ref,
     feats, sems, all_sem) = refs[len(layout):]
    rows = cot_ref.shape[0]
    step = pl.program_id(0)
    keep = pltpu.make_async_copy(feats, all_ref, all_sem)

    @pl.when(step == 0)
    def _():
        copies = []
        for at, (count, block) in enumerate(layout):
            copies.append(
                pltpu.make_async_copy(
                    sources[at].at[pl.ds(0, count), :],
                    feats.at[pl.ds(block * rows, count), :],
                    sems.at[at],
                )
            )
        for copy in copies:
            copy.start()
        for copy in copies:
            copy.wait()
        keep.start()

    listed = [
        feats[pl.ds(pl.multiple_of(ids[step, entry] * rows, rows), rows), :]
        for entry in range(entries)
    ]
    cols = wq_ref.shape[1]
    heads = cols // HEAD_SIZE
    inputs = split(jnp.concatenate(listed, axis=0))
    w_query = split(wq_ref[...])
    w_out = split(wo_ref[...])
    pairs = mul3(inputs, split(wide(wk_ref[...], wv_ref[...])))
    key_high, key_low = split(pairs[:, :cols])
    value_high, value_low = split(pairs[:, cols:])
    key_twice, key_both = wide(key_high, key_high), wide(key_high, key_low)
    value_twice, value_both = wide(value_high, value_high), wide(value_high, value_low)
    own = (inputs[0][:rows], inputs[1][:rows])
    query = mul3(own, w_query) * SCALE
    cot = split(cot_ref[...])
    grad_mixed = grad_ref[...]
    bias = bias_ref[0]
    lane = lax.broadcasted_iota(jnp.int32, (rows, cols), 1) // HEAD_SIZE
    stat_lane = lax.broadcasted_iota(jnp.int32, (rows, rows), 1)
    mixed = jnp.zeros((rows, cols), F32)
    grad_query = jnp.zeros((rows, cols), F32)
    stats = jnp.zeros((rows, rows), F32)
    for head in range(heads):
        here = lane == head
        q_high, q_low = split(jnp.where(here, query, 0.0))
        scores = mul(wide(q_high, q_low), key_twice, 1, 1) + mul(q_high, key_low, 1, 1) + bias
        top = jnp.max(scores, axis=1, keepdims=True)
        probs = jnp.exp(scores - top)
        total = jnp.sum(probs, axis=1, keepdims=True)
        p_high, p_low = split(probs)
        weighted = fold(mul(p_high, value_both)) + mul(p_low, value_high)
        inverse = 1.0 / total
        part = jnp.where(here, weighted * inverse, 0.0)
        mixed = mixed + part
        grad_part = jnp.where(here, grad_mixed, 0.0)
        delta = jnp.sum(grad_part * part, axis=1, keepdims=True)
        g_high, g_low = split(grad_part)
        grad_probs = mul(wide(g_high, g_low), value_twice, 1, 1) + mul(g_high, value_low, 1, 1)
        s_high, s_low = split(probs * (grad_probs - delta))
        back = fold(mul(s_high, key_both)) + mul(s_low, key_high)
        grad_query = grad_query + jnp.where(here, back * (inverse * SCALE), 0.0)
        stats = jnp.where(stat_lane == head, top + jnp.log(total), stats)
        stats = jnp.where(stat_lane == heads + head, delta, stats)
    mixed = split(mixed)
    grad_query = split(grad_query)
    out_ref[...] = mul3(mixed, w_out)
    feat_ref[...] = mul3(grad_query, w_query, 1, 1)
    stat_ref[0] = jnp.transpose(stats)[: 2 * heads]

    @pl.when(pl.program_id(0) == 0)
    def _():
        gq_ref[...] = jnp.zeros_like(gq_ref)
        go_ref[...] = jnp.zeros_like(go_ref)

    gq_ref[...] += mul3(own, grad_query, 0, 0)
    go_ref[...] += mul3(mixed, cot, 0, 0)

    @pl.when(step == pl.num_programs(0) - 1)
    def _():
        keep.wait()


def attend_forward(ids, pieces, total, out_cotangent, grad_mixed, bias, w_query, w_key, w_value, w_out):
    block_count, entries = ids.shape
    node_rows, width = out_cotangent.shape
    rows = node_rows // block_count
    cols = w_query.shape[1]
    heads = cols // HEAD_SIZE

    layout = [(count, block) for _, count, block in pieces]
    all_shape = jax.ShapeDtypeStruct((total * rows, width), F32)

    def whole(array):
        return pl.BlockSpec(array.shape, lambda b, ids: (0,) * array.ndim)

    own = pl.BlockSpec((rows, width), lambda b, ids: (b, 0))
    grad_shape = jax.ShapeDtypeStruct((width, cols), F32)
    out_shape = jax.ShapeDtypeStruct((cols, width), F32)
    node_shape = jax.ShapeDtypeStruct((node_rows, width), F32)
    return pl.pallas_call(
        functools.partial(forward_kernel, entries, layout),
        out_shape=(
            all_shape,
            node_shape,
            node_shape,
            jax.ShapeDtypeStruct((block_count, 2 * heads, rows), F32),
            grad_shape,
            out_shape,
        ),
        grid_spec=pltpu.PrefetchScalarGridSpec(
            num_scalar_prefetch=1,
            grid=(block_count,),
            in_specs=[pl.BlockSpec(memory_space=pl.ANY) for _ in pieces]
            + [own, pl.BlockSpec((rows, cols), lambda b, ids: (b, 0))]
            + [pl.BlockSpec((1, 1, entries * rows), lambda b, ids: (b, 0, 0))]
            + [whole(w) for w in (w_query, w_key, w_value, w_out)],
            out_specs=(
                pl.BlockSpec(memory_space=pl.ANY),
                own,
                own,
                pl.BlockSpec((1, 2 * heads, rows), lambda b, ids: (b, 0, 0)),
                whole(grad_shape),
                whole(out_shape),
            ),
            scratch_shapes=[
                pltpu.VMEM((total * rows, width), F32),
                pltpu.SemaphoreType.DMA((len(layout),)),
                pltpu.SemaphoreType.DMA,
            ],
        ),
        compiler_params=pltpu.CompilerParams(
            dimension_semantics=("arbitrary",), vmem_limit_bytes=56 * 1024 * 1024
        ),
        name="attend_forward",
    )(ids, *[array for array, _, _ in pieces], out_cotangent, grad_mixed, bias, w_query, w_key, w_value, w_out)


def backward_kernel(steps_ref, readers_ref, *refs):
    feats, cots, stats = refs[:GROUP], refs[GROUP:2 * GROUP], refs[2 * GROUP:3 * GROUP]
    lists = refs[3 * GROUP:4 * GROUP]
    (own_ref, part_ref, wq_ref, wk_ref, wv_ref,
     feat_ref, gk_ref, gv_ref, key_mem, value_mem, dk_mem, dv_mem) = refs[4 * GROUP:]
    step = pl.program_id(0)
    rows = own_ref.shape[0]
    cols = wq_ref.shape[1]
    heads = cols // HEAD_SIZE
    lane = lax.broadcasted_iota(jnp.int32, (rows, cols), 1) // HEAD_SIZE
    kind = steps_ref[1, step]

    @pl.when(step == 0)
    def _():
        gk_ref[...] = jnp.zeros_like(gk_ref)
        gv_ref[...] = jnp.zeros_like(gv_ref)

    @pl.when(kind % 2 == 1)
    def _():
        pairs = mul3(split(own_ref[...]), split(wide(wk_ref[...], wv_ref[...])))
        for head in range(heads):
            here = lane == head
            at = pl.ds(head * rows, rows)
            key_mem[at, :] = wide(*split(jnp.where(here, pairs[:, :cols], 0.0)))
            value_mem[at, :] = wide(*split(jnp.where(here, pairs[:, cols:], 0.0)))
        dk_mem[...] = jnp.zeros_like(dk_mem)
        dv_mem[...] = jnp.zeros_like(dv_mem)

    @pl.when(kind >= 4)
    def _():
        inputs = split(jnp.concatenate([ref[...] for ref in feats], axis=0))
        q_high, q_low = split(mul3(inputs, split(wq_ref[...])) * SCALE)
        g_high, g_low = split(jnp.concatenate([ref[...] for ref in cots], axis=0))
        q_twice, q_both = wide(q_high, q_high), wide(q_high, q_low)
        g_twice, g_both = wide(g_high, g_high), wide(g_high, g_low)
        mark_row = lax.broadcasted_iota(jnp.int32, (8, GROUP * rows), 0)
        mark_col = lax.broadcasted_iota(jnp.int32, (8, GROUP * rows), 1)
        marks = (mark_row == mark_col // rows).astype(BF16)
        masks = []
        for at, ref in enumerate(lists):
            entry = readers_ref[2, step * GROUP + at]
            row = ref[0, pl.ds(jnp.maximum(entry, 0), 1), :]
            kept = ((row > 0) | (entry == 0)) & (entry >= 0)
            masks.append(jnp.where(kept, 0.0, MASKED))
        masks.append(jnp.zeros((8 - GROUP, rows), F32))
        bias = mul(jnp.concatenate(masks, axis=0).astype(BF16), marks, 0, 0)
        stat = jnp.concatenate([ref[0] for ref in stats], axis=1)
        grad_key = dk_mem[...]
        grad_value = dv_mem[...]
        for head in range(heads):
            here = lane == head
            keys = key_mem[pl.ds(head * rows, rows), :]
            values = value_mem[pl.ds(head * rows, rows), :]
            scores = mul(keys, q_twice, 1, 1) + mul(keys[:, :cols], q_low, 1, 1)
            probs = jnp.exp(scores + (bias - stat[head:head + 1]))
            grad_probs = mul(values, g_twice, 1, 1) + mul(values[:, :cols], g_low, 1, 1)
            grad_scores = probs * (grad_probs - stat[heads + head:heads + head + 1])
            p_high, p_low = split(probs)
            term = fold(mul(p_high, g_both)) + mul(p_low, g_high)
            grad_value = grad_value + jnp.where(here, term, 0.0)
            s_high, s_low = split(grad_scores)
            term = fold(mul(s_high, q_both)) + mul(s_low, q_high)
            grad_key = grad_key + jnp.where(here, term, 0.0)
        dk_mem[...] = grad_key
        dv_mem[...] = grad_value

    @pl.when((kind // 2) % 2 == 1)
    def _():
        grad_key, grad_value = split(dk_mem[...]), split(dv_mem[...])
        own = split(own_ref[...])
        feat_ref[...] = (
            part_ref[...]
            + mul3(grad_key, split(wk_ref[...]), 1, 1)
            + mul3(grad_value, split(wv_ref[...]), 1, 1)
        )
        gk_ref[...] += mul3(own, grad_key, 0, 0)
        gv_ref[...] += mul3(own, grad_value, 0, 0)


def attend_backward(
    steps, readers, all_feats, all_cots, all_stats, lists, own_feats, part,
    w_query, w_key, w_value, rows,
):
    count = steps.shape[1]
    node_rows, width = own_feats.shape
    cols = w_query.shape[1]
    heads = cols // HEAD_SIZE

    def picked(at, lanes, kind):
        return pl.BlockSpec(
            (rows, lanes), lambda s, steps, readers: (readers[kind, s * GROUP + at], 0)
        )

    def picked_row(at, array, kind):
        return pl.BlockSpec(
            (1,) + array.shape[1:],
            lambda s, steps, readers: (readers[kind, s * GROUP + at], 0, 0),
        )

    def whole(array):
        return pl.BlockSpec(array.shape, lambda s, steps, readers: (0,) * array.ndim)

    own = pl.BlockSpec((rows, width), lambda s, steps, readers: (steps[0, s], 0))
    grad_shape = jax.ShapeDtypeStruct((width, cols), F32)
    return pl.pallas_call(
        backward_kernel,
        out_shape=(jax.ShapeDtypeStruct((node_rows, width), F32), grad_shape, grad_shape),
        grid_spec=pltpu.PrefetchScalarGridSpec(
            num_scalar_prefetch=2,
            grid=(count,),
            in_specs=[picked(at, width, 1) for at in range(GROUP)]
            + [picked(at, cols, 0) for at in range(GROUP)]
            + [picked_row(at, all_stats, 0) for at in range(GROUP)]
            + [picked_row(at, lists, 3) for at in range(GROUP)]
            + [own, own]
            + [whole(w) for w in (w_query, w_key, w_value)],
            out_specs=(own, whole(grad_shape), whole(grad_shape)),
            scratch_shapes=[
                pltpu.VMEM((heads * rows, 2 * cols), BF16),
                pltpu.VMEM((heads * rows, 2 * cols), BF16),
                pltpu.VMEM((rows, cols), F32),
                pltpu.VMEM((rows, cols), F32),
            ],
        ),
        compiler_params=pltpu.CompilerParams(
            dimension_semantics=("arbitrary",), vmem_limit_bytes=50 * 1024 * 1024
        ),
        name="attend_backward",
    )(
        steps, readers, *([all_feats] * GROUP), *([all_cots] * GROUP), *([all_stats] * GROUP),
        *([lists] * GROUP), own_feats, part, w_query, w_key, w_value,
    )


def plan_backward(all_ids, me, block_count, pair_limit):
    blocks, entries = all_ids.shape
    candidates = blocks * entries
    flat = all_ids.reshape(-1)
    slot = jnp.where(flat // block_count == me, flat % block_count, block_count)
    order = jnp.arange(candidates, dtype=jnp.int32)
    same = (slot[:, None] == slot[None, :]) & (order[None, :] < order[:, None])
    rank = jnp.sum(same.astype(jnp.int32), axis=1)
    block_range = jnp.arange(block_count, dtype=jnp.int32)
    tally = jnp.sum((slot[None, :] == block_range[:, None]).astype(jnp.int32), axis=1)
    chunks = (tally + GROUP - 1) // GROUP
    ends = jnp.sum(
        jnp.where(block_range[None, :] <= block_range[:, None], chunks[None, :], 0), axis=1
    )
    starts = ends - chunks
    count = (pair_limit + block_count * GROUP) // GROUP
    places = count * GROUP
    start_of = jnp.sum(
        jnp.where(slot[:, None] == block_range[None, :], starts[None, :], 0), axis=1
    )
    place = jnp.where(slot < block_count, start_of * GROUP + rank, places)
    spot = jnp.arange(places, dtype=jnp.int32)
    hit = place[None, :] == spot[:, None]
    source = jnp.sum(jnp.where(hit, order[None, :], 0), axis=1)
    filled = jnp.sum(hit.astype(jnp.int32), axis=1) > 0
    readers = source // entries
    entry = jnp.where(filled, source % entries, -1)
    step = jnp.arange(count, dtype=jnp.int32)
    block = jnp.sum((step[:, None] >= ends[None, :]).astype(jnp.int32), axis=1)
    live = block < block_count
    block = jnp.minimum(block, block_count - 1)
    first = jnp.sum((step[:, None] == starts[None, :]).astype(jnp.int32), axis=1) > 0
    last = jnp.sum((step[:, None] == ends[None, :] - 1).astype(jnp.int32), axis=1) > 0
    kind = jnp.where(
        live, first.astype(jnp.int32) + 2 * last.astype(jnp.int32) + 4, 0
    )
    return jnp.stack([block, kind]), readers, entry


def head_scatter(part):
    size = lax.axis_size("head")
    if size != 2:
        return lax.psum_scatter(part, "head", scatter_dimension=1, tiled=True)
    me = lax.axis_index("head")
    half = part.shape[1] // 2
    sent = lax.dynamic_slice_in_dim(part, (1 - me) * half, half, axis=1)
    kept = lax.dynamic_slice_in_dim(part, me * half, half, axis=1)
    return kept + lax.ppermute(sent, "head", [(0, 1), (1, 0)])


def dom_sum(first, second):
    size = lax.axis_size("dom")
    odd = lax.axis_index("dom") % 2 == 1

    def from_across(value, bit):
        return lax.ppermute(value, "dom", [(at, at ^ bit) for at in range(size)])

    mine = jnp.where(odd, second, first) + from_across(jnp.where(odd, first, second), 1)
    bit = 2
    while bit < size:
        mine = mine + from_across(mine, bit)
        bit *= 2
    other = from_across(mine, 1)
    return jnp.where(odd, other, mine), jnp.where(odd, mine, other)


def double(value, bit):
    size, me = lax.axis_size("dom"), lax.axis_index("dom")
    other = lax.ppermute(value, "dom", [(at, at ^ bit) for at in range(size)])
    upper = me & bit != 0
    low, high = jnp.where(upper, other, value), jnp.where(upper, value, other)
    return jnp.concatenate([low, high], axis=0)


def gather_feats(part, lists, block_count, make_plan):
    size, me = lax.axis_size("dom"), lax.axis_index("dom")
    if size != 16 or lax.axis_size("head") != 2 or block_count != 8:
        plan = make_plan(lax.all_gather(lists, "dom", axis=0, tiled=True), lambda ids: ids)
        everything = lax.all_gather(part, "dom", axis=0, tiled=True)
        return [(everything, everything.shape[0], 0)], lambda ids: ids, part, plan
    side = lax.axis_index("head")
    rows = part.shape[0] // block_count
    total = size * block_count

    ring = [0, 2, 4, 6, 7, 5, 3, 1]
    onward, back = [], []
    for at in range(8):
        for core in range(2):
            here, there = 2 * ring[at] + core, 2 * ring[(at + 1) % 8] + core
            onward.append((here, there))
            back.append((there, here))
    across = [(at, at ^ 1) for at in range(size)]
    other_head = [(0, 1), (1, 0)]

    def lacking(value):
        return lax.dynamic_slice_in_dim(value, 2 * side * rows, 3 * rows, axis=0)

    half = total // 2

    def swap(value):
        return lax.ppermute(value, "dom", across)

    def chip_place(chip):
        level, column = chip // 2, chip % 2
        return jnp.where(column == 0, level, 7 - level)

    def place(ids):
        owner, block = ids // block_count, ids % block_count
        gap = (chip_place(owner // 2) - chip_place(me // 2)) % 8
        slot = jnp.where(gap < 4, 2 * gap, 2 * (8 - gap) - 1)
        moved = jnp.where(gap == 0, block, (block + 5 * side) % block_count)
        spot = slot * block_count + moved
        return spot + jnp.where(owner % 2 == me % 2, 0, half)

    notes = lists.reshape(-1, lists.shape[2])
    below = notes.shape[0] // 2
    notes = jnp.concatenate([notes[:below], notes[below:]], axis=1)

    start = lax.dynamic_slice_in_dim(part, 3 * side * rows, 5 * rows, axis=0)
    start = jnp.concatenate([start, notes], axis=0)
    held = (lax.ppermute(start, "dom", onward), lax.ppermute(start, "dom", back))
    twin = swap(part)
    all_notes = [notes, swap(notes)]
    held, twin = lax.optimization_barrier((held, twin))
    pieces = [(part, block_count * rows, 0), (twin, block_count * rows, half)]

    def keep(value, swapped, slot, offset, count):
        pieces.append((value, count * rows, slot * block_count + offset))
        pieces.append((swapped, count * rows, half + slot * block_count + offset))
        if offset == 0:
            all_notes.extend([value[count * rows:], swapped[count * rows:]])

    slots, lack, lack_slots = (1, 2), (), ()
    for step in range(1, 5):
        if step < 3:
            coming = (
                lax.ppermute(held[0], "dom", onward), lax.ppermute(held[1], "dom", back)
            )
        elif step == 3:
            coming = (
                lax.ppermute(held[0][: 3 * rows], "dom", onward),
                lax.ppermute(held[1][3 * rows:], "dom", back),
            )
        else:
            coming = ()
        more = tuple(lax.ppermute(lacking(value), "head", other_head) for value in held)
        swapped = tuple(swap(value) for value in held)
        swapped_lack = tuple(swap(value) for value in lack)
        if step < 4:
            coming, held, more, swapped, lack, swapped_lack = lax.optimization_barrier(
                (coming, held, more, swapped, lack, swapped_lack)
            )
        else:
            held, swapped, lack, swapped_lack = lax.optimization_barrier(
                (held, swapped, lack, swapped_lack)
            )
        for at, slot in enumerate(slots):
            keep(held[at], swapped[at], slot, 0, 5)
        for at, slot in enumerate(lack_slots):
            keep(lack[at], swapped_lack[at], slot, 5, 3)
        lack, lack_slots = more, slots
        if step == 3:
            held, slots = (jnp.concatenate(coming, axis=0),), (7,)
            late = held[0]
        else:
            held, slots = coming, (2 * step + 1, 2 * step + 2)
    every = jnp.concatenate(all_notes, axis=0)
    width = lists.shape[2]
    every = jnp.concatenate([every[:, :width], every[:, width:]], axis=0)
    plan = make_plan(every.reshape((-1,) + lists.shape[1:]), place)
    lack, plan = lax.optimization_barrier((lack, plan))
    keep(lack[0], swap(lack[0]), 7, 5, 3)
    return pieces, place, late, plan


def per_device(
    node_features, w_query, w_key, w_value, w_out, nbr_part, nbr_slot, key_mask, out_cotangent
):
    dom_count = lax.axis_size("dom")
    block_count, list_len = nbr_part.shape
    node_rows, width = node_features.shape
    rows = node_rows // block_count
    me = lax.axis_index("dom")
    slot_cap = min(block_count, max(2, (block_count * list_len + dom_count - 1) // dom_count))
    self_ids = me * block_count + jnp.arange(block_count, dtype=jnp.int32)[:, None]
    ids = jnp.concatenate([self_ids, nbr_part * block_count + nbr_slot], axis=1)
    mask = jnp.concatenate([jnp.ones((block_count, 1, rows), jnp.int32), key_mask], axis=1)
    bias = jnp.where(mask > 0, 0.0, MASKED).reshape(block_count, 1, (list_len + 1) * rows)
    names = jnp.pad(ids, ((0, 0), (0, rows - list_len - 1))).astype(F32)[:, None]
    lists = jnp.concatenate([names, key_mask.astype(F32)], axis=1)

    def make_plan(lists, place):
        all_ids = lists[:, 0, : list_len + 1].astype(jnp.int32)
        steps, rows_of, entry = plan_backward(
            all_ids, me, block_count, dom_count * slot_cap
        )
        readers = all_ids[:, 0][rows_of]
        return steps, jnp.stack([readers, place(readers), entry, rows_of]), lists

    pieces, place, late, (steps, spots, lists) = gather_feats(
        node_features, lists, block_count, make_plan
    )
    grad_mixed = lax.dot_general(
        out_cotangent, w_out, (((1,), (1,)), ((), ())), precision=lax.Precision.HIGHEST
    )
    sent, late = lax.optimization_barrier((grad_mixed, late))
    all_grads = lax.all_gather(sent, "dom", axis=0, tiled=True)
    cols = w_query.shape[1]
    all_feats, out_part, feat_part, stats, grad_query, grad_out = attend_forward(
        place(ids), pieces, dom_count * block_count, out_cotangent, grad_mixed, bias, w_query, w_key, w_value, w_out
    )
    layer_out = head_scatter(out_part)
    pieces = [grad_out[:, at:at + cols] for at in range(0, width, cols)]
    grad_query, grad_out = dom_sum(grad_query, jnp.concatenate(pieces, axis=0))
    pieces = [grad_out[at:at + cols] for at in range(0, width, cols)]
    grad_out = jnp.concatenate(pieces, axis=1)
    all_stats = lax.all_gather(stats, "dom", axis=0, tiled=True)
    feats_part, grad_key, grad_value = attend_backward(
        steps, spots, all_feats, all_grads, all_stats, lists, node_features, feat_part,
        w_query, w_key, w_value, rows,
    )
    grad_features = head_scatter(feats_part)
    grad_key, grad_value = dom_sum(grad_key, grad_value)
    return (layer_out, grad_features, grad_query, grad_key, grad_value, grad_out)


def solution(mesh):
    placed = (
        P("dom", None),
        P(None, "head"),
        P(None, "head"),
        P(None, "head"),
        P("head", None),
        P("dom", None),
        P("dom", None),
        P("dom", None, None),
        P("dom", None),
    )
    return jax.shard_map(
        per_device,
        mesh=mesh,
        in_specs=placed,
        out_specs=(
            P("dom", "head"),
            P("dom", "head"),
            P(None, "head"),
            P(None, "head"),
            P(None, "head"),
            P("head", None),
        ),
        check_vma=False,
    )
```

```python
import functools

import jax
import jax.numpy as jnp
from jax import lax
from jax.experimental import pallas as pl
from jax.experimental.pallas import tpu as pltpu
from jax.sharding import PartitionSpec as P

HEAD_SIZE = 32
GROUP = 4
SCALE = HEAD_SIZE ** (-0.5)
MASKED = -1e30
F32 = jnp.float32
BF16 = jnp.bfloat16


def split(value):
    high = value.astype(BF16)
    return high, (value - high.astype(F32)).astype(BF16)


def mul(left, right, left_dim=1, right_dim=0):
    return lax.dot_general(
        left, right, (((left_dim,), (right_dim,)), ((), ())), preferred_element_type=F32
    )


def mul3(left, right, left_dim=1, right_dim=0):
    left_high, left_low = left
    right_high, right_low = right
    return (
        mul(left_high, right_high, left_dim, right_dim)
        + mul(left_high, right_low, left_dim, right_dim)
        + mul(left_low, right_high, left_dim, right_dim)
    )


def wide(first, second):
    return jnp.concatenate([first, second], axis=1)


def fold(value):
    half = value.shape[1] // 2
    return value[:, :half] + value[:, half:]


def forward_kernel(entries, layout, source_count, ids, *refs):
    sources = refs[:source_count]
    (cot_ref, grad_ref, bias_ref, wq_ref, wk_ref, wv_ref, wo_ref,
     all_ref, out_ref, feat_ref, stat_ref, gq_ref, go_ref,
     feats, mixed_mem, grad_mem, sems, all_sem) = refs[source_count:]
    rows = grad_ref.shape[0]
    step = pl.program_id(0)
    keep = pltpu.make_async_copy(feats, all_ref, all_sem)

    @pl.when(step == 0)
    def _():
        copies = []
        for at, (source, row, count, block) in enumerate(layout):
            copies.append(
                pltpu.make_async_copy(
                    sources[source].at[pl.ds(row, count), :],
                    feats.at[pl.ds(block * rows, count), :],
                    sems.at[at],
                )
            )
        for copy in copies:
            copy.start()
        for copy in copies:
            copy.wait()
        keep.start()

    listed = [
        feats[pl.ds(pl.multiple_of(ids[step, entry] * rows, rows), rows), :]
        for entry in range(entries)
    ]
    cols = wq_ref.shape[1]
    heads = cols // HEAD_SIZE
    inputs = split(jnp.concatenate(listed, axis=0))
    w_query = split(wq_ref[...])
    w_out = split(wo_ref[...])
    pairs = mul3(inputs, split(wide(wk_ref[...], wv_ref[...])))
    key_high, key_low = split(pairs[:, :cols])
    value_high, value_low = split(pairs[:, cols:])
    key_both, value_both = wide(key_high, key_low), wide(value_high, value_low)
    turned_high, turned_low = split(jnp.transpose(pairs))
    turned_keys = jnp.concatenate([turned_high[:cols], turned_high[:cols]], axis=0)
    turned_values = jnp.concatenate([turned_high[cols:], turned_high[cols:]], axis=0)
    own = (inputs[0][:rows], inputs[1][:rows])
    query = mul3(own, w_query) * SCALE
    grad_mixed = grad_ref[...]
    lane = lax.broadcasted_iota(jnp.int32, (rows, cols), 1) // HEAD_SIZE
    here = [lane == head for head in range(heads)]

    def spread(value):
        return jnp.concatenate([jnp.where(mask, value, 0.0) for mask in here], axis=0)

    def gather(value):
        parts = [
            jnp.where(mask, value[head * rows:(head + 1) * rows], 0.0)
            for head, mask in enumerate(here)
        ]
        return sum(parts[1:], parts[0])

    q_high, q_low = split(spread(query))
    scores = mul(wide(q_high, q_low), turned_keys) + mul(q_high, turned_low[:cols]) + bias_ref[0]
    top = jnp.max(scores, axis=1, keepdims=True)
    probs = jnp.exp(scores - top)
    total = jnp.sum(probs, axis=1, keepdims=True)
    inverse = 1.0 / total
    p_high, p_low = split(probs)
    weighted = (fold(mul(p_high, value_both)) + mul(p_low, value_high)) * inverse
    mixed = gather(weighted)
    grad_part = spread(grad_mixed)
    delta = jnp.sum(grad_part * weighted, axis=1, keepdims=True)
    g_high, g_low = split(grad_part)
    grad_probs = mul(wide(g_high, g_low), turned_values) + mul(g_high, turned_low[cols:])
    s_high, s_low = split(probs * (grad_probs - delta))
    back = (fold(mul(s_high, key_both)) + mul(s_low, key_high)) * (inverse * SCALE)
    grad_query = gather(back)
    log_total = top + jnp.log(total)
    stat_lane = lax.broadcasted_iota(jnp.int32, (rows, rows), 1)
    stats = jnp.zeros((rows, rows), F32)
    for head in range(heads):
        at = slice(head * rows, (head + 1) * rows)
        stats = jnp.where(stat_lane == head, log_total[at], stats)
        stats = jnp.where(stat_lane == heads + head, delta[at], stats)
    block = pl.ds(pl.multiple_of(step * rows, rows), rows)
    mixed_mem[block, :] = mixed
    grad_mem[block, :] = grad_query
    stat_ref[0] = jnp.transpose(stats)[: 2 * heads]

    @pl.when(step == pl.num_programs(0) - 1)
    def _():
        mixed, grad_query = split(mixed_mem[...]), split(grad_mem[...])
        first = pl.ds(pl.multiple_of(ids[0, 0] * rows, rows), mixed_mem.shape[0])
        out_ref[...] = mul3(mixed, w_out)
        feat_ref[...] = mul3(grad_query, w_query, 1, 1)
        gq_ref[...] = mul3(split(feats[first, :]), grad_query, 0, 0)
        go_ref[...] = mul3(mixed, split(cot_ref[...]), 0, 0)
        keep.wait()


def attend_forward(ids, pieces, total, out_cotangent, grad_mixed, bias, w_query, w_key, w_value, w_out):
    block_count, entries = ids.shape
    node_rows, width = out_cotangent.shape
    rows = node_rows // block_count
    cols = w_query.shape[1]
    heads = cols // HEAD_SIZE

    arrays = []
    for array, *_ in pieces:
        if not any(array is known for known in arrays):
            arrays.append(array)
    layout = [
        ([array is known for known in arrays].index(True), *rest) for array, *rest in pieces
    ]
    all_shape = jax.ShapeDtypeStruct((total * rows, width), F32)

    def whole(array):
        return pl.BlockSpec(array.shape, lambda b, ids: (0,) * array.ndim)

    grad_shape = jax.ShapeDtypeStruct((width, cols), F32)
    out_shape = jax.ShapeDtypeStruct((cols, width), F32)
    node_shape = jax.ShapeDtypeStruct((node_rows, width), F32)
    return pl.pallas_call(
        functools.partial(forward_kernel, entries, layout, len(arrays)),
        out_shape=(
            all_shape,
            node_shape,
            node_shape,
            jax.ShapeDtypeStruct((block_count, 2 * heads, rows), F32),
            grad_shape,
            out_shape,
        ),
        grid_spec=pltpu.PrefetchScalarGridSpec(
            num_scalar_prefetch=1,
            grid=(block_count,),
            in_specs=[pl.BlockSpec(memory_space=pl.ANY) for _ in arrays]
            + [whole(out_cotangent), pl.BlockSpec((rows, cols), lambda b, ids: (b, 0))]
            + [pl.BlockSpec((1, 1, entries * rows), lambda b, ids: (b, 0, 0))]
            + [whole(w) for w in (w_query, w_key, w_value, w_out)],
            out_specs=(
                pl.BlockSpec(memory_space=pl.ANY),
                whole(node_shape),
                whole(node_shape),
                pl.BlockSpec((1, 2 * heads, rows), lambda b, ids: (b, 0, 0)),
                whole(grad_shape),
                whole(out_shape),
            ),
            scratch_shapes=[
                pltpu.VMEM((total * rows, width), F32),
                pltpu.VMEM((node_rows, cols), F32),
                pltpu.VMEM((node_rows, cols), F32),
                pltpu.SemaphoreType.DMA((len(layout),)),
                pltpu.SemaphoreType.DMA,
            ],
        ),
        compiler_params=pltpu.CompilerParams(
            dimension_semantics=("arbitrary",), vmem_limit_bytes=56 * 1024 * 1024
        ),
        name="attend_forward",
    )(ids, *arrays, out_cotangent, grad_mixed, bias, w_query, w_key, w_value, w_out)


def backward_kernel(
    steps_ref, readers_ref, feats_ref, cots_ref, stats_ref, lists_ref, own_ref, part_ref,
    wq_ref, wk_ref, wv_ref, feat_ref, gk_ref, gv_ref,
    pair_mem, key_mem, value_mem, dk_mem, dv_mem, buffer, grads, sems,
):
    rows = buffer.shape[1] // GROUP
    cols = wq_ref.shape[1]
    heads = cols // HEAD_SIZE
    lane = lax.broadcasted_iota(jnp.int32, (rows, cols), 1) // HEAD_SIZE
    count = steps_ref[2, 0]

    def load(step, into):
        for at in range(GROUP):
            to = pl.ds(at * rows, rows)
            spot = readers_ref[1, step * GROUP + at]
            start = pl.ds(pl.multiple_of(spot * rows, rows), rows)
            pltpu.make_async_copy(
                feats_ref.at[start, :], buffer.at[into, to, :], sems.at[0, into]
            ).start()
            spot = readers_ref[0, step * GROUP + at]
            start = pl.ds(pl.multiple_of(spot * rows, rows), rows)
            pltpu.make_async_copy(
                cots_ref.at[start, :], grads.at[into, to, :], sems.at[1, into]
            ).start()

    load(0, 0)
    own = split(own_ref[...])
    pair_mem[...] = mul3(own, split(wide(wk_ref[...], wv_ref[...])))
    dk_mem[...] = jnp.zeros_like(dk_mem)
    dv_mem[...] = jnp.zeros_like(dv_mem)
    w_query = split(wq_ref[...])
    mark_row = lax.broadcasted_iota(jnp.int32, (8, GROUP * rows), 0)
    mark_col = lax.broadcasted_iota(jnp.int32, (8, GROUP * rows), 1)
    marks = (mark_row == mark_col // rows).astype(BF16)

    def chunk(step, carry):
        turn = step % 2
        kind = steps_ref[1, step]
        block = pl.ds(pl.multiple_of(steps_ref[0, step] * rows, rows), rows)

        @pl.when(step + 1 < count)
        def _():
            load(step + 1, 1 - turn)

        @pl.when(kind % 2 == 1)
        def _():
            pairs = pair_mem[block, :]
            for head in range(heads):
                here = lane == head
                at = pl.ds(head * rows, rows)
                key_mem[at, :] = wide(*split(jnp.where(here, pairs[:, :cols], 0.0)))
                value_mem[at, :] = wide(*split(jnp.where(here, pairs[:, cols:], 0.0)))

        pltpu.make_async_copy(buffer.at[turn], buffer.at[turn], sems.at[0, turn]).wait()
        pltpu.make_async_copy(grads.at[turn], grads.at[turn], sems.at[1, turn]).wait()
        query = mul3(split(buffer[turn]), w_query) * SCALE
        grad = grads[turn]
        q_high, q_low = split(query)
        g_high, g_low = split(grad)
        q_both, g_both = wide(q_high, q_low), wide(g_high, g_low)
        turned_high, turned_low = split(jnp.transpose(wide(query, grad)))
        turned_q = jnp.concatenate([turned_high[:cols], turned_high[:cols]], axis=0)
        turned_g = jnp.concatenate([turned_high[cols:], turned_high[cols:]], axis=0)
        masks, stats = [], []
        for at in range(GROUP):
            entry = readers_ref[2, step * GROUP + at]
            row = lists_ref[readers_ref[3, step * GROUP + at], pl.ds(jnp.maximum(entry, 0), 1), :]
            kept = ((row > 0) | (entry == 0)) & (entry >= 0)
            masks.append(jnp.where(kept, 0.0, MASKED))
            stats.append(stats_ref[readers_ref[0, step * GROUP + at]])
        masks.append(jnp.zeros((8 - GROUP, rows), F32))
        bias = mul(jnp.concatenate(masks, axis=0).astype(BF16), marks, 0, 0)
        stat = jnp.concatenate(stats, axis=1)
        keys, values = key_mem[...], value_mem[...]
        scores = mul(keys, turned_q) + mul(keys[:, :cols], turned_low[:cols])
        grad_probs = mul(values, turned_g) + mul(values[:, :cols], turned_low[cols:])

        def rows_of(first):
            return [
                jnp.broadcast_to(stat[first + head:first + head + 1], bias.shape)
                for head in range(heads)
            ]

        shift = jnp.concatenate([bias - each for each in rows_of(0)], axis=0)
        probs = jnp.exp(scores + shift)
        grad_scores = probs * (grad_probs - jnp.concatenate(rows_of(heads), axis=0))
        p_high, p_low = split(probs)
        grad_value = fold(mul(p_high, g_both)) + mul(p_low, g_high)
        s_high, s_low = split(grad_scores)
        grad_key = fold(mul(s_high, q_both)) + mul(s_low, q_high)

        def gathered(value):
            parts = [
                jnp.where(lane == head, value[head * rows:(head + 1) * rows], 0.0)
                for head in range(heads)
            ]
            return sum(parts[1:], parts[0])

        dv_mem[block, :] += gathered(grad_value)
        dk_mem[block, :] += gathered(grad_key)
        return carry

    lax.fori_loop(0, count, chunk, 0)
    grad_key, grad_value = split(dk_mem[...]), split(dv_mem[...])
    feat_ref[...] = (
        part_ref[...]
        + mul3(grad_key, split(wk_ref[...]), 1, 1)
        + mul3(grad_value, split(wv_ref[...]), 1, 1)
    )
    own = split(own_ref[...])
    gk_ref[...] = mul3(own, grad_key, 0, 0)
    gv_ref[...] = mul3(own, grad_value, 0, 0)


def attend_backward(
    steps, readers, all_feats, all_cots, all_stats, lists, own_feats, part,
    w_query, w_key, w_value, rows,
):
    node_rows, width = own_feats.shape
    cols = w_query.shape[1]
    heads = cols // HEAD_SIZE
    held = pl.BlockSpec(memory_space=pltpu.VMEM)
    scalars = pl.BlockSpec(memory_space=pltpu.SMEM)
    afar = pl.BlockSpec(memory_space=pl.ANY)
    grad_shape = jax.ShapeDtypeStruct((width, cols), F32)
    return pl.pallas_call(
        backward_kernel,
        out_shape=(jax.ShapeDtypeStruct((node_rows, width), F32), grad_shape, grad_shape),
        in_specs=[scalars, scalars, afar, afar] + [held] * 7,
        out_specs=(held, held, held),
        scratch_shapes=[
            pltpu.VMEM((node_rows, 2 * cols), F32),
            pltpu.VMEM((heads * rows, 2 * cols), BF16),
            pltpu.VMEM((heads * rows, 2 * cols), BF16),
            pltpu.VMEM((node_rows, cols), F32),
            pltpu.VMEM((node_rows, cols), F32),
            pltpu.VMEM((2, GROUP * rows, width), F32),
            pltpu.VMEM((2, GROUP * rows, cols), F32),
            pltpu.SemaphoreType.DMA((2, 2)),
        ],
        compiler_params=pltpu.CompilerParams(vmem_limit_bytes=50 * 1024 * 1024),
        name="attend_backward",
    )(
        steps, readers, all_feats, all_cots, all_stats, lists, own_feats, part,
        w_query, w_key, w_value,
    )


def plan_backward(all_ids, me, block_count, pair_limit):
    blocks, entries = all_ids.shape
    candidates = blocks * entries
    flat = all_ids.reshape(-1)
    slot = jnp.where(flat // block_count == me, flat % block_count, block_count)
    order = jnp.arange(candidates, dtype=jnp.int32)
    same = (slot[:, None] == slot[None, :]) & (order[None, :] < order[:, None])
    rank = jnp.sum(same.astype(jnp.int32), axis=1)
    block_range = jnp.arange(block_count, dtype=jnp.int32)
    tally = jnp.sum((slot[None, :] == block_range[:, None]).astype(jnp.int32), axis=1)
    chunks = (tally + GROUP - 1) // GROUP
    ends = jnp.sum(
        jnp.where(block_range[None, :] <= block_range[:, None], chunks[None, :], 0), axis=1
    )
    starts = ends - chunks
    count = (pair_limit + block_count * GROUP) // GROUP
    places = count * GROUP
    start_of = jnp.sum(
        jnp.where(slot[:, None] == block_range[None, :], starts[None, :], 0), axis=1
    )
    place = jnp.where(slot < block_count, start_of * GROUP + rank, places)
    spot = jnp.arange(places, dtype=jnp.int32)
    hit = place[None, :] == spot[:, None]
    source = jnp.sum(jnp.where(hit, order[None, :], 0), axis=1)
    filled = jnp.sum(hit.astype(jnp.int32), axis=1) > 0
    readers = source // entries
    entry = jnp.where(filled, source % entries, -1)
    step = jnp.arange(count, dtype=jnp.int32)
    block = jnp.sum((step[:, None] >= ends[None, :]).astype(jnp.int32), axis=1)
    live = block < block_count
    block = jnp.minimum(block, block_count - 1)
    first = jnp.sum((step[:, None] == starts[None, :]).astype(jnp.int32), axis=1) > 0
    last = jnp.sum((step[:, None] == ends[None, :] - 1).astype(jnp.int32), axis=1) > 0
    kind = jnp.where(
        live, first.astype(jnp.int32) + 2 * last.astype(jnp.int32) + 4, 0
    )
    return jnp.stack([block, kind, jnp.full_like(kind, ends[-1])]), readers, entry


def head_scatter(part):
    size = lax.axis_size("head")
    if size != 2:
        return lax.psum_scatter(part, "head", scatter_dimension=1, tiled=True)
    me = lax.axis_index("head")
    half = part.shape[1] // 2
    sent = lax.dynamic_slice_in_dim(part, (1 - me) * half, half, axis=1)
    kept = lax.dynamic_slice_in_dim(part, me * half, half, axis=1)
    return kept + lax.ppermute(sent, "head", [(0, 1), (1, 0)])


def dom_sum(first, second):
    size = lax.axis_size("dom")
    odd = lax.axis_index("dom") % 2 == 1

    def from_across(value, bit):
        return lax.ppermute(value, "dom", [(at, at ^ bit) for at in range(size)])

    mine = jnp.where(odd, second, first) + from_across(jnp.where(odd, first, second), 1)
    bit = 2
    while bit < size:
        mine = mine + from_across(mine, bit)
        bit *= 2
    other = from_across(mine, 1)
    return jnp.where(odd, other, mine), jnp.where(odd, mine, other)


def double(value, bit):
    size, me = lax.axis_size("dom"), lax.axis_index("dom")
    other = lax.ppermute(value, "dom", [(at, at ^ bit) for at in range(size)])
    upper = me & bit != 0
    low, high = jnp.where(upper, other, value), jnp.where(upper, value, other)
    return jnp.concatenate([low, high], axis=0)


def gather_feats(part, lists, block_count, make_plan):
    size, me = lax.axis_size("dom"), lax.axis_index("dom")
    if size != 16 or lax.axis_size("head") != 2 or block_count != 8:
        plan = make_plan(lax.all_gather(lists, "dom", axis=0, tiled=True), lambda ids: ids)
        everything = lax.all_gather(part, "dom", axis=0, tiled=True)
        return [(everything, 0, everything.shape[0], 0)], lambda ids: ids, part, plan
    side = lax.axis_index("head")
    rows = part.shape[0] // block_count
    total = size * block_count

    ring = [0, 2, 4, 6, 7, 5, 3, 1]
    onward, back = [], []
    for at in range(8):
        for core in range(2):
            here, there = 2 * ring[at] + core, 2 * ring[(at + 1) % 8] + core
            onward.append((here, there))
            back.append((there, here))
    across = [(at, at ^ 1) for at in range(size)]
    other_head = [(0, 1), (1, 0)]

    def lacking(value):
        parts = [
            lax.dynamic_slice_in_dim(each, 2 * side * rows, 3 * rows, axis=0) for each in value
        ]
        return jnp.concatenate(parts, axis=0)

    half = total // 2

    def swap(value):
        return lax.ppermute(value, "dom", across)

    def chip_place(chip):
        level, column = chip // 2, chip % 2
        return jnp.where(column == 0, level, 7 - level)

    def place(ids):
        owner, block = ids // block_count, ids % block_count
        gap = (chip_place(owner // 2) - chip_place(me // 2)) % 8
        slot = jnp.where(gap < 4, 2 * gap, 2 * (8 - gap) - 1)
        moved = jnp.where(gap == 0, block, (block + 5 * side) % block_count)
        spot = slot * block_count + moved
        return spot + jnp.where(owner % 2 == me % 2, 0, half)

    notes = lists.reshape(-1, lists.shape[2])
    below = notes.shape[0] // 2
    notes = jnp.concatenate([notes[:below], notes[below:]], axis=1)

    start = lax.dynamic_slice_in_dim(part, 3 * side * rows, 5 * rows, axis=0)
    start = jnp.concatenate([start, notes], axis=0)
    held = (lax.ppermute(start, "dom", onward), lax.ppermute(start, "dom", back))
    twin = swap(part)
    all_notes = [notes, swap(notes)]
    held, twin = lax.optimization_barrier((held, twin))
    pieces = [(part, 0, block_count * rows, 0), (twin, 0, block_count * rows, half)]

    def keep(value, swapped, slots):
        for at, slot in enumerate(slots):
            first = slot * block_count + 5
            pieces.append((value, 3 * at * rows, 3 * rows, first))
            pieces.append((swapped, 3 * at * rows, 3 * rows, half + first))

    slots, lack, lack_slots, notes = (1, 2), (), (), ()
    for step in range(1, 5):
        if step < 3:
            coming = (
                lax.ppermute(held[0], "dom", onward), lax.ppermute(held[1], "dom", back)
            )
        elif step == 3:
            coming = (
                lax.ppermute(held[0][: 3 * rows], "dom", onward),
                lax.ppermute(held[1][3 * rows:], "dom", back),
            )
            notes = jnp.concatenate(all_notes, axis=0)
            all_notes = []
        else:
            coming = ()
        more = (lax.ppermute(lacking(held), "head", other_head),)
        swapped = tuple(swap(value) for value in held)
        swapped_lack = tuple(swap(value) for value in lack)
        if step < 4:
            coming, held, more, swapped, lack, swapped_lack, notes = lax.optimization_barrier(
                (coming, held, more, swapped, lack, swapped_lack, notes)
            )
        else:
            held, swapped, lack, swapped_lack = lax.optimization_barrier(
                (held, swapped, lack, swapped_lack)
            )
        for at, slot in enumerate(slots):
            first = slot * block_count
            pieces.append((held[at], 0, 5 * rows, first))
            pieces.append((swapped[at], 0, 5 * rows, half + first))
            all_notes.extend([held[at][5 * rows:], swapped[at][5 * rows:]])
        if lack:
            keep(lack[0], swapped_lack[0], lack_slots)
        lack, lack_slots = more, slots
        if step == 3:
            held, slots = (jnp.concatenate(coming, axis=0),), (7,)
            late = held[0]
        else:
            held, slots = coming, (2 * step + 1, 2 * step + 2)
    all_notes.insert(0, notes)
    every = jnp.concatenate(all_notes, axis=0)
    width = lists.shape[2]
    every = jnp.concatenate([every[:, :width], every[:, width:]], axis=0)
    plan = make_plan(every.reshape((-1,) + lists.shape[1:]), place)
    lack, plan = lax.optimization_barrier((lack, plan))
    keep(lack[0], swap(lack[0]), (7,))
    return pieces, place, late, plan


def per_device(
    node_features, w_query, w_key, w_value, w_out, nbr_part, nbr_slot, key_mask, out_cotangent
):
    dom_count = lax.axis_size("dom")
    block_count, list_len = nbr_part.shape
    node_rows, width = node_features.shape
    rows = node_rows // block_count
    me = lax.axis_index("dom")
    slot_cap = min(block_count, max(2, (block_count * list_len + dom_count - 1) // dom_count))
    self_ids = me * block_count + jnp.arange(block_count, dtype=jnp.int32)[:, None]
    ids = jnp.concatenate([self_ids, nbr_part * block_count + nbr_slot], axis=1)
    mask = jnp.concatenate([jnp.ones((block_count, 1, rows), jnp.int32), key_mask], axis=1)
    bias = jnp.where(mask > 0, 0.0, MASKED).reshape(block_count, 1, (list_len + 1) * rows)
    names = jnp.pad(ids, ((0, 0), (0, rows - list_len - 1))).astype(F32)[:, None]
    lists = jnp.concatenate([names, key_mask.astype(F32)], axis=1)

    def make_plan(lists, place):
        all_ids = lists[:, 0, : list_len + 1].astype(jnp.int32)
        steps, rows_of, entry = plan_backward(
            all_ids, me, block_count, dom_count * slot_cap
        )
        readers = all_ids[:, 0][rows_of]
        return steps, jnp.stack([readers, place(readers), entry, rows_of]), lists

    pieces, place, late, (steps, spots, lists) = gather_feats(
        node_features, lists, block_count, make_plan
    )
    grad_mixed = lax.dot_general(
        out_cotangent, w_out, (((1,), (1,)), ((), ())), precision=lax.Precision.HIGHEST
    )
    sent, late = lax.optimization_barrier((grad_mixed, late))
    all_grads = lax.all_gather(sent, "dom", axis=0, tiled=True)
    cols = w_query.shape[1]
    all_feats, out_part, feat_part, stats, grad_query, grad_out = attend_forward(
        place(ids), pieces, dom_count * block_count, out_cotangent, grad_mixed, bias, w_query, w_key, w_value, w_out
    )
    layer_out = head_scatter(out_part)
    pieces = [grad_out[:, at:at + cols] for at in range(0, width, cols)]
    grad_query, grad_out = dom_sum(grad_query, jnp.concatenate(pieces, axis=0))
    pieces = [grad_out[at:at + cols] for at in range(0, width, cols)]
    grad_out = jnp.concatenate(pieces, axis=1)
    all_stats = lax.all_gather(stats, "dom", axis=0, tiled=True)
    feats_part, grad_key, grad_value = attend_backward(
        steps, spots, all_feats, all_grads, all_stats, lists, node_features, feat_part,
        w_query, w_key, w_value, rows,
    )
    grad_features = head_scatter(feats_part)
    grad_key, grad_value = dom_sum(grad_key, grad_value)
    return (layer_out, grad_features, grad_query, grad_key, grad_value, grad_out)


def solution(mesh):
    placed = (
        P("dom", None),
        P(None, "head"),
        P(None, "head"),
        P(None, "head"),
        P("head", None),
        P("dom", None),
        P("dom", None),
        P("dom", None, None),
        P("dom", None),
    )
    return jax.shard_map(
        per_device,
        mesh=mesh,
        in_specs=placed,
        out_specs=(
            P("dom", "head"),
            P("dom", "head"),
            P(None, "head"),
            P(None, "head"),
            P(None, "head"),
            P("head", None),
        ),
        check_vma=False,
    )
```

```python
import functools

import jax
import jax.numpy as jnp
from jax import lax
from jax.experimental import pallas as pl
from jax.experimental.pallas import tpu as pltpu
from jax.sharding import PartitionSpec as P

HEAD_SIZE = 32
GROUP = 2
SCALE = HEAD_SIZE ** (-0.5)
MASKED = -1e30
F32 = jnp.float32
BF16 = jnp.bfloat16


def split(value):
    high = value.astype(BF16)
    return high, (value - high.astype(F32)).astype(BF16)


def mul(left, right, left_dim=1, right_dim=0):
    return lax.dot_general(
        left, right, (((left_dim,), (right_dim,)), ((), ())), preferred_element_type=F32
    )


def mul3(left, right, left_dim=1, right_dim=0):
    left_high, left_low = left
    right_high, right_low = right
    return (
        mul(left_high, right_high, left_dim, right_dim)
        + mul(left_high, right_low, left_dim, right_dim)
        + mul(left_low, right_high, left_dim, right_dim)
    )


def wide(first, second):
    return jnp.concatenate([first, second], axis=1)


def pair_left(value):
    rows, cols = value.shape
    span = min(cols, 2 * HEAD_SIZE)
    lane = lax.broadcasted_iota(jnp.int32, (rows, span), 1) // HEAD_SIZE
    result = []
    for first in range(0, cols, span):
        part = value[:, first:first + span]
        parts = [jnp.where(lane == head, part, 0.0) for head in range(span // HEAD_SIZE)]
        high, low = split(jnp.concatenate(parts, axis=0))
        result.append(jnp.concatenate([high, low, high], axis=1))
    return result


def pair_products(lefts, high, low):
    span = high.shape[0] // len(lefts)
    result = []
    for at, left in enumerate(lefts):
        here = slice(at * span, (at + 1) * span)
        right = jnp.concatenate([high[here], high[here], low[here]], axis=0)
        result.append(mul(left, right))
    return jnp.concatenate(result, axis=0)


def fold(value):
    half = value.shape[1] // 2
    return value[:, :half] + value[:, half:]


def forward_kernel(entries, layout, source_count, ids, *refs):
    sources = refs[:source_count]
    (cot_ref, grad_ref, bias_ref, wq_ref, wk_ref, wv_ref, wo_ref,
     all_ref, out_ref, feat_ref, stat_ref, gq_ref, go_ref,
     feats, mixed_mem, grad_mem, sems, all_sem) = refs[source_count:]
    rows = grad_ref.shape[0]
    step = pl.program_id(0)
    keep = pltpu.make_async_copy(feats, all_ref, all_sem)

    @pl.when(step == 0)
    def _():
        copies = []
        for at, (source, row, count, block) in enumerate(layout):
            copies.append(
                pltpu.make_async_copy(
                    sources[source].at[pl.ds(row, count), :],
                    feats.at[pl.ds(block * rows, count), :],
                    sems.at[at],
                )
            )
        for copy in copies:
            copy.start()
        for copy in copies:
            copy.wait()
        keep.start()

    listed = [
        feats[pl.ds(pl.multiple_of(ids[step, entry] * rows, rows), rows), :]
        for entry in range(entries)
    ]
    cols = wq_ref.shape[1]
    heads = cols // HEAD_SIZE
    inputs = split(jnp.concatenate(listed, axis=0))
    w_query = split(wq_ref[...])
    w_out = split(wo_ref[...])
    pairs = mul3(inputs, split(wide(wk_ref[...], wv_ref[...])))
    key_high, key_low = split(pairs[:, :cols])
    value_high, value_low = split(pairs[:, cols:])
    key_both, value_both = wide(key_high, key_low), wide(value_high, value_low)
    turned_high, turned_low = split(jnp.transpose(pairs))
    own = (inputs[0][:rows], inputs[1][:rows])
    query = mul3(own, w_query) * SCALE
    grad_mixed = grad_ref[...]
    lane = lax.broadcasted_iota(jnp.int32, (rows, cols), 1) // HEAD_SIZE
    here = [lane == head for head in range(heads)]

    def spread(value):
        return jnp.concatenate([jnp.where(mask, value, 0.0) for mask in here], axis=0)

    def gather(value):
        parts = [
            jnp.where(mask, value[head * rows:(head + 1) * rows], 0.0)
            for head, mask in enumerate(here)
        ]
        return sum(parts[1:], parts[0])

    scores = pair_products(pair_left(query), turned_high[:cols], turned_low[:cols])
    scores = scores + bias_ref[0]
    top = jnp.max(scores, axis=1, keepdims=True)
    probs = jnp.exp(scores - top)
    total = jnp.sum(probs, axis=1, keepdims=True)
    inverse = 1.0 / total
    p_high, p_low = split(probs)
    weighted = (fold(mul(p_high, value_both)) + mul(p_low, value_high)) * inverse
    mixed = gather(weighted)
    grad_part = spread(grad_mixed)
    delta = jnp.sum(grad_part * weighted, axis=1, keepdims=True)
    grad_probs = pair_products(pair_left(grad_mixed), turned_high[cols:], turned_low[cols:])
    s_high, s_low = split(probs * (grad_probs - delta))
    back = (fold(mul(s_high, key_both)) + mul(s_low, key_high)) * (inverse * SCALE)
    grad_query = gather(back)
    log_total = top + jnp.log(total)
    stat_lane = lax.broadcasted_iota(jnp.int32, (rows, rows), 1)
    stats = jnp.zeros((rows, rows), F32)
    for head in range(heads):
        at = slice(head * rows, (head + 1) * rows)
        stats = jnp.where(stat_lane == head, log_total[at], stats)
        stats = jnp.where(stat_lane == heads + head, delta[at], stats)
    block = pl.ds(pl.multiple_of(step * rows, rows), rows)
    mixed_mem[block, :] = mixed
    grad_mem[block, :] = grad_query
    stat_ref[0] = jnp.transpose(stats)[: 2 * heads]

    @pl.when(step == pl.num_programs(0) - 1)
    def _():
        mixed, grad_query = split(mixed_mem[...]), split(grad_mem[...])
        first = pl.ds(pl.multiple_of(ids[0, 0] * rows, rows), mixed_mem.shape[0])
        out_ref[...] = mul3(mixed, w_out)
        feat_ref[...] = mul3(grad_query, w_query, 1, 1)
        gq_ref[...] = mul3(split(feats[first, :]), grad_query, 0, 0)
        go_ref[...] = mul3(mixed, split(cot_ref[...]), 0, 0)
        keep.wait()


def attend_forward(ids, pieces, total, out_cotangent, grad_mixed, bias, w_query, w_key, w_value, w_out):
    block_count, entries = ids.shape
    node_rows, width = out_cotangent.shape
    rows = node_rows // block_count
    cols = w_query.shape[1]
    heads = cols // HEAD_SIZE

    arrays = []
    for array, *_ in pieces:
        if not any(array is known for known in arrays):
            arrays.append(array)
    layout = [
        ([array is known for known in arrays].index(True), *rest) for array, *rest in pieces
    ]
    all_shape = jax.ShapeDtypeStruct((total * rows, width), F32)

    def whole(array):
        return pl.BlockSpec(array.shape, lambda b, ids: (0,) * array.ndim)

    grad_shape = jax.ShapeDtypeStruct((width, cols), F32)
    out_shape = jax.ShapeDtypeStruct((cols, width), F32)
    node_shape = jax.ShapeDtypeStruct((node_rows, width), F32)
    return pl.pallas_call(
        functools.partial(forward_kernel, entries, layout, len(arrays)),
        out_shape=(
            all_shape,
            node_shape,
            node_shape,
            jax.ShapeDtypeStruct((block_count, 2 * heads, rows), F32),
            grad_shape,
            out_shape,
        ),
        grid_spec=pltpu.PrefetchScalarGridSpec(
            num_scalar_prefetch=1,
            grid=(block_count,),
            in_specs=[pl.BlockSpec(memory_space=pl.ANY) for _ in arrays]
            + [whole(out_cotangent), pl.BlockSpec((rows, cols), lambda b, ids: (b, 0))]
            + [pl.BlockSpec((1, 1, entries * rows), lambda b, ids: (b, 0, 0))]
            + [whole(w) for w in (w_query, w_key, w_value, w_out)],
            out_specs=(
                pl.BlockSpec(memory_space=pl.ANY),
                whole(node_shape),
                whole(node_shape),
                pl.BlockSpec((1, 2 * heads, rows), lambda b, ids: (b, 0, 0)),
                whole(grad_shape),
                whole(out_shape),
            ),
            scratch_shapes=[
                pltpu.VMEM((total * rows, width), F32),
                pltpu.VMEM((node_rows, cols), F32),
                pltpu.VMEM((node_rows, cols), F32),
                pltpu.SemaphoreType.DMA((len(layout),)),
                pltpu.SemaphoreType.DMA,
            ],
        ),
        compiler_params=pltpu.CompilerParams(
            dimension_semantics=("arbitrary",), vmem_limit_bytes=56 * 1024 * 1024
        ),
        name="attend_forward",
    )(ids, *arrays, out_cotangent, grad_mixed, bias, w_query, w_key, w_value, w_out)


def backward_kernel(
    steps_ref, readers_ref, feats_ref, cots_ref, stats_ref, lists_ref, own_ref, part_ref,
    wq_ref, wk_ref, wv_ref, feat_ref, gk_ref, gv_ref,
    pair_mem, key_mem, value_mem, dk_mem, dv_mem, buffer, grads, sems,
):
    rows = buffer.shape[1] // GROUP
    cols = wq_ref.shape[1]
    heads = cols // HEAD_SIZE
    lane = lax.broadcasted_iota(jnp.int32, (rows, cols), 1) // HEAD_SIZE
    count = steps_ref[2, 0]

    def load(step, into):
        for at in range(GROUP):
            to = pl.ds(at * rows, rows)
            spot = readers_ref[1, step * GROUP + at]
            start = pl.ds(pl.multiple_of(spot * rows, rows), rows)
            pltpu.make_async_copy(
                feats_ref.at[start, :], buffer.at[into, to, :], sems.at[0, into]
            ).start()
            spot = readers_ref[0, step * GROUP + at]
            start = pl.ds(pl.multiple_of(spot * rows, rows), rows)
            pltpu.make_async_copy(
                cots_ref.at[start, :], grads.at[into, to, :], sems.at[1, into]
            ).start()

    load(0, 0)
    own = split(own_ref[...])
    pair_mem[...] = mul3(own, split(wide(wk_ref[...], wv_ref[...])))
    dk_mem[...] = jnp.zeros_like(dk_mem)
    dv_mem[...] = jnp.zeros_like(dv_mem)
    w_query = split(wq_ref[...])
    mark_row = lax.broadcasted_iota(jnp.int32, (8, GROUP * rows), 0)
    mark_col = lax.broadcasted_iota(jnp.int32, (8, GROUP * rows), 1)
    marks = (mark_row == mark_col // rows).astype(BF16)

    def chunk(step, carry):
        turn = step % 2
        kind = steps_ref[1, step]
        block = pl.ds(pl.multiple_of(steps_ref[0, step] * rows, rows), rows)

        @pl.when(step + 1 < count)
        def _():
            load(step + 1, 1 - turn)

        @pl.when(kind % 2 == 1)
        def _():
            pairs = pair_mem[block, :]
            for memory, value in ((key_mem, pairs[:, :cols]), (value_mem, pairs[:, cols:])):
                for at, left in enumerate(pair_left(value)):
                    memory[at] = left

        pltpu.make_async_copy(buffer.at[turn], buffer.at[turn], sems.at[0, turn]).wait()
        pltpu.make_async_copy(grads.at[turn], grads.at[turn], sems.at[1, turn]).wait()
        query = mul3(split(buffer[turn]), w_query) * SCALE
        grad = grads[turn]
        q_high, q_low = split(query)
        g_high, g_low = split(grad)
        q_both, g_both = wide(q_high, q_low), wide(g_high, g_low)
        turned_high, turned_low = split(jnp.transpose(wide(query, grad)))
        masks, stats = [], []
        for at in range(GROUP):
            entry = readers_ref[2, step * GROUP + at]
            row = lists_ref[readers_ref[3, step * GROUP + at], pl.ds(jnp.maximum(entry, 0), 1), :]
            kept = ((row > 0) | (entry == 0)) & (entry >= 0)
            masks.append(jnp.where(kept, 0.0, MASKED))
            stats.append(stats_ref[readers_ref[0, step * GROUP + at]])
        masks.append(jnp.zeros((8 - GROUP, rows), F32))
        bias = mul(jnp.concatenate(masks, axis=0).astype(BF16), marks, 0, 0)
        stat = jnp.concatenate(stats, axis=1)
        each = range(key_mem.shape[0])
        scores = pair_products(
            [key_mem[at] for at in each], turned_high[:cols], turned_low[:cols]
        )
        grad_probs = pair_products(
            [value_mem[at] for at in each], turned_high[cols:], turned_low[cols:]
        )

        def rows_of(first):
            return [
                jnp.broadcast_to(stat[first + head:first + head + 1], bias.shape)
                for head in range(heads)
            ]

        shift = jnp.concatenate([bias - each for each in rows_of(0)], axis=0)
        probs = jnp.exp(scores + shift)
        grad_scores = probs * (grad_probs - jnp.concatenate(rows_of(heads), axis=0))
        p_high, p_low = split(probs)
        grad_value = fold(mul(p_high, g_both)) + mul(p_low, g_high)
        s_high, s_low = split(grad_scores)
        grad_key = fold(mul(s_high, q_both)) + mul(s_low, q_high)

        def gathered(value):
            parts = [
                jnp.where(lane == head, value[head * rows:(head + 1) * rows], 0.0)
                for head in range(heads)
            ]
            return sum(parts[1:], parts[0])

        dv_mem[block, :] += gathered(grad_value)
        dk_mem[block, :] += gathered(grad_key)
        return carry

    lax.fori_loop(0, count, chunk, 0)
    grad_key, grad_value = split(dk_mem[...]), split(dv_mem[...])
    feat_ref[...] = (
        part_ref[...]
        + mul3(grad_key, split(wk_ref[...]), 1, 1)
        + mul3(grad_value, split(wv_ref[...]), 1, 1)
    )
    own = split(own_ref[...])
    gk_ref[...] = mul3(own, grad_key, 0, 0)
    gv_ref[...] = mul3(own, grad_value, 0, 0)


def attend_backward(
    steps, readers, all_feats, all_cots, all_stats, lists, own_feats, part,
    w_query, w_key, w_value, rows,
):
    node_rows, width = own_feats.shape
    cols = w_query.shape[1]
    span = min(cols, 2 * HEAD_SIZE)
    held = pl.BlockSpec(memory_space=pltpu.VMEM)
    scalars = pl.BlockSpec(memory_space=pltpu.SMEM)
    afar = pl.BlockSpec(memory_space=pl.ANY)
    grad_shape = jax.ShapeDtypeStruct((width, cols), F32)
    return pl.pallas_call(
        backward_kernel,
        out_shape=(jax.ShapeDtypeStruct((node_rows, width), F32), grad_shape, grad_shape),
        in_specs=[scalars, scalars, afar, afar] + [held] * 7,
        out_specs=(held, held, held),
        scratch_shapes=[
            pltpu.VMEM((node_rows, 2 * cols), F32),
            pltpu.VMEM((cols // span, span // HEAD_SIZE * rows, 3 * span), BF16),
            pltpu.VMEM((cols // span, span // HEAD_SIZE * rows, 3 * span), BF16),
            pltpu.VMEM((node_rows, cols), F32),
            pltpu.VMEM((node_rows, cols), F32),
            pltpu.VMEM((2, GROUP * rows, width), F32),
            pltpu.VMEM((2, GROUP * rows, cols), F32),
            pltpu.SemaphoreType.DMA((2, 2)),
        ],
        compiler_params=pltpu.CompilerParams(vmem_limit_bytes=50 * 1024 * 1024),
        name="attend_backward",
    )(
        steps, readers, all_feats, all_cots, all_stats, lists, own_feats, part,
        w_query, w_key, w_value,
    )


def plan_backward(all_ids, me, block_count, pair_limit):
    blocks, entries = all_ids.shape
    candidates = blocks * entries
    flat = all_ids.reshape(-1)
    slot = jnp.where(flat // block_count == me, flat % block_count, block_count)
    order = jnp.arange(candidates, dtype=jnp.int32)
    same = (slot[:, None] == slot[None, :]) & (order[None, :] < order[:, None])
    rank = jnp.sum(same.astype(jnp.int32), axis=1)
    block_range = jnp.arange(block_count, dtype=jnp.int32)
    tally = jnp.sum((slot[None, :] == block_range[:, None]).astype(jnp.int32), axis=1)
    chunks = (tally + GROUP - 1) // GROUP
    ends = jnp.sum(
        jnp.where(block_range[None, :] <= block_range[:, None], chunks[None, :], 0), axis=1
    )
    starts = ends - chunks
    count = (pair_limit + block_count * GROUP) // GROUP
    places = count * GROUP
    start_of = jnp.sum(
        jnp.where(slot[:, None] == block_range[None, :], starts[None, :], 0), axis=1
    )
    place = jnp.where(slot < block_count, start_of * GROUP + rank, places)
    spot = jnp.arange(places, dtype=jnp.int32)
    hit = place[None, :] == spot[:, None]
    source = jnp.sum(jnp.where(hit, order[None, :], 0), axis=1)
    filled = jnp.sum(hit.astype(jnp.int32), axis=1) > 0
    readers = source // entries
    entry = jnp.where(filled, source % entries, -1)
    step = jnp.arange(count, dtype=jnp.int32)
    block = jnp.sum((step[:, None] >= ends[None, :]).astype(jnp.int32), axis=1)
    live = block < block_count
    block = jnp.minimum(block, block_count - 1)
    first = jnp.sum((step[:, None] == starts[None, :]).astype(jnp.int32), axis=1) > 0
    last = jnp.sum((step[:, None] == ends[None, :] - 1).astype(jnp.int32), axis=1) > 0
    kind = jnp.where(
        live, first.astype(jnp.int32) + 2 * last.astype(jnp.int32) + 4, 0
    )
    return jnp.stack([block, kind, jnp.full_like(kind, ends[-1])]), readers, entry


def head_scatter(part):
    size = lax.axis_size("head")
    if size != 2:
        return lax.psum_scatter(part, "head", scatter_dimension=1, tiled=True)
    me = lax.axis_index("head")
    half = part.shape[1] // 2
    sent = lax.dynamic_slice_in_dim(part, (1 - me) * half, half, axis=1)
    kept = lax.dynamic_slice_in_dim(part, me * half, half, axis=1)
    return kept + lax.ppermute(sent, "head", [(0, 1), (1, 0)])


def dom_sum(first, second):
    size = lax.axis_size("dom")
    odd = lax.axis_index("dom") % 2 == 1

    def from_across(value, bit):
        return lax.ppermute(value, "dom", [(at, at ^ bit) for at in range(size)])

    mine = jnp.where(odd, second, first) + from_across(jnp.where(odd, first, second), 1)
    bit = 2
    while bit < size:
        mine = mine + from_across(mine, bit)
        bit *= 2
    other = from_across(mine, 1)
    return jnp.where(odd, other, mine), jnp.where(odd, mine, other)


def double(value, bit):
    size, me = lax.axis_size("dom"), lax.axis_index("dom")
    other = lax.ppermute(value, "dom", [(at, at ^ bit) for at in range(size)])
    upper = me & bit != 0
    low, high = jnp.where(upper, other, value), jnp.where(upper, value, other)
    return jnp.concatenate([low, high], axis=0)


def gather_feats(part, lists, block_count, make_plan):
    size, me = lax.axis_size("dom"), lax.axis_index("dom")
    if size != 16 or lax.axis_size("head") != 2 or block_count != 8:
        plan = make_plan(lax.all_gather(lists, "dom", axis=0, tiled=True), lambda ids: ids)
        everything = lax.all_gather(part, "dom", axis=0, tiled=True)
        return [(everything, 0, everything.shape[0], 0)], lambda ids: ids, part, plan
    side = lax.axis_index("head")
    rows = part.shape[0] // block_count
    total = size * block_count

    ring = [0, 2, 4, 6, 7, 5, 3, 1]
    onward, back = [], []
    for at in range(8):
        for core in range(2):
            here, there = 2 * ring[at] + core, 2 * ring[(at + 1) % 8] + core
            onward.append((here, there))
            back.append((there, here))
    across = [(at, at ^ 1) for at in range(size)]
    other_head = [(0, 1), (1, 0)]

    def lacking(value):
        parts = [
            lax.dynamic_slice_in_dim(each, 2 * side * rows, 3 * rows, axis=0) for each in value
        ]
        return jnp.concatenate(parts, axis=0)

    half = total // 2

    def swap(value):
        return lax.ppermute(value, "dom", across)

    def chip_place(chip):
        level, column = chip // 2, chip % 2
        return jnp.where(column == 0, level, 7 - level)

    def place(ids):
        owner, block = ids // block_count, ids % block_count
        gap = (chip_place(owner // 2) - chip_place(me // 2)) % 8
        slot = jnp.where(gap < 4, 2 * gap, 2 * (8 - gap) - 1)
        moved = jnp.where(gap == 0, block, (block + 5 * side) % block_count)
        spot = slot * block_count + moved
        return spot + jnp.where(owner % 2 == me % 2, 0, half)

    notes = lists.reshape(-1, lists.shape[2])
    below = notes.shape[0] // 2
    notes = jnp.concatenate([notes[:below], notes[below:]], axis=1)

    start = lax.dynamic_slice_in_dim(part, 3 * side * rows, 5 * rows, axis=0)
    start = jnp.concatenate([start, notes], axis=0)
    held = (lax.ppermute(start, "dom", onward), lax.ppermute(start, "dom", back))
    twin = swap(part)
    all_notes = [notes, swap(notes)]
    held, twin = lax.optimization_barrier((held, twin))
    pieces = [(part, 0, block_count * rows, 0), (twin, 0, block_count * rows, half)]

    def keep(value, swapped, slots):
        for at, slot in enumerate(slots):
            first = slot * block_count + 5
            pieces.append((value, 3 * at * rows, 3 * rows, first))
            pieces.append((swapped, 3 * at * rows, 3 * rows, half + first))

    def keep_ring(values, swapped, slots):
        for at, slot in enumerate(slots):
            first = slot * block_count
            pieces.append((values[at], 0, 5 * rows, first))
            pieces.append((swapped[at], 0, 5 * rows, half + first))
            all_notes.extend([values[at][5 * rows:], swapped[at][5 * rows:]])

    slots, lack, lack_slots, notes = (1, 2), (), (), ()
    for step in range(1, 5):
        if step < 3:
            coming = (
                lax.ppermute(held[0], "dom", onward), lax.ppermute(held[1], "dom", back)
            )
        elif step == 3:
            coming = (
                lax.ppermute(held[0][: 3 * rows], "dom", onward),
                lax.ppermute(held[1][3 * rows:], "dom", back),
            )
            notes = jnp.concatenate(all_notes, axis=0)
            all_notes = []
        else:
            coming = ()
        more = (lax.ppermute(lacking(held), "head", other_head),)
        if step == 3:
            waiting = (held, slots, lack, lack_slots)
            coming, held, more, notes = lax.optimization_barrier((coming, held, more, notes))
        else:
            swapped = tuple(swap(value) for value in held)
            swapped_lack = tuple(swap(value) for value in lack)
            if step < 3:
                coming, held, more, swapped, lack, swapped_lack = lax.optimization_barrier(
                    (coming, held, more, swapped, lack, swapped_lack)
                )
            else:
                old, old_slots, old_lack, old_lack_slots = waiting
                old_swapped = tuple(swap(value) for value in old)
                old_swapped_lack = tuple(swap(value) for value in old_lack)
                held, swapped, lack, swapped_lack, old_swapped, old_swapped_lack = (
                    lax.optimization_barrier(
                        (held, swapped, lack, swapped_lack, old_swapped, old_swapped_lack)
                    )
                )
                keep_ring(old, old_swapped, old_slots)
                keep(old_lack[0], old_swapped_lack[0], old_lack_slots)
            keep_ring(held, swapped, slots)
            if lack:
                keep(lack[0], swapped_lack[0], lack_slots)
        lack, lack_slots = more, slots
        if step == 3:
            held, slots = (jnp.concatenate(coming, axis=0),), (7,)
            late = held[0]
        else:
            held, slots = coming, (2 * step + 1, 2 * step + 2)
    all_notes.insert(0, notes)
    every = jnp.concatenate(all_notes, axis=0)
    width = lists.shape[2]
    every = jnp.concatenate([every[:, :width], every[:, width:]], axis=0)
    plan = make_plan(every.reshape((-1,) + lists.shape[1:]), place)
    lack, plan = lax.optimization_barrier((lack, plan))
    keep(lack[0], swap(lack[0]), (7,))
    return pieces, place, late, plan


def per_device(
    node_features, w_query, w_key, w_value, w_out, nbr_part, nbr_slot, key_mask, out_cotangent
):
    dom_count = lax.axis_size("dom")
    block_count, list_len = nbr_part.shape
    node_rows, width = node_features.shape
    rows = node_rows // block_count
    me = lax.axis_index("dom")
    slot_cap = min(block_count, max(2, (block_count * list_len + dom_count - 1) // dom_count))
    self_ids = me * block_count + jnp.arange(block_count, dtype=jnp.int32)[:, None]
    ids = jnp.concatenate([self_ids, nbr_part * block_count + nbr_slot], axis=1)
    mask = jnp.concatenate([jnp.ones((block_count, 1, rows), jnp.int32), key_mask], axis=1)
    bias = jnp.where(mask > 0, 0.0, MASKED).reshape(block_count, 1, (list_len + 1) * rows)
    names = jnp.pad(ids, ((0, 0), (0, rows - list_len - 1))).astype(F32)[:, None]
    lists = jnp.concatenate([names, key_mask.astype(F32)], axis=1)

    def make_plan(lists, place):
        all_ids = lists[:, 0, : list_len + 1].astype(jnp.int32)
        steps, rows_of, entry = plan_backward(
            all_ids, me, block_count, dom_count * slot_cap
        )
        readers = all_ids[:, 0][rows_of]
        return steps, jnp.stack([readers, place(readers), entry, rows_of]), lists

    pieces, place, late, (steps, spots, lists) = gather_feats(
        node_features, lists, block_count, make_plan
    )
    grad_mixed = lax.dot_general(
        out_cotangent, w_out, (((1,), (1,)), ((), ())), precision=lax.Precision.HIGHEST
    )
    sent, late = lax.optimization_barrier((grad_mixed, late))
    all_grads = lax.all_gather(sent, "dom", axis=0, tiled=True)
    cols = w_query.shape[1]
    all_feats, out_part, feat_part, stats, grad_query, grad_out = attend_forward(
        place(ids), pieces, dom_count * block_count, out_cotangent, grad_mixed, bias, w_query, w_key, w_value, w_out
    )
    layer_out = head_scatter(out_part)
    pieces = [grad_out[:, at:at + cols] for at in range(0, width, cols)]
    grad_query, grad_out = dom_sum(grad_query, jnp.concatenate(pieces, axis=0))
    pieces = [grad_out[at:at + cols] for at in range(0, width, cols)]
    grad_out = jnp.concatenate(pieces, axis=1)
    all_stats = lax.all_gather(stats, "dom", axis=0, tiled=True)
    feats_part, grad_key, grad_value = attend_backward(
        steps, spots, all_feats, all_grads, all_stats, lists, node_features, feat_part,
        w_query, w_key, w_value, rows,
    )
    grad_features = head_scatter(feats_part)
    grad_key, grad_value = dom_sum(grad_key, grad_value)
    return (layer_out, grad_features, grad_query, grad_key, grad_value, grad_out)


def solution(mesh):
    placed = (
        P("dom", None),
        P(None, "head"),
        P(None, "head"),
        P(None, "head"),
        P("head", None),
        P("dom", None),
        P("dom", None),
        P("dom", None, None),
        P("dom", None),
    )
    return jax.shard_map(
        per_device,
        mesh=mesh,
        in_specs=placed,
        out_specs=(
            P("dom", "head"),
            P("dom", "head"),
            P(None, "head"),
            P(None, "head"),
            P(None, "head"),
            P("head", None),
        ),
        check_vma=False,
    )
```

```python
import functools

import jax
import jax.numpy as jnp
from jax import lax
from jax.experimental import pallas as pl
from jax.experimental.pallas import tpu as pltpu
from jax.sharding import PartitionSpec as P

HEAD_SIZE = 32
GROUP = 2
RING = 6
SCALE = HEAD_SIZE ** (-0.5)
MASKED = -1e30
F32 = jnp.float32
BF16 = jnp.bfloat16


def split(value):
    high = value.astype(BF16)
    return high, (value - high.astype(F32)).astype(BF16)


def mul(left, right, left_dim=1, right_dim=0):
    return lax.dot_general(
        left, right, (((left_dim,), (right_dim,)), ((), ())), preferred_element_type=F32
    )


def mul3(left, right, left_dim=1, right_dim=0):
    left_high, left_low = left
    right_high, right_low = right
    return (
        mul(left_high, right_high, left_dim, right_dim)
        + mul(left_high, right_low, left_dim, right_dim)
        + mul(left_low, right_high, left_dim, right_dim)
    )


def wide(first, second):
    return jnp.concatenate([first, second], axis=1)


def pair_left(value):
    rows, cols = value.shape
    span = min(cols, 2 * HEAD_SIZE)
    lane = lax.broadcasted_iota(jnp.int32, (rows, span), 1) // HEAD_SIZE
    result = []
    for first in range(0, cols, span):
        part = value[:, first:first + span]
        parts = [jnp.where(lane == head, part, 0.0) for head in range(span // HEAD_SIZE)]
        high, low = split(jnp.concatenate(parts, axis=0))
        result.append(jnp.concatenate([high, low, high], axis=1))
    return result


def pair_products(lefts, high, low):
    span = high.shape[0] // len(lefts)
    result = []
    for at, left in enumerate(lefts):
        here = slice(at * span, (at + 1) * span)
        right = jnp.concatenate([high[here], high[here], low[here]], axis=0)
        result.append(mul(left, right))
    return jnp.concatenate(result, axis=0)


def fold(value):
    half = value.shape[1] // 2
    return value[:, :half] + value[:, half:]


def forward_kernel(entries, layout, source_count, ids, *refs):
    sources = refs[:source_count]
    (cot_ref, grad_ref, bias_ref, wq_ref, wk_ref, wv_ref, wo_ref,
     all_ref, out_ref, feat_ref, stat_ref, gq_ref, go_ref,
     feats, mixed_mem, grad_mem, sems, all_sem) = refs[source_count:]
    rows = grad_ref.shape[0]
    step = pl.program_id(0)
    keep = pltpu.make_async_copy(feats, all_ref, all_sem)

    @pl.when(step == 0)
    def _():
        copies = []
        for at, (source, row, count, block) in enumerate(layout):
            copies.append(
                pltpu.make_async_copy(
                    sources[source].at[pl.ds(row, count), :],
                    feats.at[pl.ds(block * rows, count), :],
                    sems.at[at],
                )
            )
        for copy in copies:
            copy.start()
        for copy in copies:
            copy.wait()
        keep.start()

    listed = [
        feats[pl.ds(pl.multiple_of(ids[step, entry] * rows, rows), rows), :]
        for entry in range(entries)
    ]
    cols = wq_ref.shape[1]
    heads = cols // HEAD_SIZE
    inputs = split(jnp.concatenate(listed, axis=0))
    w_query = split(wq_ref[...])
    w_out = split(wo_ref[...])
    pairs = mul3(inputs, split(wide(wk_ref[...], wv_ref[...])))
    key_high, key_low = split(pairs[:, :cols])
    value_high, value_low = split(pairs[:, cols:])
    key_both, value_both = wide(key_high, key_low), wide(value_high, value_low)
    turned_high, turned_low = split(jnp.transpose(pairs))
    own = (inputs[0][:rows], inputs[1][:rows])
    query = mul3(own, w_query) * SCALE
    grad_mixed = grad_ref[...]
    lane = lax.broadcasted_iota(jnp.int32, (rows, cols), 1) // HEAD_SIZE
    here = [lane == head for head in range(heads)]

    def spread(value):
        return jnp.concatenate([jnp.where(mask, value, 0.0) for mask in here], axis=0)

    def gather(value):
        parts = [
            jnp.where(mask, value[head * rows:(head + 1) * rows], 0.0)
            for head, mask in enumerate(here)
        ]
        return sum(parts[1:], parts[0])

    scores = pair_products(pair_left(query), turned_high[:cols], turned_low[:cols])
    scores = scores + bias_ref[0]
    top = jnp.max(scores, axis=1, keepdims=True)
    probs = jnp.exp(scores - top)
    total = jnp.sum(probs, axis=1, keepdims=True)
    inverse = 1.0 / total
    p_high, p_low = split(probs)
    weighted = (fold(mul(p_high, value_both)) + mul(p_low, value_high)) * inverse
    mixed = gather(weighted)
    grad_part = spread(grad_mixed)
    delta = jnp.sum(grad_part * weighted, axis=1, keepdims=True)
    grad_probs = pair_products(pair_left(grad_mixed), turned_high[cols:], turned_low[cols:])
    s_high, s_low = split(probs * (grad_probs - delta))
    back = (fold(mul(s_high, key_both)) + mul(s_low, key_high)) * (inverse * SCALE)
    grad_query = gather(back)
    log_total = top + jnp.log(total)
    stat_lane = lax.broadcasted_iota(jnp.int32, (rows, rows), 1)
    stats = jnp.zeros((rows, rows), F32)
    for head in range(heads):
        at = slice(head * rows, (head + 1) * rows)
        stats = jnp.where(stat_lane == head, log_total[at], stats)
        stats = jnp.where(stat_lane == heads + head, delta[at], stats)
    block = pl.ds(pl.multiple_of(step * rows, rows), rows)
    mixed_mem[block, :] = mixed
    grad_mem[block, :] = grad_query
    stat_ref[0] = jnp.transpose(stats)[: 2 * heads]

    @pl.when(step == pl.num_programs(0) - 1)
    def _():
        mixed, grad_query = split(mixed_mem[...]), split(grad_mem[...])
        first = pl.ds(pl.multiple_of(ids[0, 0] * rows, rows), mixed_mem.shape[0])
        out_ref[...] = mul3(mixed, w_out)
        feat_ref[...] = mul3(grad_query, w_query, 1, 1)
        gq_ref[...] = mul3(split(feats[first, :]), grad_query, 0, 0)
        go_ref[...] = mul3(mixed, split(cot_ref[...]), 0, 0)
        keep.wait()


def attend_forward(ids, pieces, total, out_cotangent, grad_mixed, bias, w_query, w_key, w_value, w_out):
    block_count, entries = ids.shape
    node_rows, width = out_cotangent.shape
    rows = node_rows // block_count
    cols = w_query.shape[1]
    heads = cols // HEAD_SIZE

    arrays = []
    for array, *_ in pieces:
        if not any(array is known for known in arrays):
            arrays.append(array)
    layout = [
        ([array is known for known in arrays].index(True), *rest) for array, *rest in pieces
    ]
    all_shape = jax.ShapeDtypeStruct((total * rows, width), F32)

    def whole(array):
        return pl.BlockSpec(array.shape, lambda b, ids: (0,) * array.ndim)

    grad_shape = jax.ShapeDtypeStruct((width, cols), F32)
    out_shape = jax.ShapeDtypeStruct((cols, width), F32)
    node_shape = jax.ShapeDtypeStruct((node_rows, width), F32)
    return pl.pallas_call(
        functools.partial(forward_kernel, entries, layout, len(arrays)),
        out_shape=(
            all_shape,
            node_shape,
            node_shape,
            jax.ShapeDtypeStruct((block_count, 2 * heads, rows), F32),
            grad_shape,
            out_shape,
        ),
        grid_spec=pltpu.PrefetchScalarGridSpec(
            num_scalar_prefetch=1,
            grid=(block_count,),
            in_specs=[pl.BlockSpec(memory_space=pl.ANY) for _ in arrays]
            + [whole(out_cotangent), pl.BlockSpec((rows, cols), lambda b, ids: (b, 0))]
            + [pl.BlockSpec((1, 1, entries * rows), lambda b, ids: (b, 0, 0))]
            + [whole(w) for w in (w_query, w_key, w_value, w_out)],
            out_specs=(
                pl.BlockSpec(memory_space=pl.ANY),
                whole(node_shape),
                whole(node_shape),
                pl.BlockSpec((1, 2 * heads, rows), lambda b, ids: (b, 0, 0)),
                whole(grad_shape),
                whole(out_shape),
            ),
            scratch_shapes=[
                pltpu.VMEM((total * rows, width), F32),
                pltpu.VMEM((node_rows, cols), F32),
                pltpu.VMEM((node_rows, cols), F32),
                pltpu.SemaphoreType.DMA((len(layout),)),
                pltpu.SemaphoreType.DMA,
            ],
        ),
        compiler_params=pltpu.CompilerParams(
            dimension_semantics=("arbitrary",), vmem_limit_bytes=56 * 1024 * 1024
        ),
        name="attend_forward",
    )(ids, *arrays, out_cotangent, grad_mixed, bias, w_query, w_key, w_value, w_out)


def backward_kernel(
    steps_ref, readers_ref, feats_ref, cots_ref, stats_ref, lists_ref, own_ref, part_ref,
    wq_ref, wk_ref, wv_ref, feat_ref, gk_ref, gv_ref,
    pair_mem, key_mem, value_mem, dk_mem, dv_mem, buffer, grads, sems,
):
    rows = buffer.shape[1] // GROUP
    cols = wq_ref.shape[1]
    heads = cols // HEAD_SIZE
    lane = lax.broadcasted_iota(jnp.int32, (rows, cols), 1) // HEAD_SIZE
    count = steps_ref[2, 0]

    def load(step, into):
        for at in range(GROUP):
            to = pl.ds(at * rows, rows)
            spot = readers_ref[1, step * GROUP + at]
            start = pl.ds(pl.multiple_of(spot * rows, rows), rows)
            pltpu.make_async_copy(
                feats_ref.at[start, :], buffer.at[into, to, :], sems.at[0, into]
            ).start()
            spot = readers_ref[0, step * GROUP + at]
            start = pl.ds(pl.multiple_of(spot * rows, rows), rows)
            pltpu.make_async_copy(
                cots_ref.at[start, :], grads.at[into, to, :], sems.at[1, into]
            ).start()

    load(0, 0)
    own = split(own_ref[...])
    pair_mem[...] = mul3(own, split(wide(wk_ref[...], wv_ref[...])))
    dk_mem[...] = jnp.zeros_like(dk_mem)
    dv_mem[...] = jnp.zeros_like(dv_mem)
    w_query = split(wq_ref[...])
    mark_row = lax.broadcasted_iota(jnp.int32, (8, GROUP * rows), 0)
    mark_col = lax.broadcasted_iota(jnp.int32, (8, GROUP * rows), 1)
    marks = (mark_row == mark_col // rows).astype(BF16)

    def chunk(step, carry):
        turn = step % 2
        kind = steps_ref[1, step]
        block = pl.ds(pl.multiple_of(steps_ref[0, step] * rows, rows), rows)

        @pl.when(step + 1 < count)
        def _():
            load(step + 1, 1 - turn)

        @pl.when(kind % 2 == 1)
        def _():
            pairs = pair_mem[block, :]
            for memory, value in ((key_mem, pairs[:, :cols]), (value_mem, pairs[:, cols:])):
                for at, left in enumerate(pair_left(value)):
                    memory[at] = left

        pltpu.make_async_copy(buffer.at[turn], buffer.at[turn], sems.at[0, turn]).wait()
        pltpu.make_async_copy(grads.at[turn], grads.at[turn], sems.at[1, turn]).wait()
        query = mul3(split(buffer[turn]), w_query) * SCALE
        grad = grads[turn]
        q_high, q_low = split(query)
        g_high, g_low = split(grad)
        q_both, g_both = wide(q_high, q_low), wide(g_high, g_low)
        turned_high, turned_low = split(jnp.transpose(wide(query, grad)))
        masks, stats = [], []
        for at in range(GROUP):
            entry = readers_ref[2, step * GROUP + at]
            row = lists_ref[readers_ref[3, step * GROUP + at], pl.ds(jnp.maximum(entry, 0), 1), :]
            kept = ((row > 0) | (entry == 0)) & (entry >= 0)
            masks.append(jnp.where(kept, 0.0, MASKED))
            stats.append(stats_ref[readers_ref[0, step * GROUP + at]])
        masks.append(jnp.zeros((8 - GROUP, rows), F32))
        bias = mul(jnp.concatenate(masks, axis=0).astype(BF16), marks, 0, 0)
        stat = jnp.concatenate(stats, axis=1)
        each = range(key_mem.shape[0])
        scores = pair_products(
            [key_mem[at] for at in each], turned_high[:cols], turned_low[:cols]
        )
        grad_probs = pair_products(
            [value_mem[at] for at in each], turned_high[cols:], turned_low[cols:]
        )

        def rows_of(first):
            return [
                jnp.broadcast_to(stat[first + head:first + head + 1], bias.shape)
                for head in range(heads)
            ]

        shift = jnp.concatenate([bias - each for each in rows_of(0)], axis=0)
        probs = jnp.exp(scores + shift)
        grad_scores = probs * (grad_probs - jnp.concatenate(rows_of(heads), axis=0))
        p_high, p_low = split(probs)
        grad_value = fold(mul(p_high, g_both)) + mul(p_low, g_high)
        s_high, s_low = split(grad_scores)
        grad_key = fold(mul(s_high, q_both)) + mul(s_low, q_high)

        def gathered(value):
            parts = [
                jnp.where(lane == head, value[head * rows:(head + 1) * rows], 0.0)
                for head in range(heads)
            ]
            return sum(parts[1:], parts[0])

        dv_mem[block, :] += gathered(grad_value)
        dk_mem[block, :] += gathered(grad_key)
        return carry

    lax.fori_loop(0, count, chunk, 0)
    grad_key, grad_value = split(dk_mem[...]), split(dv_mem[...])
    feat_ref[...] = (
        part_ref[...]
        + mul3(grad_key, split(wk_ref[...]), 1, 1)
        + mul3(grad_value, split(wv_ref[...]), 1, 1)
    )
    own = split(own_ref[...])
    gk_ref[...] = mul3(own, grad_key, 0, 0)
    gv_ref[...] = mul3(own, grad_value, 0, 0)


def attend_backward(
    steps, readers, all_feats, all_cots, all_stats, lists, own_feats, part,
    w_query, w_key, w_value, rows,
):
    node_rows, width = own_feats.shape
    cols = w_query.shape[1]
    span = min(cols, 2 * HEAD_SIZE)
    held = pl.BlockSpec(memory_space=pltpu.VMEM)
    scalars = pl.BlockSpec(memory_space=pltpu.SMEM)
    afar = pl.BlockSpec(memory_space=pl.ANY)
    grad_shape = jax.ShapeDtypeStruct((width, cols), F32)
    return pl.pallas_call(
        backward_kernel,
        out_shape=(jax.ShapeDtypeStruct((node_rows, width), F32), grad_shape, grad_shape),
        in_specs=[scalars, scalars, afar, afar] + [held] * 7,
        out_specs=(held, held, held),
        scratch_shapes=[
            pltpu.VMEM((node_rows, 2 * cols), F32),
            pltpu.VMEM((cols // span, span // HEAD_SIZE * rows, 3 * span), BF16),
            pltpu.VMEM((cols // span, span // HEAD_SIZE * rows, 3 * span), BF16),
            pltpu.VMEM((node_rows, cols), F32),
            pltpu.VMEM((node_rows, cols), F32),
            pltpu.VMEM((2, GROUP * rows, width), F32),
            pltpu.VMEM((2, GROUP * rows, cols), F32),
            pltpu.SemaphoreType.DMA((2, 2)),
        ],
        compiler_params=pltpu.CompilerParams(vmem_limit_bytes=50 * 1024 * 1024),
        name="attend_backward",
    )(
        steps, readers, all_feats, all_cots, all_stats, lists, own_feats, part,
        w_query, w_key, w_value,
    )


def plan_backward(all_ids, me, block_count, pair_limit):
    blocks, entries = all_ids.shape
    candidates = blocks * entries
    flat = all_ids.reshape(-1)
    slot = jnp.where(flat // block_count == me, flat % block_count, block_count)
    order = jnp.arange(candidates, dtype=jnp.int32)
    same = (slot[:, None] == slot[None, :]) & (order[None, :] < order[:, None])
    rank = jnp.sum(same.astype(jnp.int32), axis=1)
    block_range = jnp.arange(block_count, dtype=jnp.int32)
    tally = jnp.sum((slot[None, :] == block_range[:, None]).astype(jnp.int32), axis=1)
    chunks = (tally + GROUP - 1) // GROUP
    ends = jnp.sum(
        jnp.where(block_range[None, :] <= block_range[:, None], chunks[None, :], 0), axis=1
    )
    starts = ends - chunks
    count = (pair_limit + block_count * GROUP) // GROUP
    places = count * GROUP
    start_of = jnp.sum(
        jnp.where(slot[:, None] == block_range[None, :], starts[None, :], 0), axis=1
    )
    place = jnp.where(slot < block_count, start_of * GROUP + rank, places)
    spot = jnp.arange(places, dtype=jnp.int32)
    hit = place[None, :] == spot[:, None]
    source = jnp.sum(jnp.where(hit, order[None, :], 0), axis=1)
    filled = jnp.sum(hit.astype(jnp.int32), axis=1) > 0
    readers = source // entries
    entry = jnp.where(filled, source % entries, -1)
    step = jnp.arange(count, dtype=jnp.int32)
    block = jnp.sum((step[:, None] >= ends[None, :]).astype(jnp.int32), axis=1)
    live = block < block_count
    block = jnp.minimum(block, block_count - 1)
    first = jnp.sum((step[:, None] == starts[None, :]).astype(jnp.int32), axis=1) > 0
    last = jnp.sum((step[:, None] == ends[None, :] - 1).astype(jnp.int32), axis=1) > 0
    kind = jnp.where(
        live, first.astype(jnp.int32) + 2 * last.astype(jnp.int32) + 4, 0
    )
    return jnp.stack([block, kind, jnp.full_like(kind, ends[-1])]), readers, entry


def head_scatter(part):
    size = lax.axis_size("head")
    if size != 2:
        return lax.psum_scatter(part, "head", scatter_dimension=1, tiled=True)
    me = lax.axis_index("head")
    half = part.shape[1] // 2
    sent = lax.dynamic_slice_in_dim(part, (1 - me) * half, half, axis=1)
    kept = lax.dynamic_slice_in_dim(part, me * half, half, axis=1)
    return kept + lax.ppermute(sent, "head", [(0, 1), (1, 0)])


def dom_sum(first, second):
    size = lax.axis_size("dom")
    odd = lax.axis_index("dom") % 2 == 1

    def from_across(value, bit):
        return lax.ppermute(value, "dom", [(at, at ^ bit) for at in range(size)])

    mine = jnp.where(odd, second, first) + from_across(jnp.where(odd, first, second), 1)
    bit = 2
    while bit < size:
        mine = mine + from_across(mine, bit)
        bit *= 2
    other = from_across(mine, 1)
    return jnp.where(odd, other, mine), jnp.where(odd, mine, other)


def double(value, bit):
    size, me = lax.axis_size("dom"), lax.axis_index("dom")
    other = lax.ppermute(value, "dom", [(at, at ^ bit) for at in range(size)])
    upper = me & bit != 0
    low, high = jnp.where(upper, other, value), jnp.where(upper, value, other)
    return jnp.concatenate([low, high], axis=0)


def gather_feats(part, lists, block_count, make_plan):
    size, me = lax.axis_size("dom"), lax.axis_index("dom")
    if size != 16 or lax.axis_size("head") != 2 or block_count != 8:
        plan = make_plan(lax.all_gather(lists, "dom", axis=0, tiled=True), lambda ids: ids)
        everything = lax.all_gather(part, "dom", axis=0, tiled=True)
        return [(everything, 0, everything.shape[0], 0)], lambda ids: ids, part, plan
    side = lax.axis_index("head")
    lacked = block_count - RING
    rows = part.shape[0] // block_count
    total = size * block_count

    ring = [0, 2, 4, 6, 7, 5, 3, 1]
    onward, back = [], []
    for at in range(8):
        for core in range(2):
            here, there = 2 * ring[at] + core, 2 * ring[(at + 1) % 8] + core
            onward.append((here, there))
            back.append((there, here))
    across = [(at, at ^ 1) for at in range(size)]
    other_head = [(0, 1), (1, 0)]

    def lacking(value):
        parts = [
            lax.dynamic_slice_in_dim(each, (RING - lacked) * side * rows, lacked * rows, axis=0)
            for each in value
        ]
        return jnp.concatenate(parts, axis=0)

    half = total // 2

    def swap(value):
        return lax.ppermute(value, "dom", across)

    def chip_place(chip):
        level, column = chip // 2, chip % 2
        return jnp.where(column == 0, level, 7 - level)

    def place(ids):
        owner, block = ids // block_count, ids % block_count
        gap = (chip_place(owner // 2) - chip_place(me // 2)) % 8
        slot = jnp.where(gap < 4, 2 * gap, 2 * (8 - gap) - 1)
        moved = jnp.where(gap == 0, block, (block + RING * side) % block_count)
        spot = slot * block_count + moved
        return spot + jnp.where(owner % 2 == me % 2, 0, half)

    notes = lists.reshape(-1, lists.shape[2])
    below = notes.shape[0] // 2
    notes = jnp.concatenate([notes[:below], notes[below:]], axis=1)

    start = lax.dynamic_slice_in_dim(part, lacked * side * rows, RING * rows, axis=0)
    start = jnp.concatenate([start, notes], axis=0)
    held = (lax.ppermute(start, "dom", onward), lax.ppermute(start, "dom", back))
    twin = swap(part)
    all_notes = [notes, swap(notes)]
    held, twin = lax.optimization_barrier((held, twin))
    pieces = [(part, 0, block_count * rows, 0), (twin, 0, block_count * rows, half)]

    def keep(value, swapped, slots):
        for at, slot in enumerate(slots):
            first = slot * block_count + RING
            pieces.append((value, lacked * at * rows, lacked * rows, first))
            pieces.append((swapped, lacked * at * rows, lacked * rows, half + first))

    def keep_ring(values, swapped, slots):
        for at, slot in enumerate(slots):
            first = slot * block_count
            pieces.append((values[at], 0, RING * rows, first))
            pieces.append((swapped[at], 0, RING * rows, half + first))
            all_notes.extend([values[at][RING * rows:], swapped[at][RING * rows:]])

    slots, lack, lack_slots, notes = (1, 2), (), (), ()
    for step in range(1, 5):
        if step < 3:
            coming = (
                lax.ppermute(held[0], "dom", onward), lax.ppermute(held[1], "dom", back)
            )
        elif step == 3:
            coming = (
                lax.ppermute(held[0][: RING // 2 * rows], "dom", onward),
                lax.ppermute(held[1][RING // 2 * rows:], "dom", back),
            )
            notes = jnp.concatenate(all_notes, axis=0)
            all_notes = []
        else:
            coming = ()
        more = (lax.ppermute(lacking(held), "head", other_head),)
        if step == 3:
            waiting = (held, slots, lack, lack_slots)
            coming, held, more, notes = lax.optimization_barrier((coming, held, more, notes))
        else:
            swapped = tuple(swap(value) for value in held)
            swapped_lack = tuple(swap(value) for value in lack)
            if step < 3:
                coming, held, more, swapped, lack, swapped_lack = lax.optimization_barrier(
                    (coming, held, more, swapped, lack, swapped_lack)
                )
            else:
                old, old_slots, old_lack, old_lack_slots = waiting
                old_swapped = tuple(swap(value) for value in old)
                old_swapped_lack = tuple(swap(value) for value in old_lack)
                held, swapped, lack, swapped_lack, old_swapped, old_swapped_lack = (
                    lax.optimization_barrier(
                        (held, swapped, lack, swapped_lack, old_swapped, old_swapped_lack)
                    )
                )
                keep_ring(old, old_swapped, old_slots)
                keep(old_lack[0], old_swapped_lack[0], old_lack_slots)
            keep_ring(held, swapped, slots)
            if lack:
                keep(lack[0], swapped_lack[0], lack_slots)
        lack, lack_slots = more, slots
        if step == 3:
            held, slots = (jnp.concatenate(coming, axis=0),), (7,)
            late = held[0]
        else:
            held, slots = coming, (2 * step + 1, 2 * step + 2)
    all_notes.insert(0, notes)
    every = jnp.concatenate(all_notes, axis=0)
    width = lists.shape[2]
    every = jnp.concatenate([every[:, :width], every[:, width:]], axis=0)
    plan = make_plan(every.reshape((-1,) + lists.shape[1:]), place)
    lack, plan = lax.optimization_barrier((lack, plan))
    keep(lack[0], swap(lack[0]), (7,))
    return pieces, place, late, plan


def per_device(
    node_features, w_query, w_key, w_value, w_out, nbr_part, nbr_slot, key_mask, out_cotangent
):
    dom_count = lax.axis_size("dom")
    block_count, list_len = nbr_part.shape
    node_rows, width = node_features.shape
    rows = node_rows // block_count
    me = lax.axis_index("dom")
    slot_cap = min(block_count, max(2, (block_count * list_len + dom_count - 1) // dom_count))
    self_ids = me * block_count + jnp.arange(block_count, dtype=jnp.int32)[:, None]
    ids = jnp.concatenate([self_ids, nbr_part * block_count + nbr_slot], axis=1)
    mask = jnp.concatenate([jnp.ones((block_count, 1, rows), jnp.int32), key_mask], axis=1)
    bias = jnp.where(mask > 0, 0.0, MASKED).reshape(block_count, 1, (list_len + 1) * rows)
    names = jnp.pad(ids, ((0, 0), (0, rows - list_len - 1))).astype(F32)[:, None]
    lists = jnp.concatenate([names, key_mask.astype(F32)], axis=1)

    def make_plan(lists, place):
        all_ids = lists[:, 0, : list_len + 1].astype(jnp.int32)
        steps, rows_of, entry = plan_backward(
            all_ids, me, block_count, dom_count * slot_cap
        )
        readers = all_ids[:, 0][rows_of]
        return steps, jnp.stack([readers, place(readers), entry, rows_of]), lists

    pieces, place, late, (steps, spots, lists) = gather_feats(
        node_features, lists, block_count, make_plan
    )
    grad_mixed = lax.dot_general(
        out_cotangent, w_out, (((1,), (1,)), ((), ())), precision=lax.Precision.HIGHEST
    )
    sent, late = lax.optimization_barrier((grad_mixed, late))
    all_grads = lax.all_gather(sent, "dom", axis=0, tiled=True)
    cols = w_query.shape[1]
    all_feats, out_part, feat_part, stats, grad_query, grad_out = attend_forward(
        place(ids), pieces, dom_count * block_count, out_cotangent, grad_mixed, bias, w_query, w_key, w_value, w_out
    )
    layer_out = head_scatter(out_part)
    all_stats = lax.all_gather(stats, "dom", axis=0, tiled=True)
    pieces = [grad_out[:, at:at + cols] for at in range(0, width, cols)]
    grad_query, grad_out = dom_sum(grad_query, jnp.concatenate(pieces, axis=0))
    pieces = [grad_out[at:at + cols] for at in range(0, width, cols)]
    grad_out = jnp.concatenate(pieces, axis=1)
    feats_part, grad_key, grad_value = attend_backward(
        steps, spots, all_feats, all_grads, all_stats, lists, node_features, feat_part,
        w_query, w_key, w_value, rows,
    )
    grad_features = head_scatter(feats_part)
    grad_key, grad_value = dom_sum(grad_key, grad_value)
    return (layer_out, grad_features, grad_query, grad_key, grad_value, grad_out)


def solution(mesh):
    placed = (
        P("dom", None),
        P(None, "head"),
        P(None, "head"),
        P(None, "head"),
        P("head", None),
        P("dom", None),
        P("dom", None),
        P("dom", None, None),
        P("dom", None),
    )
    return jax.shard_map(
        per_device,
        mesh=mesh,
        in_specs=placed,
        out_specs=(
            P("dom", "head"),
            P("dom", "head"),
            P(None, "head"),
            P(None, "head"),
            P(None, "head"),
            P("head", None),
        ),
        check_vma=False,
    )
```

```python
import functools

import jax
import jax.numpy as jnp
from jax import lax
from jax.experimental import pallas as pl
from jax.experimental.pallas import tpu as pltpu
from jax.sharding import PartitionSpec as P

HEAD_SIZE = 32
GROUP = 2
RING = 6
SCALE = HEAD_SIZE ** (-0.5)
MASKED = -1e30
F32 = jnp.float32
BF16 = jnp.bfloat16


def split(value):
    high = value.astype(BF16)
    return high, (value - high.astype(F32)).astype(BF16)


def mul(left, right, left_dim=1, right_dim=0):
    return lax.dot_general(
        left, right, (((left_dim,), (right_dim,)), ((), ())), preferred_element_type=F32
    )


def mul3(left, right, left_dim=1, right_dim=0):
    left_high, left_low = left
    right_high, right_low = right
    return (
        mul(left_high, right_high, left_dim, right_dim)
        + mul(left_high, right_low, left_dim, right_dim)
        + mul(left_low, right_high, left_dim, right_dim)
    )


def wide(first, second):
    return jnp.concatenate([first, second], axis=1)


def pair_left(value):
    rows, cols = value.shape
    span = min(cols, 2 * HEAD_SIZE)
    lane = lax.broadcasted_iota(jnp.int32, (rows, span), 1) // HEAD_SIZE
    result = []
    for first in range(0, cols, span):
        part = value[:, first:first + span]
        parts = [jnp.where(lane == head, part, 0.0) for head in range(span // HEAD_SIZE)]
        high, low = split(jnp.concatenate(parts, axis=0))
        result.append(jnp.concatenate([high, low, high], axis=1))
    return result


def pair_products(lefts, high, low):
    span = high.shape[0] // len(lefts)
    result = []
    for at, left in enumerate(lefts):
        here = slice(at * span, (at + 1) * span)
        right = jnp.concatenate([high[here], high[here], low[here]], axis=0)
        result.append(mul(left, right))
    return jnp.concatenate(result, axis=0)


def fold(value):
    half = value.shape[1] // 2
    return value[:, :half] + value[:, half:]


def forward_kernel(entries, layout, source_count, ids, *refs):
    sources = refs[:source_count]
    (cot_ref, grad_ref, bias_ref, wq_ref, wk_ref, wv_ref, wo_ref,
     all_ref, out_ref, feat_ref, stat_ref, gq_ref, go_ref,
     feats, mixed_mem, grad_mem, sems, all_sem) = refs[source_count:]
    rows = grad_ref.shape[0]
    step = pl.program_id(0)
    keep = pltpu.make_async_copy(feats, all_ref, all_sem)

    @pl.when(step == 0)
    def _():
        copies = []
        for at, (source, row, count, block) in enumerate(layout):
            copies.append(
                pltpu.make_async_copy(
                    sources[source].at[pl.ds(row, count), :],
                    feats.at[pl.ds(block * rows, count), :],
                    sems.at[at],
                )
            )
        for copy in copies:
            copy.start()
        for copy in copies:
            copy.wait()
        keep.start()

    listed = [
        feats[pl.ds(pl.multiple_of(ids[step, entry] * rows, rows), rows), :]
        for entry in range(entries)
    ]
    cols = wq_ref.shape[1]
    heads = cols // HEAD_SIZE
    inputs = split(jnp.concatenate(listed, axis=0))
    w_query = split(wq_ref[...])
    w_out = split(wo_ref[...])
    pairs = mul3(inputs, split(wide(wk_ref[...], wv_ref[...])))
    key_high, key_low = split(pairs[:, :cols])
    value_high, value_low = split(pairs[:, cols:])
    key_both, value_both = wide(key_high, key_low), wide(value_high, value_low)
    turned_high, turned_low = split(jnp.transpose(pairs))
    own = (inputs[0][:rows], inputs[1][:rows])
    query = mul3(own, w_query) * SCALE
    grad_mixed = grad_ref[...]
    lane = lax.broadcasted_iota(jnp.int32, (rows, cols), 1) // HEAD_SIZE
    here = [lane == head for head in range(heads)]

    def spread(value):
        return jnp.concatenate([jnp.where(mask, value, 0.0) for mask in here], axis=0)

    def gather(value):
        parts = [
            jnp.where(mask, value[head * rows:(head + 1) * rows], 0.0)
            for head, mask in enumerate(here)
        ]
        return sum(parts[1:], parts[0])

    scores = pair_products(pair_left(query), turned_high[:cols], turned_low[:cols])
    scores = scores + bias_ref[0]
    top = jnp.max(scores, axis=1, keepdims=True)
    probs = jnp.exp(scores - top)
    total = jnp.sum(probs, axis=1, keepdims=True)
    inverse = 1.0 / total
    p_high, p_low = split(probs)
    weighted = (fold(mul(p_high, value_both)) + mul(p_low, value_high)) * inverse
    mixed = gather(weighted)
    grad_part = spread(grad_mixed)
    delta = jnp.sum(grad_part * weighted, axis=1, keepdims=True)
    grad_probs = pair_products(pair_left(grad_mixed), turned_high[cols:], turned_low[cols:])
    s_high, s_low = split(probs * (grad_probs - delta))
    back = (fold(mul(s_high, key_both)) + mul(s_low, key_high)) * (inverse * SCALE)
    grad_query = gather(back)
    log_total = top + jnp.log(total)
    stat_lane = lax.broadcasted_iota(jnp.int32, (rows, rows), 1)
    stats = jnp.zeros((rows, rows), F32)
    for head in range(heads):
        at = slice(head * rows, (head + 1) * rows)
        stats = jnp.where(stat_lane == head, log_total[at], stats)
        stats = jnp.where(stat_lane == heads + head, delta[at], stats)
    block = pl.ds(pl.multiple_of(step * rows, rows), rows)
    mixed_mem[block, :] = mixed
    grad_mem[block, :] = grad_query
    stat_ref[0] = jnp.transpose(stats)[: 2 * heads]

    @pl.when(step == pl.num_programs(0) - 1)
    def _():
        mixed, grad_query = split(mixed_mem[...]), split(grad_mem[...])
        first = pl.ds(pl.multiple_of(ids[0, 0] * rows, rows), mixed_mem.shape[0])
        out_ref[...] = mul3(mixed, w_out)
        feat_ref[...] = mul3(grad_query, w_query, 1, 1)
        gq_ref[...] = mul3(split(feats[first, :]), grad_query, 0, 0)
        go_ref[...] = mul3(mixed, split(cot_ref[...]), 0, 0)
        keep.wait()


def attend_forward(ids, pieces, total, out_cotangent, grad_mixed, bias, w_query, w_key, w_value, w_out):
    block_count, entries = ids.shape
    node_rows, width = out_cotangent.shape
    rows = node_rows // block_count
    cols = w_query.shape[1]
    heads = cols // HEAD_SIZE

    arrays = []
    for array, *_ in pieces:
        if not any(array is known for known in arrays):
            arrays.append(array)
    layout = [
        ([array is known for known in arrays].index(True), *rest) for array, *rest in pieces
    ]
    all_shape = jax.ShapeDtypeStruct((total * rows, width), F32)

    def whole(array):
        return pl.BlockSpec(array.shape, lambda b, ids: (0,) * array.ndim)

    grad_shape = jax.ShapeDtypeStruct((width, cols), F32)
    out_shape = jax.ShapeDtypeStruct((cols, width), F32)
    node_shape = jax.ShapeDtypeStruct((node_rows, width), F32)
    return pl.pallas_call(
        functools.partial(forward_kernel, entries, layout, len(arrays)),
        out_shape=(
            all_shape,
            node_shape,
            node_shape,
            jax.ShapeDtypeStruct((block_count, 2 * heads, rows), F32),
            grad_shape,
            out_shape,
        ),
        grid_spec=pltpu.PrefetchScalarGridSpec(
            num_scalar_prefetch=1,
            grid=(block_count,),
            in_specs=[pl.BlockSpec(memory_space=pl.ANY) for _ in arrays]
            + [whole(out_cotangent), pl.BlockSpec((rows, cols), lambda b, ids: (b, 0))]
            + [pl.BlockSpec((1, 1, entries * rows), lambda b, ids: (b, 0, 0))]
            + [whole(w) for w in (w_query, w_key, w_value, w_out)],
            out_specs=(
                pl.BlockSpec(memory_space=pl.ANY),
                whole(node_shape),
                whole(node_shape),
                pl.BlockSpec((1, 2 * heads, rows), lambda b, ids: (b, 0, 0)),
                whole(grad_shape),
                whole(out_shape),
            ),
            scratch_shapes=[
                pltpu.VMEM((total * rows, width), F32),
                pltpu.VMEM((node_rows, cols), F32),
                pltpu.VMEM((node_rows, cols), F32),
                pltpu.SemaphoreType.DMA((len(layout),)),
                pltpu.SemaphoreType.DMA,
            ],
        ),
        compiler_params=pltpu.CompilerParams(
            dimension_semantics=("arbitrary",), vmem_limit_bytes=56 * 1024 * 1024
        ),
        name="attend_forward",
    )(ids, *arrays, out_cotangent, grad_mixed, bias, w_query, w_key, w_value, w_out)


def backward_kernel(
    steps_ref, readers_ref, feats_ref, cots_ref, stats_ref, lists_ref, own_ref, part_ref,
    wq_ref, wk_ref, wv_ref, feat_ref, gk_ref, gv_ref,
    pair_mem, key_mem, value_mem, dk_mem, dv_mem, buffer, grads, sems,
):
    rows = buffer.shape[1] // GROUP
    cols = wq_ref.shape[1]
    heads = cols // HEAD_SIZE
    lane = lax.broadcasted_iota(jnp.int32, (rows, cols), 1) // HEAD_SIZE
    count = steps_ref[2, 0]

    def load(step, into):
        for at in range(GROUP):
            to = pl.ds(at * rows, rows)
            spot = readers_ref[1, step * GROUP + at]
            start = pl.ds(pl.multiple_of(spot * rows, rows), rows)
            pltpu.make_async_copy(
                feats_ref.at[start, :], buffer.at[into, to, :], sems.at[0, into]
            ).start()
            spot = readers_ref[0, step * GROUP + at]
            start = pl.ds(pl.multiple_of(spot * rows, rows), rows)
            pltpu.make_async_copy(
                cots_ref.at[start, :], grads.at[into, to, :], sems.at[1, into]
            ).start()

    load(0, 0)
    own = split(own_ref[...])
    pair_mem[...] = mul3(own, split(wide(wk_ref[...], wv_ref[...])))
    dk_mem[...] = jnp.zeros_like(dk_mem)
    dv_mem[...] = jnp.zeros_like(dv_mem)
    w_query = split(wq_ref[...])
    mark_row = lax.broadcasted_iota(jnp.int32, (8, GROUP * rows), 0)
    mark_col = lax.broadcasted_iota(jnp.int32, (8, GROUP * rows), 1)
    marks = (mark_row == mark_col // rows).astype(BF16)

    def chunk(step, carry):
        turn = step % 2
        kind = steps_ref[1, step]
        block = pl.ds(pl.multiple_of(steps_ref[0, step] * rows, rows), rows)

        @pl.when(step + 1 < count)
        def _():
            load(step + 1, 1 - turn)

        @pl.when(kind % 2 == 1)
        def _():
            pairs = pair_mem[block, :]
            for memory, value in ((key_mem, pairs[:, :cols]), (value_mem, pairs[:, cols:])):
                for at, left in enumerate(pair_left(value)):
                    memory[at] = left

        pltpu.make_async_copy(buffer.at[turn], buffer.at[turn], sems.at[0, turn]).wait()
        pltpu.make_async_copy(grads.at[turn], grads.at[turn], sems.at[1, turn]).wait()
        query = mul3(split(buffer[turn]), w_query) * SCALE
        grad = grads[turn]
        q_high, q_low = split(query)
        g_high, g_low = split(grad)
        q_both, g_both = wide(q_high, q_low), wide(g_high, g_low)
        turned_high, turned_low = split(jnp.transpose(wide(query, grad)))
        masks, stats = [], []
        for at in range(GROUP):
            entry = readers_ref[2, step * GROUP + at]
            row = lists_ref[readers_ref[3, step * GROUP + at], pl.ds(jnp.maximum(entry, 0), 1), :]
            kept = ((row > 0) | (entry == 0)) & (entry >= 0)
            masks.append(jnp.where(kept, 0.0, MASKED))
            stats.append(stats_ref[readers_ref[4, step * GROUP + at]])
        masks.append(jnp.zeros((8 - GROUP, rows), F32))
        bias = mul(jnp.concatenate(masks, axis=0).astype(BF16), marks, 0, 0)
        stat = jnp.concatenate(stats, axis=1)
        each = range(key_mem.shape[0])
        scores = pair_products(
            [key_mem[at] for at in each], turned_high[:cols], turned_low[:cols]
        )
        grad_probs = pair_products(
            [value_mem[at] for at in each], turned_high[cols:], turned_low[cols:]
        )

        def rows_of(first):
            return [
                jnp.broadcast_to(stat[first + head:first + head + 1], bias.shape)
                for head in range(heads)
            ]

        shift = jnp.concatenate([bias - each for each in rows_of(0)], axis=0)
        probs = jnp.exp(scores + shift)
        grad_scores = probs * (grad_probs - jnp.concatenate(rows_of(heads), axis=0))
        p_high, p_low = split(probs)
        grad_value = fold(mul(p_high, g_both)) + mul(p_low, g_high)
        s_high, s_low = split(grad_scores)
        grad_key = fold(mul(s_high, q_both)) + mul(s_low, q_high)

        def gathered(value):
            parts = [
                jnp.where(lane == head, value[head * rows:(head + 1) * rows], 0.0)
                for head in range(heads)
            ]
            return sum(parts[1:], parts[0])

        dv_mem[block, :] += gathered(grad_value)
        dk_mem[block, :] += gathered(grad_key)
        return carry

    lax.fori_loop(0, count, chunk, 0)
    grad_key, grad_value = split(dk_mem[...]), split(dv_mem[...])
    feat_ref[...] = (
        part_ref[...]
        + mul3(grad_key, split(wk_ref[...]), 1, 1)
        + mul3(grad_value, split(wv_ref[...]), 1, 1)
    )
    own = split(own_ref[...])
    gk_ref[...] = mul3(own, grad_key, 0, 0)
    gv_ref[...] = mul3(own, grad_value, 0, 0)


def attend_backward(
    steps, readers, all_feats, all_cots, all_stats, lists, own_feats, part,
    w_query, w_key, w_value, rows,
):
    node_rows, width = own_feats.shape
    cols = w_query.shape[1]
    span = min(cols, 2 * HEAD_SIZE)
    held = pl.BlockSpec(memory_space=pltpu.VMEM)
    scalars = pl.BlockSpec(memory_space=pltpu.SMEM)
    afar = pl.BlockSpec(memory_space=pl.ANY)
    grad_shape = jax.ShapeDtypeStruct((width, cols), F32)
    return pl.pallas_call(
        backward_kernel,
        out_shape=(jax.ShapeDtypeStruct((node_rows, width), F32), grad_shape, grad_shape),
        in_specs=[scalars, scalars, afar, afar] + [held] * 7,
        out_specs=(held, held, held),
        scratch_shapes=[
            pltpu.VMEM((node_rows, 2 * cols), F32),
            pltpu.VMEM((cols // span, span // HEAD_SIZE * rows, 3 * span), BF16),
            pltpu.VMEM((cols // span, span // HEAD_SIZE * rows, 3 * span), BF16),
            pltpu.VMEM((node_rows, cols), F32),
            pltpu.VMEM((node_rows, cols), F32),
            pltpu.VMEM((2, GROUP * rows, width), F32),
            pltpu.VMEM((2, GROUP * rows, cols), F32),
            pltpu.SemaphoreType.DMA((2, 2)),
        ],
        compiler_params=pltpu.CompilerParams(vmem_limit_bytes=50 * 1024 * 1024),
        name="attend_backward",
    )(
        steps, readers, all_feats, all_cots, all_stats, lists, own_feats, part,
        w_query, w_key, w_value,
    )


def plan_backward(all_ids, me, block_count, pair_limit):
    blocks, entries = all_ids.shape
    candidates = blocks * entries
    flat = all_ids.reshape(-1)
    slot = jnp.where(flat // block_count == me, flat % block_count, block_count)
    order = jnp.arange(candidates, dtype=jnp.int32)
    same = (slot[:, None] == slot[None, :]) & (order[None, :] < order[:, None])
    rank = jnp.sum(same.astype(jnp.int32), axis=1)
    block_range = jnp.arange(block_count, dtype=jnp.int32)
    tally = jnp.sum((slot[None, :] == block_range[:, None]).astype(jnp.int32), axis=1)
    chunks = (tally + GROUP - 1) // GROUP
    ends = jnp.sum(
        jnp.where(block_range[None, :] <= block_range[:, None], chunks[None, :], 0), axis=1
    )
    starts = ends - chunks
    count = (pair_limit + block_count * GROUP) // GROUP
    places = count * GROUP
    start_of = jnp.sum(
        jnp.where(slot[:, None] == block_range[None, :], starts[None, :], 0), axis=1
    )
    place = jnp.where(slot < block_count, start_of * GROUP + rank, places)
    spot = jnp.arange(places, dtype=jnp.int32)
    hit = place[None, :] == spot[:, None]
    source = jnp.sum(jnp.where(hit, order[None, :], 0), axis=1)
    filled = jnp.sum(hit.astype(jnp.int32), axis=1) > 0
    readers = source // entries
    entry = jnp.where(filled, source % entries, -1)
    step = jnp.arange(count, dtype=jnp.int32)
    block = jnp.sum((step[:, None] >= ends[None, :]).astype(jnp.int32), axis=1)
    live = block < block_count
    block = jnp.minimum(block, block_count - 1)
    first = jnp.sum((step[:, None] == starts[None, :]).astype(jnp.int32), axis=1) > 0
    last = jnp.sum((step[:, None] == ends[None, :] - 1).astype(jnp.int32), axis=1) > 0
    kind = jnp.where(
        live, first.astype(jnp.int32) + 2 * last.astype(jnp.int32) + 4, 0
    )
    return jnp.stack([block, kind, jnp.full_like(kind, ends[-1])]), readers, entry


def head_scatter(part):
    size = lax.axis_size("head")
    if size != 2:
        return lax.psum_scatter(part, "head", scatter_dimension=1, tiled=True)
    me = lax.axis_index("head")
    half = part.shape[1] // 2
    sent = lax.dynamic_slice_in_dim(part, (1 - me) * half, half, axis=1)
    kept = lax.dynamic_slice_in_dim(part, me * half, half, axis=1)
    return kept + lax.ppermute(sent, "head", [(0, 1), (1, 0)])


def dom_sum(first, second):
    size = lax.axis_size("dom")
    odd = lax.axis_index("dom") % 2 == 1

    def from_across(value, bit):
        return lax.ppermute(value, "dom", [(at, at ^ bit) for at in range(size)])

    mine = jnp.where(odd, second, first) + from_across(jnp.where(odd, first, second), 1)
    bit = 2
    while bit < size:
        mine = mine + from_across(mine, bit)
        bit *= 2
    other = from_across(mine, 1)
    return jnp.where(odd, other, mine), jnp.where(odd, mine, other)


def double(value, bit):
    size, me = lax.axis_size("dom"), lax.axis_index("dom")
    other = lax.ppermute(value, "dom", [(at, at ^ bit) for at in range(size)])
    upper = me & bit != 0
    low, high = jnp.where(upper, other, value), jnp.where(upper, value, other)
    return jnp.concatenate([low, high], axis=0)


def doubled_place(device, size):
    place, bit = jnp.zeros_like(device), 1
    while bit < size:
        place = 2 * place + device // bit % 2
        bit *= 2
    return place


def gather_feats(part, lists, block_count, make_plan, early):
    size, me = lax.axis_size("dom"), lax.axis_index("dom")
    if size != 16 or lax.axis_size("head") != 2 or block_count != 8:
        plan = make_plan(lax.all_gather(lists, "dom", axis=0, tiled=True), lambda ids: ids)
        everything = lax.all_gather(part, "dom", axis=0, tiled=True)
        return [(everything, 0, everything.shape[0], 0)], lambda ids: ids, part, plan, early
    side = lax.axis_index("head")
    lacked = block_count - RING
    rows = part.shape[0] // block_count
    total = size * block_count

    ring = [0, 2, 4, 6, 7, 5, 3, 1]
    onward, back = [], []
    for at in range(8):
        for core in range(2):
            here, there = 2 * ring[at] + core, 2 * ring[(at + 1) % 8] + core
            onward.append((here, there))
            back.append((there, here))
    across = [(at, at ^ 1) for at in range(size)]
    other_head = [(0, 1), (1, 0)]

    def lacking(value):
        parts = [
            lax.dynamic_slice_in_dim(each, (RING - lacked) * side * rows, lacked * rows, axis=0)
            for each in value
        ]
        return jnp.concatenate(parts, axis=0)

    half = total // 2

    def swap(value):
        return lax.ppermute(value, "dom", across)

    def chip_place(chip):
        level, column = chip // 2, chip % 2
        return jnp.where(column == 0, level, 7 - level)

    def place(ids):
        owner, block = ids // block_count, ids % block_count
        gap = (chip_place(owner // 2) - chip_place(me // 2)) % 8
        slot = jnp.where(gap < 4, 2 * gap, 2 * (8 - gap) - 1)
        moved = jnp.where(gap == 0, block, (block + RING * side) % block_count)
        spot = slot * block_count + moved
        return spot + jnp.where(owner % 2 == me % 2, 0, half)

    notes = lists.reshape(-1, lists.shape[2])
    below = notes.shape[0] // 2
    notes = jnp.concatenate([notes[:below], notes[below:]], axis=1)

    start = lax.dynamic_slice_in_dim(part, lacked * side * rows, RING * rows, axis=0)
    start = jnp.concatenate([start, notes], axis=0)
    held = (lax.ppermute(start, "dom", onward), lax.ppermute(start, "dom", back))
    twin = swap(part)
    all_notes = [notes, swap(notes)]
    held, twin, early = lax.optimization_barrier((held, twin, early))
    pieces = [(part, 0, block_count * rows, 0), (twin, 0, block_count * rows, half)]

    def keep(value, swapped, slots):
        for at, slot in enumerate(slots):
            first = slot * block_count + RING
            pieces.append((value, lacked * at * rows, lacked * rows, first))
            pieces.append((swapped, lacked * at * rows, lacked * rows, half + first))

    def keep_ring(values, swapped, slots):
        for at, slot in enumerate(slots):
            first = slot * block_count
            pieces.append((values[at], 0, RING * rows, first))
            pieces.append((swapped[at], 0, RING * rows, half + first))
            all_notes.extend([values[at][RING * rows:], swapped[at][RING * rows:]])

    slots, lack, lack_slots, notes = (1, 2), (), (), ()
    for step in range(1, 5):
        if step < 3:
            coming = (
                lax.ppermute(held[0], "dom", onward), lax.ppermute(held[1], "dom", back)
            )
        elif step == 3:
            coming = (
                lax.ppermute(held[0][: RING // 2 * rows], "dom", onward),
                lax.ppermute(held[1][RING // 2 * rows:], "dom", back),
            )
            notes = jnp.concatenate(all_notes, axis=0)
            all_notes = []
        else:
            coming = ()
        more = (lax.ppermute(lacking(held), "head", other_head),)
        if step == 3:
            waiting = (held, slots, lack, lack_slots)
            coming, held, more, notes = lax.optimization_barrier((coming, held, more, notes))
        else:
            swapped = tuple(swap(value) for value in held)
            swapped_lack = tuple(swap(value) for value in lack)
            if step < 3:
                coming, held, more, swapped, lack, swapped_lack = lax.optimization_barrier(
                    (coming, held, more, swapped, lack, swapped_lack)
                )
            else:
                old, old_slots, old_lack, old_lack_slots = waiting
                old_swapped = tuple(swap(value) for value in old)
                old_swapped_lack = tuple(swap(value) for value in old_lack)
                held, swapped, lack, swapped_lack, old_swapped, old_swapped_lack = (
                    lax.optimization_barrier(
                        (held, swapped, lack, swapped_lack, old_swapped, old_swapped_lack)
                    )
                )
                keep_ring(old, old_swapped, old_slots)
                keep(old_lack[0], old_swapped_lack[0], old_lack_slots)
            keep_ring(held, swapped, slots)
            if lack:
                keep(lack[0], swapped_lack[0], lack_slots)
        lack, lack_slots = more, slots
        if step == 3:
            held, slots = (jnp.concatenate(coming, axis=0),), (7,)
            late = held[0]
        else:
            held, slots = coming, (2 * step + 1, 2 * step + 2)
    all_notes.insert(0, notes)
    every = jnp.concatenate(all_notes, axis=0)
    width = lists.shape[2]
    every = jnp.concatenate([every[:, :width], every[:, width:]], axis=0)
    plan = make_plan(every.reshape((-1,) + lists.shape[1:]), place)
    lack, plan = lax.optimization_barrier((lack, plan))
    keep(lack[0], swap(lack[0]), (7,))
    return pieces, place, late, plan, early


def per_device(
    node_features, w_query, w_key, w_value, w_out, nbr_part, nbr_slot, key_mask, out_cotangent
):
    dom_count = lax.axis_size("dom")
    block_count, list_len = nbr_part.shape
    node_rows, width = node_features.shape
    rows = node_rows // block_count
    me = lax.axis_index("dom")
    slot_cap = min(block_count, max(2, (block_count * list_len + dom_count - 1) // dom_count))
    self_ids = me * block_count + jnp.arange(block_count, dtype=jnp.int32)[:, None]
    ids = jnp.concatenate([self_ids, nbr_part * block_count + nbr_slot], axis=1)
    mask = jnp.concatenate([jnp.ones((block_count, 1, rows), jnp.int32), key_mask], axis=1)
    bias = jnp.where(mask > 0, 0.0, MASKED).reshape(block_count, 1, (list_len + 1) * rows)
    names = jnp.pad(ids, ((0, 0), (0, rows - list_len - 1))).astype(F32)[:, None]
    lists = jnp.concatenate([names, key_mask.astype(F32)], axis=1)

    def make_plan(lists, place):
        all_ids = lists[:, 0, : list_len + 1].astype(jnp.int32)
        steps, rows_of, entry = plan_backward(
            all_ids, me, block_count, dom_count * slot_cap
        )
        readers = all_ids[:, 0][rows_of]
        stat_of = doubled_place(readers // block_count, dom_count) * block_count
        stat_of = stat_of + readers % block_count
        return steps, jnp.stack([readers, place(readers), entry, rows_of, stat_of]), lists

    grad_mixed = lax.dot_general(
        out_cotangent, w_out, (((1,), (1,)), ((), ())), precision=lax.Precision.HIGHEST
    )
    pieces, place, late, (steps, spots, lists), grad_mixed = gather_feats(
        node_features, lists, block_count, make_plan, grad_mixed
    )
    sent, late = lax.optimization_barrier((grad_mixed, late))
    all_grads = lax.all_gather(sent, "dom", axis=0, tiled=True)
    cols = w_query.shape[1]
    all_feats, out_part, feat_part, stats, grad_query, grad_out = attend_forward(
        place(ids), pieces, dom_count * block_count, out_cotangent, grad_mixed, bias, w_query, w_key, w_value, w_out
    )
    layer_out = head_scatter(out_part)
    all_stats = stats
    bit = dom_count // 2
    while bit:
        all_stats = double(all_stats, bit)
        bit //= 2
    pieces = [grad_out[:, at:at + cols] for at in range(0, width, cols)]
    grad_query, grad_out = dom_sum(grad_query, jnp.concatenate(pieces, axis=0))
    pieces = [grad_out[at:at + cols] for at in range(0, width, cols)]
    grad_out = jnp.concatenate(pieces, axis=1)
    feats_part, grad_key, grad_value = attend_backward(
        steps, spots, all_feats, all_grads, all_stats, lists, node_features, feat_part,
        w_query, w_key, w_value, rows,
    )
    grad_features = head_scatter(feats_part)
    grad_key, grad_value = dom_sum(grad_key, grad_value)
    return (layer_out, grad_features, grad_query, grad_key, grad_value, grad_out)


def solution(mesh):
    placed = (
        P("dom", None),
        P(None, "head"),
        P(None, "head"),
        P(None, "head"),
        P("head", None),
        P("dom", None),
        P("dom", None),
        P("dom", None, None),
        P("dom", None),
    )
    return jax.shard_map(
        per_device,
        mesh=mesh,
        in_specs=placed,
        out_specs=(
            P("dom", "head"),
            P("dom", "head"),
            P(None, "head"),
            P(None, "head"),
            P(None, "head"),
            P("head", None),
        ),
        check_vma=False,
    )
```

```python
import functools

import jax
import jax.numpy as jnp
from jax import lax
from jax.experimental import pallas as pl
from jax.experimental.pallas import tpu as pltpu
from jax.sharding import PartitionSpec as P

HEAD_SIZE = 32
GROUP = 2
RING = 6
SCALE = HEAD_SIZE ** (-0.5)
MASKED = -1e30
F32 = jnp.float32
BF16 = jnp.bfloat16


def split(value):
    high = value.astype(BF16)
    return high, (value - high.astype(F32)).astype(BF16)


def mul(left, right, left_dim=1, right_dim=0):
    return lax.dot_general(
        left, right, (((left_dim,), (right_dim,)), ((), ())), preferred_element_type=F32
    )


def mul3(left, right, left_dim=1, right_dim=0):
    left_high, left_low = left
    right_high, right_low = right
    return (
        mul(left_high, right_high, left_dim, right_dim)
        + mul(left_high, right_low, left_dim, right_dim)
        + mul(left_low, right_high, left_dim, right_dim)
    )


def wide(first, second):
    return jnp.concatenate([first, second], axis=1)


def pair_left(value):
    rows, cols = value.shape
    span = min(cols, 2 * HEAD_SIZE)
    lane = lax.broadcasted_iota(jnp.int32, (rows, span), 1) // HEAD_SIZE
    result = []
    for first in range(0, cols, span):
        part = value[:, first:first + span]
        parts = [jnp.where(lane == head, part, 0.0) for head in range(span // HEAD_SIZE)]
        high, low = split(jnp.concatenate(parts, axis=0))
        result.append(jnp.concatenate([high, low, high], axis=1))
    return result


def pair_products(lefts, high, low):
    span = high.shape[0] // len(lefts)
    result = []
    for at, left in enumerate(lefts):
        here = slice(at * span, (at + 1) * span)
        right = jnp.concatenate([high[here], high[here], low[here]], axis=0)
        result.append(mul(left, right))
    return jnp.concatenate(result, axis=0)


def fold(value):
    half = value.shape[1] // 2
    return value[:, :half] + value[:, half:]


def forward_kernel(entries, layout, source_count, ids, *refs):
    sources = refs[:source_count]
    (cot_ref, grad_ref, bias_ref, wq_ref, wk_ref, wv_ref, wo_ref,
     all_ref, out_ref, feat_ref, stat_ref, gq_ref, go_ref,
     feats, mixed_mem, grad_mem, sems, all_sem) = refs[source_count:]
    rows = grad_ref.shape[0]
    step = pl.program_id(0)
    keep = pltpu.make_async_copy(feats, all_ref, all_sem)

    @pl.when(step == 0)
    def _():
        copies = []
        for at, (source, row, count, block) in enumerate(layout):
            copies.append(
                pltpu.make_async_copy(
                    sources[source].at[pl.ds(row, count), :],
                    feats.at[pl.ds(block * rows, count), :],
                    sems.at[at],
                )
            )
        for copy in copies:
            copy.start()
        for copy in copies:
            copy.wait()
        keep.start()

    listed = [
        feats[pl.ds(pl.multiple_of(ids[step, entry] * rows, rows), rows), :]
        for entry in range(entries)
    ]
    cols = wq_ref.shape[1]
    heads = cols // HEAD_SIZE
    inputs = split(jnp.concatenate(listed, axis=0))
    w_query = split(wq_ref[...])
    w_out = split(wo_ref[...])
    pairs = mul3(inputs, split(wide(wk_ref[...], wv_ref[...])))
    key_high, key_low = split(pairs[:, :cols])
    value_high, value_low = split(pairs[:, cols:])
    key_both, value_both = wide(key_high, key_low), wide(value_high, value_low)
    turned_high, turned_low = split(jnp.transpose(pairs))
    own = (inputs[0][:rows], inputs[1][:rows])
    query = mul3(own, w_query) * SCALE
    grad_mixed = grad_ref[...]
    lane = lax.broadcasted_iota(jnp.int32, (rows, cols), 1) // HEAD_SIZE
    here = [lane == head for head in range(heads)]

    def spread(value):
        return jnp.concatenate([jnp.where(mask, value, 0.0) for mask in here], axis=0)

    def gather(value):
        parts = [
            jnp.where(mask, value[head * rows:(head + 1) * rows], 0.0)
            for head, mask in enumerate(here)
        ]
        return sum(parts[1:], parts[0])

    scores = pair_products(pair_left(query), turned_high[:cols], turned_low[:cols])
    scores = scores + bias_ref[0]
    top = jnp.max(scores, axis=1, keepdims=True)
    probs = jnp.exp(scores - top)
    total = jnp.sum(probs, axis=1, keepdims=True)
    inverse = 1.0 / total
    p_high, p_low = split(probs)
    weighted = (fold(mul(p_high, value_both)) + mul(p_low, value_high)) * inverse
    mixed = gather(weighted)
    grad_part = spread(grad_mixed)
    delta = jnp.sum(grad_part * weighted, axis=1, keepdims=True)
    grad_probs = pair_products(pair_left(grad_mixed), turned_high[cols:], turned_low[cols:])
    s_high, s_low = split(probs * (grad_probs - delta))
    back = (fold(mul(s_high, key_both)) + mul(s_low, key_high)) * (inverse * SCALE)
    grad_query = gather(back)
    log_total = top + jnp.log(total)
    stat_lane = lax.broadcasted_iota(jnp.int32, (rows, rows), 1)
    stats = jnp.zeros((rows, rows), F32)
    for head in range(heads):
        at = slice(head * rows, (head + 1) * rows)
        stats = jnp.where(stat_lane == head, log_total[at], stats)
        stats = jnp.where(stat_lane == heads + head, delta[at], stats)
    block = pl.ds(pl.multiple_of(step * rows, rows), rows)
    mixed_mem[block, :] = mixed
    grad_mem[block, :] = grad_query
    stat_ref[0] = jnp.transpose(stats)[: 2 * heads]

    @pl.when(step == pl.num_programs(0) - 1)
    def _():
        mixed, grad_query = split(mixed_mem[...]), split(grad_mem[...])
        first = pl.ds(pl.multiple_of(ids[0, 0] * rows, rows), mixed_mem.shape[0])
        out_ref[...] = mul3(mixed, w_out)
        feat_ref[...] = mul3(grad_query, w_query, 1, 1)
        gq_ref[...] = mul3(split(feats[first, :]), grad_query, 0, 0)
        go_ref[...] = mul3(mixed, split(cot_ref[...]), 0, 0)
        keep.wait()


def attend_forward(ids, pieces, total, out_cotangent, grad_mixed, bias, w_query, w_key, w_value, w_out):
    block_count, entries = ids.shape
    node_rows, width = out_cotangent.shape
    rows = node_rows // block_count
    cols = w_query.shape[1]
    heads = cols // HEAD_SIZE

    arrays = []
    for array, *_ in pieces:
        if not any(array is known for known in arrays):
            arrays.append(array)
    layout = [
        ([array is known for known in arrays].index(True), *rest) for array, *rest in pieces
    ]
    all_shape = jax.ShapeDtypeStruct((total * rows, width), F32)

    def whole(array):
        return pl.BlockSpec(array.shape, lambda b, ids: (0,) * array.ndim)

    grad_shape = jax.ShapeDtypeStruct((width, cols), F32)
    out_shape = jax.ShapeDtypeStruct((cols, width), F32)
    node_shape = jax.ShapeDtypeStruct((node_rows, width), F32)
    return pl.pallas_call(
        functools.partial(forward_kernel, entries, layout, len(arrays)),
        out_shape=(
            all_shape,
            node_shape,
            node_shape,
            jax.ShapeDtypeStruct((block_count, 2 * heads, rows), F32),
            grad_shape,
            out_shape,
        ),
        grid_spec=pltpu.PrefetchScalarGridSpec(
            num_scalar_prefetch=1,
            grid=(block_count,),
            in_specs=[pl.BlockSpec(memory_space=pl.ANY) for _ in arrays]
            + [whole(out_cotangent), pl.BlockSpec((rows, cols), lambda b, ids: (b, 0))]
            + [pl.BlockSpec((1, 1, entries * rows), lambda b, ids: (b, 0, 0))]
            + [whole(w) for w in (w_query, w_key, w_value, w_out)],
            out_specs=(
                pl.BlockSpec(memory_space=pl.ANY),
                whole(node_shape),
                whole(node_shape),
                pl.BlockSpec((1, 2 * heads, rows), lambda b, ids: (b, 0, 0)),
                whole(grad_shape),
                whole(out_shape),
            ),
            scratch_shapes=[
                pltpu.VMEM((total * rows, width), F32),
                pltpu.VMEM((node_rows, cols), F32),
                pltpu.VMEM((node_rows, cols), F32),
                pltpu.SemaphoreType.DMA((len(layout),)),
                pltpu.SemaphoreType.DMA,
            ],
        ),
        compiler_params=pltpu.CompilerParams(
            dimension_semantics=("arbitrary",), vmem_limit_bytes=56 * 1024 * 1024
        ),
        name="attend_forward",
    )(ids, *arrays, out_cotangent, grad_mixed, bias, w_query, w_key, w_value, w_out)


def backward_kernel(
    steps_ref, readers_ref, feats_ref, cots_ref, stats_ref, lists_ref, own_ref, part_ref,
    wq_ref, wk_ref, wv_ref, feat_ref, gk_ref, gv_ref,
    pair_mem, key_mem, value_mem, dk_mem, dv_mem, buffer, grads, sems,
):
    rows = buffer.shape[1] // GROUP
    cols = wq_ref.shape[1]
    heads = cols // HEAD_SIZE
    lane = lax.broadcasted_iota(jnp.int32, (rows, cols), 1) // HEAD_SIZE
    count = steps_ref[2, 0]

    def load(step, into):
        for at in range(GROUP):
            to = pl.ds(at * rows, rows)
            spot = readers_ref[1, step * GROUP + at]
            start = pl.ds(pl.multiple_of(spot * rows, rows), rows)
            pltpu.make_async_copy(
                feats_ref.at[start, :], buffer.at[into, to, :], sems.at[0, into]
            ).start()
            spot = readers_ref[0, step * GROUP + at]
            start = pl.ds(pl.multiple_of(spot * rows, rows), rows)
            pltpu.make_async_copy(
                cots_ref.at[start, :], grads.at[into, to, :], sems.at[1, into]
            ).start()

    load(0, 0)
    own = split(own_ref[...])
    pair_mem[...] = mul3(own, split(wide(wk_ref[...], wv_ref[...])))
    dk_mem[...] = jnp.zeros_like(dk_mem)
    dv_mem[...] = jnp.zeros_like(dv_mem)
    w_query = split(wq_ref[...])
    mark_row = lax.broadcasted_iota(jnp.int32, (8, GROUP * rows), 0)
    mark_col = lax.broadcasted_iota(jnp.int32, (8, GROUP * rows), 1)
    marks = (mark_row == mark_col // rows).astype(BF16)

    def chunk(step, carry):
        turn = step % 2
        kind = steps_ref[1, step]
        block = pl.ds(pl.multiple_of(steps_ref[0, step] * rows, rows), rows)

        @pl.when(step + 1 < count)
        def _():
            load(step + 1, 1 - turn)

        @pl.when(kind % 2 == 1)
        def _():
            pairs = pair_mem[block, :]
            for memory, value in ((key_mem, pairs[:, :cols]), (value_mem, pairs[:, cols:])):
                for at, left in enumerate(pair_left(value)):
                    memory[at] = left

        pltpu.make_async_copy(buffer.at[turn], buffer.at[turn], sems.at[0, turn]).wait()
        pltpu.make_async_copy(grads.at[turn], grads.at[turn], sems.at[1, turn]).wait()
        query = mul3(split(buffer[turn]), w_query) * SCALE
        grad = grads[turn]
        q_high, q_low = split(query)
        g_high, g_low = split(grad)
        q_both, g_both = wide(q_high, q_low), wide(g_high, g_low)
        turned_high, turned_low = split(jnp.transpose(wide(query, grad)))
        masks, stats = [], []
        for at in range(GROUP):
            entry = readers_ref[2, step * GROUP + at]
            row = lists_ref[readers_ref[3, step * GROUP + at], pl.ds(jnp.maximum(entry, 0), 1), :]
            kept = ((row > 0) | (entry == 0)) & (entry >= 0)
            masks.append(jnp.where(kept, 0.0, MASKED))
            stats.append(stats_ref[readers_ref[4, step * GROUP + at]])
        masks.append(jnp.zeros((8 - GROUP, rows), F32))
        bias = mul(jnp.concatenate(masks, axis=0).astype(BF16), marks, 0, 0)
        stat = jnp.concatenate(stats, axis=1)
        each = range(key_mem.shape[0])
        scores = pair_products(
            [key_mem[at] for at in each], turned_high[:cols], turned_low[:cols]
        )
        grad_probs = pair_products(
            [value_mem[at] for at in each], turned_high[cols:], turned_low[cols:]
        )

        def rows_of(first):
            return [
                jnp.broadcast_to(stat[first + head:first + head + 1], bias.shape)
                for head in range(heads)
            ]

        shift = jnp.concatenate([bias - each for each in rows_of(0)], axis=0)
        probs = jnp.exp(scores + shift)
        grad_scores = probs * (grad_probs - jnp.concatenate(rows_of(heads), axis=0))
        p_high, p_low = split(probs)
        grad_value = fold(mul(p_high, g_both)) + mul(p_low, g_high)
        s_high, s_low = split(grad_scores)
        grad_key = fold(mul(s_high, q_both)) + mul(s_low, q_high)

        def gathered(value):
            parts = [
                jnp.where(lane == head, value[head * rows:(head + 1) * rows], 0.0)
                for head in range(heads)
            ]
            return sum(parts[1:], parts[0])

        dv_mem[block, :] += gathered(grad_value)
        dk_mem[block, :] += gathered(grad_key)
        return carry

    lax.fori_loop(0, count, chunk, 0)
    grad_key, grad_value = split(dk_mem[...]), split(dv_mem[...])
    feat_ref[...] = (
        part_ref[...]
        + mul3(grad_key, split(wk_ref[...]), 1, 1)
        + mul3(grad_value, split(wv_ref[...]), 1, 1)
    )
    own = split(own_ref[...])
    gk_ref[...] = mul3(own, grad_key, 0, 0)
    gv_ref[...] = mul3(own, grad_value, 0, 0)


def attend_backward(
    steps, readers, all_feats, all_cots, all_stats, lists, own_feats, part,
    w_query, w_key, w_value, rows,
):
    node_rows, width = own_feats.shape
    cols = w_query.shape[1]
    span = min(cols, 2 * HEAD_SIZE)
    held = pl.BlockSpec(memory_space=pltpu.VMEM)
    scalars = pl.BlockSpec(memory_space=pltpu.SMEM)
    afar = pl.BlockSpec(memory_space=pl.ANY)
    grad_shape = jax.ShapeDtypeStruct((width, cols), F32)
    return pl.pallas_call(
        backward_kernel,
        out_shape=(jax.ShapeDtypeStruct((node_rows, width), F32), grad_shape, grad_shape),
        in_specs=[scalars, scalars, afar, afar] + [held] * 7,
        out_specs=(held, held, held),
        scratch_shapes=[
            pltpu.VMEM((node_rows, 2 * cols), F32),
            pltpu.VMEM((cols // span, span // HEAD_SIZE * rows, 3 * span), BF16),
            pltpu.VMEM((cols // span, span // HEAD_SIZE * rows, 3 * span), BF16),
            pltpu.VMEM((node_rows, cols), F32),
            pltpu.VMEM((node_rows, cols), F32),
            pltpu.VMEM((2, GROUP * rows, width), F32),
            pltpu.VMEM((2, GROUP * rows, cols), F32),
            pltpu.SemaphoreType.DMA((2, 2)),
        ],
        compiler_params=pltpu.CompilerParams(vmem_limit_bytes=50 * 1024 * 1024),
        name="attend_backward",
    )(
        steps, readers, all_feats, all_cots, all_stats, lists, own_feats, part,
        w_query, w_key, w_value,
    )


def plan_backward(all_ids, me, block_count, pair_limit):
    blocks, entries = all_ids.shape
    candidates = blocks * entries
    flat = all_ids.reshape(-1)
    slot = jnp.where(flat // block_count == me, flat % block_count, block_count)
    order = jnp.arange(candidates, dtype=jnp.int32)
    same = (slot[:, None] == slot[None, :]) & (order[None, :] < order[:, None])
    rank = jnp.sum(same.astype(jnp.int32), axis=1)
    block_range = jnp.arange(block_count, dtype=jnp.int32)
    tally = jnp.sum((slot[None, :] == block_range[:, None]).astype(jnp.int32), axis=1)
    chunks = (tally + GROUP - 1) // GROUP
    ends = jnp.sum(
        jnp.where(block_range[None, :] <= block_range[:, None], chunks[None, :], 0), axis=1
    )
    starts = ends - chunks
    count = (pair_limit + block_count * GROUP) // GROUP
    places = count * GROUP
    start_of = jnp.sum(
        jnp.where(slot[:, None] == block_range[None, :], starts[None, :], 0), axis=1
    )
    place = jnp.where(slot < block_count, start_of * GROUP + rank, places)
    spot = jnp.arange(places, dtype=jnp.int32)
    hit = place[None, :] == spot[:, None]
    source = jnp.sum(jnp.where(hit, order[None, :], 0), axis=1)
    filled = jnp.sum(hit.astype(jnp.int32), axis=1) > 0
    readers = source // entries
    entry = jnp.where(filled, source % entries, -1)
    step = jnp.arange(count, dtype=jnp.int32)
    block = jnp.sum((step[:, None] >= ends[None, :]).astype(jnp.int32), axis=1)
    live = block < block_count
    block = jnp.minimum(block, block_count - 1)
    first = jnp.sum((step[:, None] == starts[None, :]).astype(jnp.int32), axis=1) > 0
    last = jnp.sum((step[:, None] == ends[None, :] - 1).astype(jnp.int32), axis=1) > 0
    kind = jnp.where(
        live, first.astype(jnp.int32) + 2 * last.astype(jnp.int32) + 4, 0
    )
    return jnp.stack([block, kind, jnp.full_like(kind, ends[-1])]), readers, entry


def head_parts(part):
    me = lax.axis_index("head")
    half = part.shape[1] // 2
    sent = lax.dynamic_slice_in_dim(part, (1 - me) * half, half, axis=1)
    return sent, lax.dynamic_slice_in_dim(part, me * half, half, axis=1)


def head_scatter(part, parts=None):
    if lax.axis_size("head") != 2:
        return lax.psum_scatter(part, "head", scatter_dimension=1, tiled=True)
    sent, kept = head_parts(part) if parts is None else parts
    return kept + lax.ppermute(sent, "head", [(0, 1), (1, 0)])


def from_across(value, bit):
    pairs = [(at, at ^ bit) for at in range(lax.axis_size("dom"))]
    return lax.ppermute(value, "dom", pairs)


def dom_sum_start(first, second):
    odd = lax.axis_index("dom") % 2 == 1
    mine = jnp.where(odd, second, first) + from_across(jnp.where(odd, first, second), 1)
    return mine + from_across(mine, 2)


def dom_sum_end(mine):
    odd = lax.axis_index("dom") % 2 == 1
    bit = 4
    while bit < lax.axis_size("dom"):
        mine = mine + from_across(mine, bit)
        bit *= 2
    other = from_across(mine, 1)
    return jnp.where(odd, other, mine), jnp.where(odd, mine, other)


def double(value, bit):
    size, me = lax.axis_size("dom"), lax.axis_index("dom")
    other = lax.ppermute(value, "dom", [(at, at ^ bit) for at in range(size)])
    upper = me & bit != 0
    low, high = jnp.where(upper, other, value), jnp.where(upper, value, other)
    return jnp.concatenate([low, high], axis=0)


def doubled_place(device, size):
    place, bit = jnp.zeros_like(device), 1
    while bit < size:
        place = 2 * place + device // bit % 2
        bit *= 2
    return place


def gather_feats(part, lists, block_count, make_plan, early):
    size, me = lax.axis_size("dom"), lax.axis_index("dom")
    if size != 16 or lax.axis_size("head") != 2 or block_count != 8:
        plan = make_plan(lax.all_gather(lists, "dom", axis=0, tiled=True), lambda ids: ids)
        everything = lax.all_gather(part, "dom", axis=0, tiled=True)
        return [(everything, 0, everything.shape[0], 0)], lambda ids: ids, part, plan, early
    side = lax.axis_index("head")
    lacked = block_count - RING
    rows = part.shape[0] // block_count
    total = size * block_count

    ring = [0, 2, 4, 6, 7, 5, 3, 1]
    onward, back = [], []
    for at in range(8):
        for core in range(2):
            here, there = 2 * ring[at] + core, 2 * ring[(at + 1) % 8] + core
            onward.append((here, there))
            back.append((there, here))
    across = [(at, at ^ 1) for at in range(size)]
    other_head = [(0, 1), (1, 0)]

    def lacking(value):
        parts = [
            lax.dynamic_slice_in_dim(each, (RING - lacked) * side * rows, lacked * rows, axis=0)
            for each in value
        ]
        return jnp.concatenate(parts, axis=0)

    half = total // 2

    def swap(value):
        return lax.ppermute(value, "dom", across)

    def chip_place(chip):
        level, column = chip // 2, chip % 2
        return jnp.where(column == 0, level, 7 - level)

    def place(ids):
        owner, block = ids // block_count, ids % block_count
        gap = (chip_place(owner // 2) - chip_place(me // 2)) % 8
        slot = jnp.where(gap < 4, 2 * gap, 2 * (8 - gap) - 1)
        moved = jnp.where(gap == 0, block, (block + RING * side) % block_count)
        spot = slot * block_count + moved
        return spot + jnp.where(owner % 2 == me % 2, 0, half)

    notes = lists.reshape(-1, lists.shape[2])
    below = notes.shape[0] // 2
    notes = jnp.concatenate([notes[:below], notes[below:]], axis=1)

    start = lax.dynamic_slice_in_dim(part, lacked * side * rows, RING * rows, axis=0)
    start = jnp.concatenate([start, notes], axis=0)
    held = (lax.ppermute(start, "dom", onward), lax.ppermute(start, "dom", back))
    twin = swap(part)
    all_notes = [notes, swap(notes)]
    held, twin, early = lax.optimization_barrier((held, twin, early))
    pieces = [(part, 0, block_count * rows, 0), (twin, 0, block_count * rows, half)]

    def keep(value, swapped, slots):
        for at, slot in enumerate(slots):
            first = slot * block_count + RING
            pieces.append((value, lacked * at * rows, lacked * rows, first))
            pieces.append((swapped, lacked * at * rows, lacked * rows, half + first))

    def keep_ring(values, swapped, slots):
        for at, slot in enumerate(slots):
            first = slot * block_count
            pieces.append((values[at], 0, RING * rows, first))
            pieces.append((swapped[at], 0, RING * rows, half + first))
            all_notes.extend([values[at][RING * rows:], swapped[at][RING * rows:]])

    slots, lack, lack_slots, notes = (1, 2), (), (), ()
    for step in range(1, 5):
        if step < 3:
            coming = (
                lax.ppermute(held[0], "dom", onward), lax.ppermute(held[1], "dom", back)
            )
        elif step == 3:
            coming = (
                lax.ppermute(held[0][: RING // 2 * rows], "dom", onward),
                lax.ppermute(held[1][RING // 2 * rows:], "dom", back),
            )
            notes = jnp.concatenate(all_notes, axis=0)
            all_notes = []
        else:
            coming = ()
        sent = lacking(held)
        if step == 4:
            held, sent, waiting = lax.optimization_barrier((held, sent, waiting))
        more = (lax.ppermute(sent, "head", other_head),)
        if step == 3:
            coming, held, more, notes = lax.optimization_barrier((coming, held, more, notes))
            waiting, waiting_slots = (held, lack), (slots, lack_slots)
        else:
            swapped = tuple(swap(value) for value in held)
            swapped_lack = tuple(swap(value) for value in lack) if step < 3 else ()
            if step < 3:
                coming, held, more, swapped, lack, swapped_lack = lax.optimization_barrier(
                    (coming, held, more, swapped, lack, swapped_lack)
                )
            else:
                (old, old_lack), (old_slots, old_lack_slots) = waiting, waiting_slots
                old_swapped = tuple(swap(value) for value in old)
                old_swapped_lack = tuple(swap(value) for value in old_lack)
                held, swapped, lack, old_swapped, old_swapped_lack = (
                    lax.optimization_barrier(
                        (held, swapped, lack, old_swapped, old_swapped_lack)
                    )
                )
                last, last_slots = lack, lack_slots
                keep_ring(old, old_swapped, old_slots)
                keep(old_lack[0], old_swapped_lack[0], old_lack_slots)
            keep_ring(held, swapped, slots)
            if swapped_lack:
                keep(lack[0], swapped_lack[0], lack_slots)
        lack, lack_slots = more, slots
        if step == 3:
            held, slots = (jnp.concatenate(coming, axis=0),), (7,)
            late = held[0]
        else:
            held, slots = coming, (2 * step + 1, 2 * step + 2)
    all_notes.insert(0, notes)
    every = jnp.concatenate(all_notes, axis=0)
    width = lists.shape[2]
    every = jnp.concatenate([every[:, :width], every[:, width:]], axis=0)
    plan = make_plan(every.reshape((-1,) + lists.shape[1:]), place)
    lack, last, plan = lax.optimization_barrier((lack, last, plan))
    keep(last[0], swap(last[0]), last_slots)
    keep(lack[0], swap(lack[0]), (7,))
    return pieces, place, late, plan, early


def per_device(
    node_features, w_query, w_key, w_value, w_out, nbr_part, nbr_slot, key_mask, out_cotangent
):
    dom_count = lax.axis_size("dom")
    block_count, list_len = nbr_part.shape
    node_rows, width = node_features.shape
    rows = node_rows // block_count
    me = lax.axis_index("dom")
    slot_cap = min(block_count, max(2, (block_count * list_len + dom_count - 1) // dom_count))
    self_ids = me * block_count + jnp.arange(block_count, dtype=jnp.int32)[:, None]
    ids = jnp.concatenate([self_ids, nbr_part * block_count + nbr_slot], axis=1)
    mask = jnp.concatenate([jnp.ones((block_count, 1, rows), jnp.int32), key_mask], axis=1)
    bias = jnp.where(mask > 0, 0.0, MASKED).reshape(block_count, 1, (list_len + 1) * rows)
    names = jnp.pad(ids, ((0, 0), (0, rows - list_len - 1))).astype(F32)[:, None]
    lists = jnp.concatenate([names, key_mask.astype(F32)], axis=1)

    def make_plan(lists, place):
        all_ids = lists[:, 0, : list_len + 1].astype(jnp.int32)
        steps, rows_of, entry = plan_backward(
            all_ids, me, block_count, dom_count * slot_cap
        )
        readers = all_ids[:, 0][rows_of]
        stat_of = doubled_place(readers // block_count, dom_count) * block_count
        stat_of = stat_of + readers % block_count
        return steps, jnp.stack([readers, place(readers), entry, rows_of, stat_of]), lists

    grad_mixed = lax.dot_general(
        out_cotangent, w_out, (((1,), (1,)), ((), ())), precision=lax.Precision.HIGHEST
    )
    pieces, place, late, (steps, spots, lists), grad_mixed = gather_feats(
        node_features, lists, block_count, make_plan, grad_mixed
    )
    sent, late = lax.optimization_barrier((grad_mixed, late))
    all_grads = lax.all_gather(sent, "dom", axis=0, tiled=True)
    cols = w_query.shape[1]
    all_feats, out_part, feat_part, stats, grad_query, grad_out = attend_forward(
        place(ids), pieces, dom_count * block_count, out_cotangent, grad_mixed, bias, w_query, w_key, w_value, w_out
    )
    all_stats, bit, out_parts = stats, dom_count // 2, None
    while bit:
        all_stats = double(all_stats, bit)
        if out_parts is None and lax.axis_size("head") == 2:
            all_stats, out_parts = lax.optimization_barrier((all_stats, head_parts(out_part)))
        bit //= 2
    layer_out = head_scatter(out_part, out_parts)
    pieces = [grad_out[:, at:at + cols] for at in range(0, width, cols)]
    early_sum = dom_sum_start(grad_query, jnp.concatenate(pieces, axis=0))
    feats_part, grad_key, grad_value = attend_backward(
        steps, spots, all_feats, all_grads, all_stats, lists, node_features, feat_part,
        w_query, w_key, w_value, rows,
    )
    early_sum, feats_part, grad_key, grad_value = lax.optimization_barrier(
        (early_sum, feats_part, grad_key, grad_value)
    )
    grad_features = head_scatter(feats_part)
    late_sum = dom_sum_start(grad_key, grad_value)
    grad_query, grad_out = dom_sum_end(early_sum)
    pieces = [grad_out[at:at + cols] for at in range(0, width, cols)]
    grad_out = jnp.concatenate(pieces, axis=1)
    grad_key, grad_value = dom_sum_end(late_sum)
    return (layer_out, grad_features, grad_query, grad_key, grad_value, grad_out)


def solution(mesh):
    placed = (
        P("dom", None),
        P(None, "head"),
        P(None, "head"),
        P(None, "head"),
        P("head", None),
        P("dom", None),
        P("dom", None),
        P("dom", None, None),
        P("dom", None),
    )
    return jax.shard_map(
        per_device,
        mesh=mesh,
        in_specs=placed,
        out_specs=(
            P("dom", "head"),
            P("dom", "head"),
            P(None, "head"),
            P(None, "head"),
            P(None, "head"),
            P("head", None),
        ),
        check_vma=False,
    )
```

```python
import functools

import jax
import jax.numpy as jnp
from jax import lax
from jax.experimental import pallas as pl
from jax.experimental.pallas import tpu as pltpu
from jax.sharding import PartitionSpec as P

HEAD_SIZE = 32
GROUP = 2
RING = 6
SCALE = HEAD_SIZE ** (-0.5)
MASKED = -1e30
F32 = jnp.float32
BF16 = jnp.bfloat16


def split(value):
    high = value.astype(BF16)
    return high, (value - high.astype(F32)).astype(BF16)


def mul(left, right, left_dim=1, right_dim=0):
    return lax.dot_general(
        left, right, (((left_dim,), (right_dim,)), ((), ())), preferred_element_type=F32
    )


def mul3(left, right, left_dim=1, right_dim=0):
    left_high, left_low = left
    right_high, right_low = right
    return (
        mul(left_high, right_high, left_dim, right_dim)
        + mul(left_high, right_low, left_dim, right_dim)
        + mul(left_low, right_high, left_dim, right_dim)
    )


def wide(first, second):
    return jnp.concatenate([first, second], axis=1)


def pair_left(value):
    rows, cols = value.shape
    span = min(cols, 2 * HEAD_SIZE)
    lane = lax.broadcasted_iota(jnp.int32, (rows, span), 1) // HEAD_SIZE
    result = []
    for first in range(0, cols, span):
        part = value[:, first:first + span]
        parts = [jnp.where(lane == head, part, 0.0) for head in range(span // HEAD_SIZE)]
        high, low = split(jnp.concatenate(parts, axis=0))
        result.append(jnp.concatenate([high, low, high], axis=1))
    return result


def pair_products(lefts, high, low):
    span = high.shape[0] // len(lefts)
    result = []
    for at, left in enumerate(lefts):
        here = slice(at * span, (at + 1) * span)
        right = jnp.concatenate([high[here], high[here], low[here]], axis=0)
        result.append(mul(left, right))
    return jnp.concatenate(result, axis=0)


def fold(value):
    half = value.shape[1] // 2
    return value[:, :half] + value[:, half:]


def forward_kernel(entries, layout, source_count, ids, *refs):
    sources = refs[:source_count]
    (cot_ref, grad_ref, bias_ref, wq_ref, wk_ref, wv_ref, wo_ref,
     all_ref, out_ref, feat_ref, stat_ref, gq_ref, go_ref,
     feats, mixed_mem, grad_mem, sems, all_sem) = refs[source_count:]
    rows = grad_ref.shape[0]
    step = pl.program_id(0)
    keep = pltpu.make_async_copy(feats, all_ref, all_sem)

    @pl.when(step == 0)
    def _():
        copies = []
        for at, (source, row, count, block) in enumerate(layout):
            copies.append(
                pltpu.make_async_copy(
                    sources[source].at[pl.ds(row, count), :],
                    feats.at[pl.ds(block * rows, count), :],
                    sems.at[at],
                )
            )
        for copy in copies:
            copy.start()
        for copy in copies:
            copy.wait()
        keep.start()

    listed = [
        feats[pl.ds(pl.multiple_of(ids[step, entry] * rows, rows), rows), :]
        for entry in range(entries)
    ]
    cols = wq_ref.shape[1]
    heads = cols // HEAD_SIZE
    inputs = split(jnp.concatenate(listed, axis=0))
    w_query = split(wq_ref[...])
    w_out = split(wo_ref[...])
    pairs = mul3(inputs, split(wide(wk_ref[...], wv_ref[...])))
    key_high, key_low = split(pairs[:, :cols])
    value_high, value_low = split(pairs[:, cols:])
    key_both, value_both = wide(key_high, key_low), wide(value_high, value_low)
    turned_high, turned_low = split(jnp.transpose(pairs))
    own = (inputs[0][:rows], inputs[1][:rows])
    query = mul3(own, w_query) * SCALE
    grad_mixed = grad_ref[...]
    lane = lax.broadcasted_iota(jnp.int32, (rows, cols), 1) // HEAD_SIZE
    here = [lane == head for head in range(heads)]

    def spread(value):
        return jnp.concatenate([jnp.where(mask, value, 0.0) for mask in here], axis=0)

    def gather(value):
        parts = [
            jnp.where(mask, value[head * rows:(head + 1) * rows], 0.0)
            for head, mask in enumerate(here)
        ]
        return sum(parts[1:], parts[0])

    scores = pair_products(pair_left(query), turned_high[:cols], turned_low[:cols])
    scores = scores + bias_ref[0]
    top = jnp.max(scores, axis=1, keepdims=True)
    probs = jnp.exp(scores - top)
    total = jnp.sum(probs, axis=1, keepdims=True)
    inverse = 1.0 / total
    p_high, p_low = split(probs)
    weighted = (fold(mul(p_high, value_both)) + mul(p_low, value_high)) * inverse
    mixed = gather(weighted)
    grad_part = spread(grad_mixed)
    delta = jnp.sum(grad_part * weighted, axis=1, keepdims=True)
    grad_probs = pair_products(pair_left(grad_mixed), turned_high[cols:], turned_low[cols:])
    s_high, s_low = split(probs * (grad_probs - delta))
    back = (fold(mul(s_high, key_both)) + mul(s_low, key_high)) * (inverse * SCALE)
    grad_query = gather(back)
    log_total = top + jnp.log(total)
    stat_lane = lax.broadcasted_iota(jnp.int32, (rows, rows), 1)
    stats = jnp.zeros((rows, rows), F32)
    for head in range(heads):
        at = slice(head * rows, (head + 1) * rows)
        stats = jnp.where(stat_lane == head, log_total[at], stats)
        stats = jnp.where(stat_lane == heads + head, delta[at], stats)
    block = pl.ds(pl.multiple_of(step * rows, rows), rows)
    mixed_mem[block, :] = mixed
    grad_mem[block, :] = grad_query
    stat_ref[0] = jnp.transpose(stats)[: 2 * heads]

    @pl.when(step == pl.num_programs(0) - 1)
    def _():
        mixed, grad_query = split(mixed_mem[...]), split(grad_mem[...])
        first = pl.ds(pl.multiple_of(ids[0, 0] * rows, rows), mixed_mem.shape[0])
        out_ref[...] = mul3(mixed, w_out)
        feat_ref[...] = mul3(grad_query, w_query, 1, 1)
        gq_ref[...] = mul3(split(feats[first, :]), grad_query, 0, 0)
        go_ref[...] = mul3(mixed, split(cot_ref[...]), 0, 0)
        keep.wait()


def attend_forward(ids, pieces, total, out_cotangent, grad_mixed, bias, w_query, w_key, w_value, w_out):
    block_count, entries = ids.shape
    node_rows, width = out_cotangent.shape
    rows = node_rows // block_count
    cols = w_query.shape[1]
    heads = cols // HEAD_SIZE

    arrays = []
    for array, *_ in pieces:
        if not any(array is known for known in arrays):
            arrays.append(array)
    layout = [
        ([array is known for known in arrays].index(True), *rest) for array, *rest in pieces
    ]
    all_shape = jax.ShapeDtypeStruct((total * rows, width), F32)

    def whole(array):
        return pl.BlockSpec(array.shape, lambda b, ids: (0,) * array.ndim)

    grad_shape = jax.ShapeDtypeStruct((width, cols), F32)
    out_shape = jax.ShapeDtypeStruct((cols, width), F32)
    node_shape = jax.ShapeDtypeStruct((node_rows, width), F32)
    return pl.pallas_call(
        functools.partial(forward_kernel, entries, layout, len(arrays)),
        out_shape=(
            all_shape,
            node_shape,
            node_shape,
            jax.ShapeDtypeStruct((block_count, 2 * heads, rows), F32),
            grad_shape,
            out_shape,
        ),
        grid_spec=pltpu.PrefetchScalarGridSpec(
            num_scalar_prefetch=1,
            grid=(block_count,),
            in_specs=[pl.BlockSpec(memory_space=pl.ANY) for _ in arrays]
            + [whole(out_cotangent), pl.BlockSpec((rows, cols), lambda b, ids: (b, 0))]
            + [pl.BlockSpec((1, 1, entries * rows), lambda b, ids: (b, 0, 0))]
            + [whole(w) for w in (w_query, w_key, w_value, w_out)],
            out_specs=(
                pl.BlockSpec(memory_space=pl.ANY),
                whole(node_shape),
                whole(node_shape),
                pl.BlockSpec((1, 2 * heads, rows), lambda b, ids: (b, 0, 0)),
                whole(grad_shape),
                whole(out_shape),
            ),
            scratch_shapes=[
                pltpu.VMEM((total * rows, width), F32),
                pltpu.VMEM((node_rows, cols), F32),
                pltpu.VMEM((node_rows, cols), F32),
                pltpu.SemaphoreType.DMA((len(layout),)),
                pltpu.SemaphoreType.DMA,
            ],
        ),
        compiler_params=pltpu.CompilerParams(
            dimension_semantics=("arbitrary",), vmem_limit_bytes=56 * 1024 * 1024
        ),
        name="attend_forward",
    )(ids, *arrays, out_cotangent, grad_mixed, bias, w_query, w_key, w_value, w_out)


def backward_kernel(
    steps_ref, readers_ref, feats_ref, cots_ref, stats_ref, lists_ref, own_ref, part_ref,
    wq_ref, wk_ref, wv_ref, feat_ref, gk_ref, gv_ref,
    pair_mem, key_mem, value_mem, dk_mem, dv_mem, buffer, grads, sems,
):
    rows = buffer.shape[1] // GROUP
    cols = wq_ref.shape[1]
    heads = cols // HEAD_SIZE
    lane = lax.broadcasted_iota(jnp.int32, (rows, cols), 1) // HEAD_SIZE
    count = steps_ref[2, 0]

    def load(step, into):
        for at in range(GROUP):
            to = pl.ds(at * rows, rows)
            spot = readers_ref[1, step * GROUP + at]
            start = pl.ds(pl.multiple_of(spot * rows, rows), rows)
            pltpu.make_async_copy(
                feats_ref.at[start, :], buffer.at[into, to, :], sems.at[0, into]
            ).start()
            spot = readers_ref[0, step * GROUP + at]
            start = pl.ds(pl.multiple_of(spot * rows, rows), rows)
            pltpu.make_async_copy(
                cots_ref.at[start, :], grads.at[into, to, :], sems.at[1, into]
            ).start()

    load(0, 0)
    own = split(own_ref[...])
    pair_mem[...] = mul3(own, split(wide(wk_ref[...], wv_ref[...])))
    dk_mem[...] = jnp.zeros_like(dk_mem)
    dv_mem[...] = jnp.zeros_like(dv_mem)
    w_query = split(wq_ref[...])
    mark_row = lax.broadcasted_iota(jnp.int32, (8, GROUP * rows), 0)
    mark_col = lax.broadcasted_iota(jnp.int32, (8, GROUP * rows), 1)
    marks = (mark_row == mark_col // rows).astype(BF16)

    def chunk(step, carry):
        turn = step % 2
        kind = steps_ref[1, step]
        block = pl.ds(pl.multiple_of(steps_ref[0, step] * rows, rows), rows)

        @pl.when(step + 1 < count)
        def _():
            load(step + 1, 1 - turn)

        @pl.when(kind % 2 == 1)
        def _():
            pairs = pair_mem[block, :]
            for memory, value in ((key_mem, pairs[:, :cols]), (value_mem, pairs[:, cols:])):
                for at, left in enumerate(pair_left(value)):
                    memory[at] = left

        pltpu.make_async_copy(buffer.at[turn], buffer.at[turn], sems.at[0, turn]).wait()
        pltpu.make_async_copy(grads.at[turn], grads.at[turn], sems.at[1, turn]).wait()
        query = mul3(split(buffer[turn]), w_query) * SCALE
        grad = grads[turn]
        q_high, q_low = split(query)
        g_high, g_low = split(grad)
        q_both, g_both = wide(q_high, q_low), wide(g_high, g_low)
        turned_high, turned_low = split(jnp.transpose(wide(query, grad)))
        masks, stats = [], []
        for at in range(GROUP):
            entry = readers_ref[2, step * GROUP + at]
            row = lists_ref[readers_ref[3, step * GROUP + at], pl.ds(jnp.maximum(entry, 0), 1), :]
            kept = ((row > 0) | (entry == 0)) & (entry >= 0)
            masks.append(jnp.where(kept, 0.0, MASKED))
            stats.append(stats_ref[readers_ref[4, step * GROUP + at]])
        masks.append(jnp.zeros((8 - GROUP, rows), F32))
        bias = mul(jnp.concatenate(masks, axis=0).astype(BF16), marks, 0, 0)
        stat = jnp.concatenate(stats, axis=1)
        each = range(key_mem.shape[0])
        scores = pair_products(
            [key_mem[at] for at in each], turned_high[:cols], turned_low[:cols]
        )
        grad_probs = pair_products(
            [value_mem[at] for at in each], turned_high[cols:], turned_low[cols:]
        )

        def rows_of(first):
            return [
                jnp.broadcast_to(stat[first + head:first + head + 1], bias.shape)
                for head in range(heads)
            ]

        shift = jnp.concatenate([bias - each for each in rows_of(0)], axis=0)
        probs = jnp.exp(scores + shift)
        grad_scores = probs * (grad_probs - jnp.concatenate(rows_of(heads), axis=0))
        p_high, p_low = split(probs)
        grad_value = fold(mul(p_high, g_both)) + mul(p_low, g_high)
        s_high, s_low = split(grad_scores)
        grad_key = fold(mul(s_high, q_both)) + mul(s_low, q_high)

        def gathered(value):
            parts = [
                jnp.where(lane == head, value[head * rows:(head + 1) * rows], 0.0)
                for head in range(heads)
            ]
            return sum(parts[1:], parts[0])

        dv_mem[block, :] += gathered(grad_value)
        dk_mem[block, :] += gathered(grad_key)
        return carry

    lax.fori_loop(0, count, chunk, 0)
    grad_key, grad_value = split(dk_mem[...]), split(dv_mem[...])
    feat_ref[...] = (
        part_ref[...]
        + mul3(grad_key, split(wk_ref[...]), 1, 1)
        + mul3(grad_value, split(wv_ref[...]), 1, 1)
    )
    own = split(own_ref[...])
    gk_ref[...] = mul3(own, grad_key, 0, 0)
    gv_ref[...] = mul3(own, grad_value, 0, 0)


def attend_backward(
    steps, readers, all_feats, all_cots, all_stats, lists, own_feats, part,
    w_query, w_key, w_value, rows,
):
    node_rows, width = own_feats.shape
    cols = w_query.shape[1]
    span = min(cols, 2 * HEAD_SIZE)
    held = pl.BlockSpec(memory_space=pltpu.VMEM)
    scalars = pl.BlockSpec(memory_space=pltpu.SMEM)
    afar = pl.BlockSpec(memory_space=pl.ANY)
    grad_shape = jax.ShapeDtypeStruct((width, cols), F32)
    return pl.pallas_call(
        backward_kernel,
        out_shape=(jax.ShapeDtypeStruct((node_rows, width), F32), grad_shape, grad_shape),
        in_specs=[scalars, scalars, afar, afar] + [held] * 7,
        out_specs=(held, held, held),
        scratch_shapes=[
            pltpu.VMEM((node_rows, 2 * cols), F32),
            pltpu.VMEM((cols // span, span // HEAD_SIZE * rows, 3 * span), BF16),
            pltpu.VMEM((cols // span, span // HEAD_SIZE * rows, 3 * span), BF16),
            pltpu.VMEM((node_rows, cols), F32),
            pltpu.VMEM((node_rows, cols), F32),
            pltpu.VMEM((2, GROUP * rows, width), F32),
            pltpu.VMEM((2, GROUP * rows, cols), F32),
            pltpu.SemaphoreType.DMA((2, 2)),
        ],
        compiler_params=pltpu.CompilerParams(vmem_limit_bytes=50 * 1024 * 1024),
        name="attend_backward",
    )(
        steps, readers, all_feats, all_cots, all_stats, lists, own_feats, part,
        w_query, w_key, w_value,
    )


def plan_backward(all_ids, me, block_count, pair_limit):
    blocks, entries = all_ids.shape
    candidates = blocks * entries
    flat = all_ids.reshape(-1)
    slot = jnp.where(flat // block_count == me, flat % block_count, block_count)
    order = jnp.arange(candidates, dtype=jnp.int32)
    same = (slot[:, None] == slot[None, :]) & (order[None, :] < order[:, None])
    rank = jnp.sum(same.astype(jnp.int32), axis=1)
    block_range = jnp.arange(block_count, dtype=jnp.int32)
    tally = jnp.sum((slot[None, :] == block_range[:, None]).astype(jnp.int32), axis=1)
    chunks = (tally + GROUP - 1) // GROUP
    ends = jnp.sum(
        jnp.where(block_range[None, :] <= block_range[:, None], chunks[None, :], 0), axis=1
    )
    starts = ends - chunks
    count = (pair_limit + block_count * GROUP) // GROUP
    places = count * GROUP
    start_of = jnp.sum(
        jnp.where(slot[:, None] == block_range[None, :], starts[None, :], 0), axis=1
    )
    place = jnp.where(slot < block_count, start_of * GROUP + rank, places)
    spot = jnp.arange(places, dtype=jnp.int32)
    hit = place[None, :] == spot[:, None]
    source = jnp.sum(jnp.where(hit, order[None, :], 0), axis=1)
    filled = jnp.sum(hit.astype(jnp.int32), axis=1) > 0
    readers = source // entries
    entry = jnp.where(filled, source % entries, -1)
    step = jnp.arange(count, dtype=jnp.int32)
    block = jnp.sum((step[:, None] >= ends[None, :]).astype(jnp.int32), axis=1)
    live = block < block_count
    block = jnp.minimum(block, block_count - 1)
    first = jnp.sum((step[:, None] == starts[None, :]).astype(jnp.int32), axis=1) > 0
    last = jnp.sum((step[:, None] == ends[None, :] - 1).astype(jnp.int32), axis=1) > 0
    kind = jnp.where(
        live, first.astype(jnp.int32) + 2 * last.astype(jnp.int32) + 4, 0
    )
    return jnp.stack([block, kind, jnp.full_like(kind, ends[-1])]), readers, entry


def head_parts(part):
    me = lax.axis_index("head")
    half = part.shape[1] // 2
    sent = lax.dynamic_slice_in_dim(part, (1 - me) * half, half, axis=1)
    return sent, lax.dynamic_slice_in_dim(part, me * half, half, axis=1)


def head_scatter(part, parts=None):
    if lax.axis_size("head") != 2:
        return lax.psum_scatter(part, "head", scatter_dimension=1, tiled=True)
    sent, kept = head_parts(part) if parts is None else parts
    return kept + lax.ppermute(sent, "head", [(0, 1), (1, 0)])


def from_across(value, bit):
    pairs = [(at, at ^ bit) for at in range(lax.axis_size("dom"))]
    return lax.ppermute(value, "dom", pairs)


def dom_sum(first, second):
    odd = lax.axis_index("dom") % 2 == 1
    mine = jnp.where(odd, second, first) + from_across(jnp.where(odd, first, second), 1)
    bit = 2
    while bit < lax.axis_size("dom"):
        mine = mine + from_across(mine, bit)
        bit *= 2
    other = from_across(mine, 1)
    return jnp.where(odd, other, mine), jnp.where(odd, mine, other)


def double(value, bit):
    size, me = lax.axis_size("dom"), lax.axis_index("dom")
    other = lax.ppermute(value, "dom", [(at, at ^ bit) for at in range(size)])
    upper = me & bit != 0
    low, high = jnp.where(upper, other, value), jnp.where(upper, value, other)
    return jnp.concatenate([low, high], axis=0)


def doubled_place(device, size):
    place, bit = jnp.zeros_like(device), 1
    while bit < size:
        place = 2 * place + device // bit % 2
        bit *= 2
    return place


def gather_feats(part, lists, block_count, make_plan, early):
    size, me = lax.axis_size("dom"), lax.axis_index("dom")
    if size != 16 or lax.axis_size("head") != 2 or block_count != 8:
        plan = make_plan(lax.all_gather(lists, "dom", axis=0, tiled=True), lambda ids: ids)
        everything = lax.all_gather(part, "dom", axis=0, tiled=True)
        return [(everything, 0, everything.shape[0], 0)], lambda ids: ids, part, plan, early
    side = lax.axis_index("head")
    lacked = block_count - RING
    rows = part.shape[0] // block_count
    total = size * block_count

    ring = [0, 2, 4, 6, 7, 5, 3, 1]
    onward, back = [], []
    for at in range(8):
        for core in range(2):
            here, there = 2 * ring[at] + core, 2 * ring[(at + 1) % 8] + core
            onward.append((here, there))
            back.append((there, here))
    across = [(at, at ^ 1) for at in range(size)]
    other_head = [(0, 1), (1, 0)]

    def lacking(value):
        parts = [
            lax.dynamic_slice_in_dim(each, (RING - lacked) * side * rows, lacked * rows, axis=0)
            for each in value
        ]
        return jnp.concatenate(parts, axis=0)

    half = total // 2

    def swap(value):
        return lax.ppermute(value, "dom", across)

    def chip_place(chip):
        level, column = chip // 2, chip % 2
        return jnp.where(column == 0, level, 7 - level)

    def place(ids):
        owner, block = ids // block_count, ids % block_count
        gap = (chip_place(owner // 2) - chip_place(me // 2)) % 8
        slot = jnp.where(gap < 4, 2 * gap, 2 * (8 - gap) - 1)
        moved = jnp.where(gap == 0, block, (block + RING * side) % block_count)
        spot = slot * block_count + moved
        return spot + jnp.where(owner % 2 == me % 2, 0, half)

    notes = lists.reshape(-1, lists.shape[2])
    below = notes.shape[0] // 2
    notes = jnp.concatenate([notes[:below], notes[below:]], axis=1)

    start = lax.dynamic_slice_in_dim(part, lacked * side * rows, RING * rows, axis=0)
    start = jnp.concatenate([start, notes], axis=0)
    held = (lax.ppermute(start, "dom", onward), lax.ppermute(start, "dom", back))
    twin = swap(part)
    all_notes = [notes, swap(notes)]
    held, twin, early = lax.optimization_barrier((held, twin, early))
    pieces = [(part, 0, block_count * rows, 0), (twin, 0, block_count * rows, half)]

    def keep(value, swapped, slots):
        for at, slot in enumerate(slots):
            first = slot * block_count + RING
            pieces.append((value, lacked * at * rows, lacked * rows, first))
            pieces.append((swapped, lacked * at * rows, lacked * rows, half + first))

    def keep_ring(values, swapped, slots):
        for at, slot in enumerate(slots):
            first = slot * block_count
            pieces.append((values[at], 0, RING * rows, first))
            pieces.append((swapped[at], 0, RING * rows, half + first))
            all_notes.extend([values[at][RING * rows:], swapped[at][RING * rows:]])

    slots, lack, lack_slots, notes = (1, 2), (), (), ()
    for step in range(1, 5):
        if step < 3:
            coming = (
                lax.ppermute(held[0], "dom", onward), lax.ppermute(held[1], "dom", back)
            )
        elif step == 3:
            coming = (
                lax.ppermute(held[0][: RING // 2 * rows], "dom", onward),
                lax.ppermute(held[1][RING // 2 * rows:], "dom", back),
            )
            notes = jnp.concatenate(all_notes, axis=0)
            all_notes = []
        else:
            coming = ()
        sent = lacking(held)
        if step == 4:
            held, sent, waiting = lax.optimization_barrier((held, sent, waiting))
        more = (lax.ppermute(sent, "head", other_head),)
        if step == 3:
            coming, held, more, notes = lax.optimization_barrier((coming, held, more, notes))
            waiting, waiting_slots = (held, lack), (slots, lack_slots)
        else:
            swapped = tuple(swap(value) for value in held)
            swapped_lack = tuple(swap(value) for value in lack) if step < 3 else ()
            if step < 3:
                coming, held, more, swapped, lack, swapped_lack = lax.optimization_barrier(
                    (coming, held, more, swapped, lack, swapped_lack)
                )
            else:
                (old, old_lack), (old_slots, old_lack_slots) = waiting, waiting_slots
                old_swapped = tuple(swap(value) for value in old)
                old_swapped_lack = tuple(swap(value) for value in old_lack)
                held, swapped, lack, old_swapped, old_swapped_lack = (
                    lax.optimization_barrier(
                        (held, swapped, lack, old_swapped, old_swapped_lack)
                    )
                )
                last, last_slots = lack, lack_slots
                keep_ring(old, old_swapped, old_slots)
                keep(old_lack[0], old_swapped_lack[0], old_lack_slots)
            keep_ring(held, swapped, slots)
            if swapped_lack:
                keep(lack[0], swapped_lack[0], lack_slots)
        lack, lack_slots = more, slots
        if step == 3:
            held, slots = (jnp.concatenate(coming, axis=0),), (7,)
            late = held[0]
        else:
            held, slots = coming, (2 * step + 1, 2 * step + 2)
    all_notes.insert(0, notes)
    every = jnp.concatenate(all_notes, axis=0)
    width = lists.shape[2]
    every = jnp.concatenate([every[:, :width], every[:, width:]], axis=0)
    plan = make_plan(every.reshape((-1,) + lists.shape[1:]), place)
    lack, last, plan = lax.optimization_barrier((lack, last, plan))
    keep(last[0], swap(last[0]), last_slots)
    keep(lack[0], swap(lack[0]), (7,))
    return pieces, place, late, plan, early


def per_device(
    node_features, w_query, w_key, w_value, w_out, nbr_part, nbr_slot, key_mask, out_cotangent
):
    dom_count = lax.axis_size("dom")
    block_count, list_len = nbr_part.shape
    node_rows, width = node_features.shape
    rows = node_rows // block_count
    me = lax.axis_index("dom")
    slot_cap = min(block_count, max(2, (block_count * list_len + dom_count - 1) // dom_count))
    self_ids = me * block_count + jnp.arange(block_count, dtype=jnp.int32)[:, None]
    ids = jnp.concatenate([self_ids, nbr_part * block_count + nbr_slot], axis=1)
    mask = jnp.concatenate([jnp.ones((block_count, 1, rows), jnp.int32), key_mask], axis=1)
    bias = jnp.where(mask > 0, 0.0, MASKED).reshape(block_count, 1, (list_len + 1) * rows)
    names = jnp.pad(ids, ((0, 0), (0, rows - list_len - 1))).astype(F32)[:, None]
    lists = jnp.concatenate([names, key_mask.astype(F32)], axis=1)

    def make_plan(lists, place):
        all_ids = lists[:, 0, : list_len + 1].astype(jnp.int32)
        steps, rows_of, entry = plan_backward(
            all_ids, me, block_count, dom_count * slot_cap
        )
        readers = all_ids[:, 0][rows_of]
        stat_of = doubled_place(readers // block_count, dom_count) * block_count
        stat_of = stat_of + readers % block_count
        return steps, jnp.stack([readers, place(readers), entry, rows_of, stat_of]), lists

    grad_mixed = lax.dot_general(
        out_cotangent, w_out, (((1,), (1,)), ((), ())), precision=lax.Precision.HIGHEST
    )
    pieces, place, late, (steps, spots, lists), grad_mixed = gather_feats(
        node_features, lists, block_count, make_plan, grad_mixed
    )
    sent, late = lax.optimization_barrier((grad_mixed, late))
    all_grads = lax.all_gather(sent, "dom", axis=0, tiled=True)
    cols = w_query.shape[1]
    all_feats, out_part, feat_part, stats, grad_query, grad_out = attend_forward(
        place(ids), pieces, dom_count * block_count, out_cotangent, grad_mixed, bias, w_query, w_key, w_value, w_out
    )
    all_stats, bit, out_parts = stats, dom_count // 2, None
    while bit:
        all_stats = double(all_stats, bit)
        if out_parts is None and lax.axis_size("head") == 2:
            all_stats, out_parts = lax.optimization_barrier((all_stats, head_parts(out_part)))
        bit //= 2
    layer_out = head_scatter(out_part, out_parts)
    pieces = [grad_out[:, at:at + cols] for at in range(0, width, cols)]
    grad_query, grad_out = dom_sum(grad_query, jnp.concatenate(pieces, axis=0))
    pieces = [grad_out[at:at + cols] for at in range(0, width, cols)]
    grad_out = jnp.concatenate(pieces, axis=1)
    feats_part, grad_key, grad_value = attend_backward(
        steps, spots, all_feats, all_grads, all_stats, lists, node_features, feat_part,
        w_query, w_key, w_value, rows,
    )
    grad_features = head_scatter(feats_part)
    grad_key, grad_value = dom_sum(grad_key, grad_value)
    return (layer_out, grad_features, grad_query, grad_key, grad_value, grad_out)


def solution(mesh):
    placed = (
        P("dom", None),
        P(None, "head"),
        P(None, "head"),
        P(None, "head"),
        P("head", None),
        P("dom", None),
        P("dom", None),
        P("dom", None, None),
        P("dom", None),
    )
    return jax.shard_map(
        per_device,
        mesh=mesh,
        in_specs=placed,
        out_specs=(
            P("dom", "head"),
            P("dom", "head"),
            P(None, "head"),
            P(None, "head"),
            P(None, "head"),
            P("head", None),
        ),
        check_vma=False,
    )
```
